128 devices in a mesh: pair: 16 (over y_hi, z, core), rows: 8 (over y_lo, x).
Axes of the slice: x: 4, y: 4 (y_hi: 2, y_lo: 2; y = y_hi * 2 + y_lo), z: 4, core: 2. Of those that a mesh axis runs over, the one named last changes fastest.
Arguments:
- matrix: float32 [4096, 16384], P(('rows', 'pair')), may hold values from -6 to 6
- plan: int32 [32], replicated, may hold values from 0 to 31, each once
Outputs:
- rotated: float32 [4096, 16384], P('rows', 'pair')
The draws below stay inside these ranges and needn't reach their ends.
Inputs may be any that keep to these rules, and one draw needn't show every extreme that they name: `plan`: each block number appears once.
All inputs are finite; a program needn't handle non-finite values.
Results may differ from the reference program's by a relative error of at most 0.0003.
Values sent between devices are 32-bit elements; how exact they have to be, the bound alone decides.
A program may use at most 64 MiB of HBM per device.

```python
import jax
import jax.numpy as jnp
from jax import lax

BLK = 512
STEPS = 2
BLOCKS = 32
COLS = 16384
ROWS = 4096
N_PAIR = 16


def shard_levels(own_key, shape, split, least, high):
    level, own = 1.0, jax.random.fold_in(own_key, 6)
    for dim, blocks in split:
        heights = jnp.exp(jax.random.uniform(jax.random.fold_in(own, dim), (blocks,), jnp.float32, least / len(split), high / len(split)))
        level = level * jnp.repeat(heights, shape[dim] // blocks).reshape([-1 if axis == dim else 1 for axis in range(len(shape))])
    return level


def bell_draw(stream_key, dims, scale, limit, pieces=(), kind=jnp.bfloat16):
    loudness = shard_levels(stream_key, dims, pieces, -0.22, 0.18) if pieces else 1.0
    values = jax.random.normal(stream_key, dims, jnp.float32) * scale * loudness
    return jnp.minimum(jnp.maximum(values, -limit), limit).astype(kind)


def setup_inputs(seed: int = 0) -> dict:
    keys = jax.random.split(jax.random.key(seed), 3)
    matrix = bell_draw(keys[0], (ROWS, COLS), 1.0, 6.0, ((0, 128),), jnp.float32)
    plan = jax.random.permutation(keys[1], BLOCKS).astype(jnp.int32)
    return dict(matrix=matrix, plan=plan)


epsilon = 1e-06
high = lax.Precision.HIGHEST

def normalize(gram):
    width = gram.shape[0]
    diagonal = jnp.diagonal(gram) + epsilon
    inverse = 1.0 / jnp.sqrt(diagonal)
    normed = gram * inverse[:, None] * inverse[None, :]
    spread = 1.5 * jnp.sqrt(jnp.sum(normed * normed)) / jnp.sqrt(jnp.float32(width))
    scaled_gram = normed / spread
    identity = jnp.eye(width, dtype=jnp.float32)
    first_iter = 0.5 * (3.0 * identity - scaled_gram)
    factor = 0.5 * jnp.sqrt(diagonal) / jnp.sqrt(spread)
    return (scaled_gram, first_iter, inverse, factor, identity)

def pair_step(block):
    gram = jnp.dot(block.T, block, precision=high, preferred_element_type=jnp.float32)
    scaled_gram, first_iter, inverse, factor, identity = normalize(gram)
    second_term = jnp.dot(scaled_gram, first_iter, precision=high, preferred_element_type=jnp.float32)
    middle = 3.0 * identity - jnp.dot(first_iter, second_term, precision=high, preferred_element_type=jnp.float32)
    product = jnp.dot(block * inverse[None, :], middle, precision=high, preferred_element_type=jnp.float32)
    return jnp.dot(product, first_iter, precision=high, preferred_element_type=jnp.float32) * factor[None, :]

def reference(matrix, plan):
    blocks = matrix.reshape(ROWS, BLOCKS, BLK)
    slots = jnp.take(blocks, plan, axis=1)
    uppers = jnp.transpose(slots[:, 0::2, :], (1, 0, 2))
    lowers = jnp.transpose(slots[:, 1::2, :], (1, 0, 2))
    for turn_index in range(STEPS):
        joined = jnp.concatenate([uppers, lowers], axis=2)
        moved = lax.map(pair_step, joined)
        uppers = moved[:, :, :BLK]
        lowers = moved[:, :, BLK:]
        new_uppers = jnp.concatenate([uppers[0:1], lowers[0:1], uppers[1:N_PAIR - 1]], axis=0)
        new_lowers = jnp.concatenate([lowers[1:], uppers[N_PAIR - 1:]], axis=0)
        uppers, lowers = (new_uppers, new_lowers)
    stacked = jnp.stack([uppers, lowers], axis=1)
    return jnp.transpose(stacked, (2, 0, 1, 3)).reshape(ROWS, COLS)
```

```python
import jax
import jax.numpy as jnp
from jax import lax
from jax.sharding import PartitionSpec as P

BLK = 512
STEPS = 2


epsilon = 1e-06
high = lax.Precision.HIGHEST
fast = lax.Precision.HIGH


def from_behind(x, axis, by):
    count = lax.axis_size(axis)
    pairs = [(i, i + by) for i in range(count) if 0 <= i + by < count]
    return lax.ppermute(x, axis, pairs)


def inner_gram(left, right):
    return lax.dot_general(
        left, right, (((0,), (0,)), ((), ())), precision=high, preferred_element_type=jnp.float32
    )


def masked_diagonal(block):
    width = block.shape[0]
    eye = lax.broadcasted_iota(jnp.int32, (width, width), 0) == lax.broadcasted_iota(jnp.int32, (width, width), 1)
    return jnp.sum(jnp.where(eye, block, 0.0), axis=0)


def normalize(gram, diagonal):
    width = gram.shape[0]
    diagonal = diagonal + epsilon
    inverse = 1.0 / jnp.sqrt(diagonal)
    normed = gram * inverse[:, None] * inverse[None, :]
    spread = 1.5 * jnp.sqrt(jnp.sum(normed * normed)) / jnp.sqrt(jnp.float32(width))
    scaled_gram = normed / spread
    identity = jnp.eye(width, dtype=jnp.float32)
    first_iter = 0.5 * (3.0 * identity - scaled_gram)
    factor = 0.5 * jnp.sqrt(diagonal) / jnp.sqrt(spread)
    return (scaled_gram, first_iter, inverse, factor, identity)


def per_device(matrix, plan):
    local_rows = matrix.shape[0]
    blocks = matrix.reshape(local_rows, -1, BLK)
    slots = jnp.take(blocks, plan, axis=1).reshape(local_rows, -1)
    current = lax.all_to_all(slots, "pair", split_axis=1, concat_axis=0, tiled=True)
    pair_index = lax.axis_index("pair")
    pair_count = lax.axis_size("pair")
    for turn_index in range(STEPS):
        upper = current[:, :BLK]
        lower = current[:, BLK:]
        upper_gram, lower_gram, cross_gram = lax.psum(
            (inner_gram(upper, upper), inner_gram(lower, lower), inner_gram(upper, lower)), "rows"
        )
        gram = jnp.concatenate(
            [
                jnp.concatenate([upper_gram, cross_gram], axis=1),
                jnp.concatenate([cross_gram.T, lower_gram], axis=1),
            ],
            axis=0,
        )
        diagonal = jnp.concatenate([masked_diagonal(upper_gram), masked_diagonal(lower_gram)])
        scaled_gram, first_iter, inverse, factor, identity = normalize(gram, diagonal)
        weighted = current * inverse[None, :]
        second_term = jnp.dot(
            scaled_gram, first_iter, precision=fast, preferred_element_type=jnp.float32
        )
        middle = 3.0 * identity - jnp.dot(
            first_iter, second_term, precision=fast, preferred_element_type=jnp.float32
        )
        product = jnp.dot(weighted, middle, precision=fast, preferred_element_type=jnp.float32)
        current = (
            jnp.dot(product, first_iter, precision=fast, preferred_element_type=jnp.float32)
            * factor[None, :]
        )
        upper = current[:, :BLK]
        lower = current[:, BLK:]
        outgoing = jnp.where(pair_index == 0, lower, upper)
        arrived_up = from_behind(outgoing, "pair", 1)
        arrived_down = from_behind(lower, "pair", -1)
        new_upper = jnp.where(pair_index == 0, upper, arrived_up)
        new_lower = jnp.where(pair_index == pair_count - 1, upper, arrived_down)
        current = jnp.concatenate([new_upper, new_lower], axis=1)
    return current


def solution(mesh):
    placed = (P(("rows", "pair"), None), P())
    return jax.shard_map(
        per_device, mesh=mesh, in_specs=placed, out_specs=P("rows", "pair"), check_vma=False
    )
```

```python
import functools

import jax
import jax.numpy as jnp
from jax import lax
from jax.sharding import PartitionSpec as P

BLK = 512
STEPS = 2


epsilon = 1e-06
high = lax.Precision.HIGHEST
fast = lax.Precision.HIGH


def shifted(v, axis, count, by):
    return lax.ppermute(v, axis, [(i, (i + by) % count) for i in range(count)])


def scatter_sum(v, axis, count):
    me = lax.axis_index(axis)
    chunks = v.reshape(count, v.shape[0] // count, *v.shape[1:])
    total = lax.dynamic_index_in_dim(chunks, me, keepdims=False)
    for by in range(1, count):
        piece = lax.dynamic_index_in_dim(chunks, (me + by) % count, keepdims=False)
        total = total + shifted(piece, axis, count, by)
    return total


def gather_all(v, axis, count):
    me = lax.axis_index(axis)
    out = jnp.zeros((count,) + v.shape, v.dtype)
    out = lax.dynamic_update_index_in_dim(out, v, me, 0)
    for by in range(1, count):
        out = lax.dynamic_update_index_in_dim(out, shifted(v, axis, count, by), (me - by) % count, 0)
    return out.reshape(count * v.shape[0], *v.shape[1:])


def rows_sum(v, outer, inner):
    part = scatter_sum(scatter_sum(v, "x", inner), "ylo", outer)
    return gather_all(gather_all(part, "ylo", outer), "x", inner)


def summed_gram(upper, lower, outer, inner):
    width = upper.shape[1]
    row = lax.broadcasted_iota(jnp.int32, (width, width), 0)
    col = lax.broadcasted_iota(jnp.int32, (width, width), 1)
    upper_gram = inner_gram(upper, upper)
    lower_gram = inner_gram(lower, lower)
    cross_gram = inner_gram(upper, lower)
    packed = jnp.where(col >= row, upper_gram, lower_gram)
    tail = jnp.zeros((64, width), jnp.float32).at[0].set(masked_diagonal(lower_gram))
    total = rows_sum(jnp.concatenate([packed, cross_gram, tail]), outer, inner)
    packed, cross_gram, lower_diagonal = total[:width], total[width : 2 * width], total[2 * width]
    strict_upper = jnp.where(col > row, packed, 0.0)
    upper_gram = jnp.where(col >= row, packed, 0.0) + strict_upper.T
    strict_lower = jnp.where(col < row, packed, 0.0)
    lower_gram = strict_lower + strict_lower.T + jnp.where(col == row, lower_diagonal[None, :], 0.0)
    return upper_gram, lower_gram, cross_gram, masked_diagonal(packed), lower_diagonal


def from_behind(x, axis, by):
    count = lax.axis_size(axis)
    pairs = [(i, i + by) for i in range(count) if 0 <= i + by < count]
    return lax.ppermute(x, axis, pairs)


def inner_gram(left, right):
    return lax.dot_general(
        left, right, (((0,), (0,)), ((), ())), precision=high, preferred_element_type=jnp.float32
    )


def masked_diagonal(block):
    width = block.shape[0]
    eye = lax.broadcasted_iota(jnp.int32, (width, width), 0) == lax.broadcasted_iota(jnp.int32, (width, width), 1)
    return jnp.sum(jnp.where(eye, block, 0.0), axis=0)


def normalize(gram, diagonal):
    width = gram.shape[0]
    diagonal = diagonal + epsilon
    inverse = 1.0 / jnp.sqrt(diagonal)
    normed = gram * inverse[:, None] * inverse[None, :]
    spread = 1.5 * jnp.sqrt(jnp.sum(normed * normed)) / jnp.sqrt(jnp.float32(width))
    scaled_gram = normed / spread
    identity = jnp.eye(width, dtype=jnp.float32)
    first_iter = 0.5 * (3.0 * identity - scaled_gram)
    factor = 0.5 * jnp.sqrt(diagonal) / jnp.sqrt(spread)
    return (scaled_gram, first_iter, inverse, factor, identity)


def per_device(matrix, plan, outer, inner):
    local_rows = matrix.shape[0]
    blocks = matrix.reshape(local_rows, -1, BLK)
    slots = jnp.take(blocks, plan, axis=1).reshape(local_rows, -1)
    current = lax.all_to_all(slots, "pair", split_axis=1, concat_axis=0, tiled=True)
    pair_index = lax.axis_index("pair")
    pair_count = lax.axis_size("pair")
    for turn_index in range(STEPS):
        upper = current[:, :BLK]
        lower = current[:, BLK:]
        upper_gram, lower_gram, cross_gram, upper_diagonal, lower_diagonal = summed_gram(
            upper, lower, outer, inner
        )
        gram = jnp.concatenate(
            [
                jnp.concatenate([upper_gram, cross_gram], axis=1),
                jnp.concatenate([cross_gram.T, lower_gram], axis=1),
            ],
            axis=0,
        )
        diagonal = jnp.concatenate([upper_diagonal, lower_diagonal])
        scaled_gram, first_iter, inverse, factor, identity = normalize(gram, diagonal)
        weighted = current * inverse[None, :]
        second_term = jnp.dot(
            scaled_gram, first_iter, precision=fast, preferred_element_type=jnp.float32
        )
        middle = 3.0 * identity - jnp.dot(
            first_iter, second_term, precision=fast, preferred_element_type=jnp.float32
        )
        product = jnp.dot(weighted, middle, precision=fast, preferred_element_type=jnp.float32)
        current = (
            jnp.dot(product, first_iter, precision=fast, preferred_element_type=jnp.float32)
            * factor[None, :]
        )
        upper = current[:, :BLK]
        lower = current[:, BLK:]
        outgoing = jnp.where(pair_index == 0, lower, upper)
        arrived_up = from_behind(outgoing, "pair", 1)
        arrived_down = from_behind(lower, "pair", -1)
        new_upper = jnp.where(pair_index == 0, upper, arrived_up)
        new_lower = jnp.where(pair_index == pair_count - 1, upper, arrived_down)
        current = jnp.concatenate([new_upper, new_lower], axis=1)
    return current


def solution(mesh):
    pairs, rows = mesh.shape["pair"], mesh.shape["rows"]
    inner = 4
    outer = rows // inner
    split = jax.sharding.Mesh(mesh.devices.reshape(pairs, outer, inner), ("pair", "ylo", "x"))
    placed = (P(("ylo", "x", "pair"), None), P())
    return jax.shard_map(
        functools.partial(per_device, outer=outer, inner=inner),
        mesh=split,
        in_specs=placed,
        out_specs=P(("ylo", "x"), "pair"),
        check_vma=False,
    )
```

```python
import functools

import jax
import jax.numpy as jnp
from jax import lax
from jax.sharding import PartitionSpec as P

BLK = 512
STEPS = 2


epsilon = 1e-06
high = lax.Precision.HIGHEST
fast = lax.Precision.HIGH


def shifted(v, axis, count, by):
    return lax.ppermute(v, axis, [(i, (i + by) % count) for i in range(count)])


def scatter_sum(v, axis, count):
    me = lax.axis_index(axis)
    chunks = v.reshape(count, v.shape[0] // count, *v.shape[1:])
    total = lax.dynamic_index_in_dim(chunks, me, keepdims=False)
    for by in range(1, count):
        piece = lax.dynamic_index_in_dim(chunks, (me + by) % count, keepdims=False)
        total = total + shifted(piece, axis, count, by)
    return total


def gather_all(v, axis, count):
    me = lax.axis_index(axis)
    out = jnp.zeros((count,) + v.shape, v.dtype)
    out = lax.dynamic_update_index_in_dim(out, v, me, 0)
    for by in range(1, count):
        out = lax.dynamic_update_index_in_dim(out, shifted(v, axis, count, by), (me - by) % count, 0)
    return out.reshape(count * v.shape[0], *v.shape[1:])


def rows_sum(v, outer, inner):
    half = v.shape[1] // 2
    first, second = v[:, :half], v[:, half:]
    first = scatter_sum(scatter_sum(first, "x", inner), "ylo", outer)
    second = scatter_sum(scatter_sum(second, "ylo", outer), "x", inner)
    first = gather_all(gather_all(first, "ylo", outer), "x", inner)
    second = gather_all(gather_all(second, "x", inner), "ylo", outer)
    return jnp.concatenate([first, second], axis=1)


def summed_gram(upper, lower, outer, inner):
    width = upper.shape[1]
    row = lax.broadcasted_iota(jnp.int32, (width, width), 0)
    col = lax.broadcasted_iota(jnp.int32, (width, width), 1)
    upper_gram = inner_gram(upper, upper)
    lower_gram = inner_gram(lower, lower)
    cross_gram = inner_gram(upper, lower)
    packed = jnp.where(col >= row, upper_gram, lower_gram)
    tail = jnp.zeros((64, width), jnp.float32).at[0].set(masked_diagonal(lower_gram))
    total = rows_sum(jnp.concatenate([packed, cross_gram, tail]), outer, inner)
    packed, cross_gram, lower_diagonal = total[:width], total[width : 2 * width], total[2 * width]
    strict_upper = jnp.where(col > row, packed, 0.0)
    upper_gram = jnp.where(col >= row, packed, 0.0) + strict_upper.T
    strict_lower = jnp.where(col < row, packed, 0.0)
    lower_gram = strict_lower + strict_lower.T + jnp.where(col == row, lower_diagonal[None, :], 0.0)
    return upper_gram, lower_gram, cross_gram, masked_diagonal(packed), lower_diagonal


def from_behind(x, axis, by):
    count = lax.axis_size(axis)
    pairs = [(i, i + by) for i in range(count) if 0 <= i + by < count]
    return lax.ppermute(x, axis, pairs)


def inner_gram(left, right):
    return lax.dot_general(
        left, right, (((0,), (0,)), ((), ())), precision=high, preferred_element_type=jnp.float32
    )


def masked_diagonal(block):
    width = block.shape[0]
    eye = lax.broadcasted_iota(jnp.int32, (width, width), 0) == lax.broadcasted_iota(jnp.int32, (width, width), 1)
    return jnp.sum(jnp.where(eye, block, 0.0), axis=0)


def normalize(gram, diagonal):
    width = gram.shape[0]
    diagonal = diagonal + epsilon
    inverse = 1.0 / jnp.sqrt(diagonal)
    normed = gram * inverse[:, None] * inverse[None, :]
    spread = 1.5 * jnp.sqrt(jnp.sum(normed * normed)) / jnp.sqrt(jnp.float32(width))
    scaled_gram = normed / spread
    identity = jnp.eye(width, dtype=jnp.float32)
    first_iter = 0.5 * (3.0 * identity - scaled_gram)
    factor = 0.5 * jnp.sqrt(diagonal) / jnp.sqrt(spread)
    return (scaled_gram, first_iter, inverse, factor, identity)


def per_device(matrix, plan, outer, inner):
    local_rows = matrix.shape[0]
    blocks = matrix.reshape(local_rows, -1, BLK)
    slots = jnp.take(blocks, plan, axis=1).reshape(local_rows, -1)
    current = lax.all_to_all(slots, "pair", split_axis=1, concat_axis=0, tiled=True)
    pair_index = lax.axis_index("pair")
    pair_count = lax.axis_size("pair")
    for turn_index in range(STEPS):
        upper = current[:, :BLK]
        lower = current[:, BLK:]
        upper_gram, lower_gram, cross_gram, upper_diagonal, lower_diagonal = summed_gram(
            upper, lower, outer, inner
        )
        gram = jnp.concatenate(
            [
                jnp.concatenate([upper_gram, cross_gram], axis=1),
                jnp.concatenate([cross_gram.T, lower_gram], axis=1),
            ],
            axis=0,
        )
        diagonal = jnp.concatenate([upper_diagonal, lower_diagonal])
        scaled_gram, first_iter, inverse, factor, identity = normalize(gram, diagonal)
        weighted = current * inverse[None, :]
        second_term = jnp.dot(
            scaled_gram, first_iter, precision=fast, preferred_element_type=jnp.float32
        )
        middle = 3.0 * identity - jnp.dot(
            first_iter, second_term, precision=fast, preferred_element_type=jnp.float32
        )
        product = jnp.dot(weighted, middle, precision=fast, preferred_element_type=jnp.float32)
        current = (
            jnp.dot(product, first_iter, precision=fast, preferred_element_type=jnp.float32)
            * factor[None, :]
        )
        upper = current[:, :BLK]
        lower = current[:, BLK:]
        outgoing = jnp.where(pair_index == 0, lower, upper)
        arrived_up = from_behind(outgoing, "pair", 1)
        arrived_down = from_behind(lower, "pair", -1)
        new_upper = jnp.where(pair_index == 0, upper, arrived_up)
        new_lower = jnp.where(pair_index == pair_count - 1, upper, arrived_down)
        current = jnp.concatenate([new_upper, new_lower], axis=1)
    return current


def solution(mesh):
    pairs, rows = mesh.shape["pair"], mesh.shape["rows"]
    inner = 4
    outer = rows // inner
    split = jax.sharding.Mesh(mesh.devices.reshape(pairs, outer, inner), ("pair", "ylo", "x"))
    placed = (P(("ylo", "x", "pair"), None), P())
    return jax.shard_map(
        functools.partial(per_device, outer=outer, inner=inner),
        mesh=split,
        in_specs=placed,
        out_specs=P(("ylo", "x"), "pair"),
        check_vma=False,
    )
```

```python
import functools

import jax
import jax.numpy as jnp
from jax import lax
from jax.experimental import pallas as pl
from jax.experimental.pallas import tpu as pltpu
from jax.sharding import PartitionSpec as P

MESH = pl.DeviceIdType.MESH

BLK = 512
STEPS = 2


epsilon = 1e-06
high = lax.Precision.HIGHEST
fast = lax.Precision.HIGH


def shifted(v, axis, count, by):
    return lax.ppermute(v, axis, [(i, (i + by) % count) for i in range(count)])


def scatter_sum(v, axis, count):
    me = lax.axis_index(axis)
    chunks = v.reshape(count, v.shape[0] // count, *v.shape[1:])
    total = lax.dynamic_index_in_dim(chunks, me, keepdims=False)
    for by in range(1, count):
        piece = lax.dynamic_index_in_dim(chunks, (me + by) % count, keepdims=False)
        total = total + shifted(piece, axis, count, by)
    return total


def gather_all(v, axis, count):
    me = lax.axis_index(axis)
    out = jnp.zeros((count,) + v.shape, v.dtype)
    out = lax.dynamic_update_index_in_dim(out, v, me, 0)
    for by in range(1, count):
        out = lax.dynamic_update_index_in_dim(out, shifted(v, axis, count, by), (me - by) % count, 0)
    return out.reshape(count * v.shape[0], *v.shape[1:])


def rows_sum_kernel(
    outer, inner, payload, out, received, acc, halves, own, gathered, send_sem, recv_sem, y_send, y_recv, ag_send, ag_recv
):
    pair = lax.axis_index("pair")
    me_y = lax.axis_index("ylo")
    me_x = lax.axis_index("x")
    chunk = payload.shape[0] // inner
    half = chunk // outer
    partner = (me_y + 1) % outer

    barrier = pltpu.get_barrier_semaphore()
    for by in range(1, inner):
        pl.semaphore_signal(barrier, inc=1, device_id=(pair, me_y, (me_x + by) % inner), device_id_type=MESH)
    pl.semaphore_signal(barrier, inc=1, device_id=(pair, partner, me_x), device_id_type=MESH)
    pl.semaphore_wait(barrier, inner)

    copies = []
    for by in range(1, inner):
        target = (me_x + by) % inner
        copy = pltpu.make_async_remote_copy(
            src_ref=payload.at[pl.ds(pl.multiple_of(target * chunk, 8), chunk)],
            dst_ref=received.at[by - 1],
            send_sem=send_sem.at[by - 1],
            recv_sem=recv_sem.at[by - 1],
            device_id=(pair, me_y, target),
            device_id_type=MESH,
        )
        copy.start()
        copies.append(copy)
    for copy in copies:
        copy.wait()
    total = payload[pl.ds(pl.multiple_of(me_x * chunk, 8), chunk), :]
    for by in range(1, inner):
        total = total + received[by - 1]
    acc[...] = total

    copy = pltpu.make_async_remote_copy(
        src_ref=acc.at[pl.ds(pl.multiple_of(partner * half, 8), half)],
        dst_ref=halves.at[0],
        send_sem=y_send.at[0],
        recv_sem=y_recv.at[0],
        device_id=(pair, partner, me_x),
        device_id_type=MESH,
    )
    copy.start()
    copy.wait()
    own[...] = acc[pl.ds(pl.multiple_of(me_y * half, 8), half), :] + halves[0]

    copy = pltpu.make_async_remote_copy(
        src_ref=own,
        dst_ref=halves.at[1],
        send_sem=y_send.at[1],
        recv_sem=y_recv.at[1],
        device_id=(pair, partner, me_x),
        device_id_type=MESH,
    )
    copy.start()
    copy.wait()
    gathered[me_x, pl.ds(pl.multiple_of(me_y * half, 8), half), :] = own[...]
    gathered[me_x, pl.ds(pl.multiple_of(partner * half, 8), half), :] = halves[1]

    copies = []
    for by in range(1, inner):
        copy = pltpu.make_async_remote_copy(
            src_ref=gathered.at[me_x],
            dst_ref=gathered.at[me_x],
            send_sem=ag_send.at[by - 1],
            recv_sem=ag_recv.at[by - 1],
            device_id=(pair, me_y, (me_x + by) % inner),
            device_id_type=MESH,
        )
        copy.start()
        copies.append(copy)
    for copy in copies:
        copy.wait()
    for k in range(inner):
        out[pl.ds(k * chunk, chunk), :] = gathered[k]


def rows_sum(v, outer, inner):
    rows, width = v.shape
    chunk = rows // inner
    half = chunk // outer
    return pl.pallas_call(
        functools.partial(rows_sum_kernel, outer, inner),
        out_shape=jax.ShapeDtypeStruct(v.shape, v.dtype),
        in_specs=[pl.BlockSpec(memory_space=pltpu.VMEM)],
        out_specs=pl.BlockSpec(memory_space=pltpu.VMEM),
        scratch_shapes=[
            pltpu.VMEM((inner - 1, chunk, width), jnp.float32),
            pltpu.VMEM((chunk, width), jnp.float32),
            pltpu.VMEM((2, half, width), jnp.float32),
            pltpu.VMEM((half, width), jnp.float32),
            pltpu.VMEM((inner, chunk, width), jnp.float32),
            pltpu.SemaphoreType.DMA((inner - 1,)),
            pltpu.SemaphoreType.DMA((inner - 1,)),
            pltpu.SemaphoreType.DMA((2,)),
            pltpu.SemaphoreType.DMA((2,)),
            pltpu.SemaphoreType.DMA((inner - 1,)),
            pltpu.SemaphoreType.DMA((inner - 1,)),
        ],
        compiler_params=pltpu.CompilerParams(collective_id=0, has_side_effects=True),
    )(v)


def summed_gram(upper, lower, outer, inner):
    width = upper.shape[1]
    row = lax.broadcasted_iota(jnp.int32, (width, width), 0)
    col = lax.broadcasted_iota(jnp.int32, (width, width), 1)
    upper_gram = inner_gram(upper, upper)
    lower_gram = inner_gram(lower, lower)
    cross_gram = inner_gram(upper, lower)
    packed = jnp.where(col >= row, upper_gram, lower_gram)
    tail = jnp.zeros((64, width), jnp.float32).at[0].set(masked_diagonal(lower_gram))
    total = rows_sum(jnp.concatenate([packed, cross_gram, tail]), outer, inner)
    packed, cross_gram, lower_diagonal = total[:width], total[width : 2 * width], total[2 * width]
    strict_upper = jnp.where(col > row, packed, 0.0)
    upper_gram = jnp.where(col >= row, packed, 0.0) + strict_upper.T
    strict_lower = jnp.where(col < row, packed, 0.0)
    lower_gram = strict_lower + strict_lower.T + jnp.where(col == row, lower_diagonal[None, :], 0.0)
    return upper_gram, lower_gram, cross_gram, masked_diagonal(packed), lower_diagonal


def from_behind(x, axis, by):
    count = lax.axis_size(axis)
    pairs = [(i, i + by) for i in range(count) if 0 <= i + by < count]
    return lax.ppermute(x, axis, pairs)


def inner_gram(left, right):
    return lax.dot_general(
        left, right, (((0,), (0,)), ((), ())), precision=high, preferred_element_type=jnp.float32
    )


def masked_diagonal(block):
    width = block.shape[0]
    eye = lax.broadcasted_iota(jnp.int32, (width, width), 0) == lax.broadcasted_iota(jnp.int32, (width, width), 1)
    return jnp.sum(jnp.where(eye, block, 0.0), axis=0)


def normalize(gram, diagonal):
    width = gram.shape[0]
    diagonal = diagonal + epsilon
    inverse = 1.0 / jnp.sqrt(diagonal)
    normed = gram * inverse[:, None] * inverse[None, :]
    spread = 1.5 * jnp.sqrt(jnp.sum(normed * normed)) / jnp.sqrt(jnp.float32(width))
    scaled_gram = normed / spread
    identity = jnp.eye(width, dtype=jnp.float32)
    first_iter = 0.5 * (3.0 * identity - scaled_gram)
    factor = 0.5 * jnp.sqrt(diagonal) / jnp.sqrt(spread)
    return (scaled_gram, first_iter, inverse, factor, identity)


def per_device(matrix, plan, outer, inner):
    local_rows = matrix.shape[0]
    blocks = matrix.reshape(local_rows, -1, BLK)
    slots = jnp.take(blocks, plan, axis=1).reshape(local_rows, -1)
    current = lax.all_to_all(slots, "pair", split_axis=1, concat_axis=0, tiled=True)
    pair_index = lax.axis_index("pair")
    pair_count = lax.axis_size("pair")
    for turn_index in range(STEPS):
        upper = current[:, :BLK]
        lower = current[:, BLK:]
        upper_gram, lower_gram, cross_gram, upper_diagonal, lower_diagonal = summed_gram(
            upper, lower, outer, inner
        )
        gram = jnp.concatenate(
            [
                jnp.concatenate([upper_gram, cross_gram], axis=1),
                jnp.concatenate([cross_gram.T, lower_gram], axis=1),
            ],
            axis=0,
        )
        diagonal = jnp.concatenate([upper_diagonal, lower_diagonal])
        scaled_gram, first_iter, inverse, factor, identity = normalize(gram, diagonal)
        weighted = current * inverse[None, :]
        second_term = jnp.dot(
            scaled_gram, first_iter, precision=fast, preferred_element_type=jnp.float32
        )
        middle = 3.0 * identity - jnp.dot(
            first_iter, second_term, precision=fast, preferred_element_type=jnp.float32
        )
        product = jnp.dot(weighted, middle, precision=fast, preferred_element_type=jnp.float32)
        current = (
            jnp.dot(product, first_iter, precision=fast, preferred_element_type=jnp.float32)
            * factor[None, :]
        )
        upper = current[:, :BLK]
        lower = current[:, BLK:]
        outgoing = jnp.where(pair_index == 0, lower, upper)
        arrived_up = from_behind(outgoing, "pair", 1)
        arrived_down = from_behind(lower, "pair", -1)
        new_upper = jnp.where(pair_index == 0, upper, arrived_up)
        new_lower = jnp.where(pair_index == pair_count - 1, upper, arrived_down)
        current = jnp.concatenate([new_upper, new_lower], axis=1)
    return current


def solution(mesh):
    pairs, rows = mesh.shape["pair"], mesh.shape["rows"]
    inner = 4
    outer = rows // inner
    split = jax.sharding.Mesh(mesh.devices.reshape(pairs, outer, inner), ("pair", "ylo", "x"))
    placed = (P(("ylo", "x", "pair"), None), P())
    return jax.shard_map(
        functools.partial(per_device, outer=outer, inner=inner),
        mesh=split,
        in_specs=placed,
        out_specs=P(("ylo", "x"), "pair"),
        check_vma=False,
    )
```

```python
import functools

import jax
import jax.numpy as jnp
from jax import lax
from jax.experimental import pallas as pl
from jax.experimental.pallas import tpu as pltpu
from jax.sharding import PartitionSpec as P

MESH = pl.DeviceIdType.MESH

BLK = 512
STEPS = 2


epsilon = 1e-06
high = lax.Precision.HIGHEST
fast = lax.Precision.HIGH


def shifted(v, axis, count, by):
    return lax.ppermute(v, axis, [(i, (i + by) % count) for i in range(count)])


def scatter_sum(v, axis, count):
    me = lax.axis_index(axis)
    chunks = v.reshape(count, v.shape[0] // count, *v.shape[1:])
    total = lax.dynamic_index_in_dim(chunks, me, keepdims=False)
    for by in range(1, count):
        piece = lax.dynamic_index_in_dim(chunks, (me + by) % count, keepdims=False)
        total = total + shifted(piece, axis, count, by)
    return total


def gather_all(v, axis, count):
    me = lax.axis_index(axis)
    out = jnp.zeros((count,) + v.shape, v.dtype)
    out = lax.dynamic_update_index_in_dim(out, v, me, 0)
    for by in range(1, count):
        out = lax.dynamic_update_index_in_dim(out, shifted(v, axis, count, by), (me - by) % count, 0)
    return out.reshape(count * v.shape[0], *v.shape[1:])


def rows_sum_kernel(
    outer, inner, payload, out, received, acc, halves, own, gathered, send_sem, recv_sem, y_send, y_recv, ag_send, ag_recv
):
    pair = lax.axis_index("pair")
    me_y = lax.axis_index("ylo")
    me_x = lax.axis_index("x")
    chunk = payload.shape[0] // inner
    half = chunk // outer
    partner = (me_y + 1) % outer

    barrier = pltpu.get_barrier_semaphore()
    for by in range(1, inner):
        pl.semaphore_signal(barrier, inc=1, device_id=(pair, me_y, (me_x + by) % inner), device_id_type=MESH)
    pl.semaphore_signal(barrier, inc=1, device_id=(pair, partner, me_x), device_id_type=MESH)
    pl.semaphore_wait(barrier, inner)

    copies = []
    for by in range(1, inner):
        target = (me_x + by) % inner
        copy = pltpu.make_async_remote_copy(
            src_ref=payload.at[pl.ds(pl.multiple_of(target * chunk, 8), chunk)],
            dst_ref=received.at[by - 1],
            send_sem=send_sem.at[by - 1],
            recv_sem=recv_sem.at[by - 1],
            device_id=(pair, me_y, target),
            device_id_type=MESH,
        )
        copy.start()
        copies.append(copy)
    for copy in copies:
        copy.wait()
    total = payload[pl.ds(pl.multiple_of(me_x * chunk, 8), chunk), :]
    for by in range(1, inner):
        total = total + received[by - 1]
    acc[...] = total

    copy = pltpu.make_async_remote_copy(
        src_ref=acc.at[pl.ds(pl.multiple_of(partner * half, 8), half)],
        dst_ref=halves.at[0],
        send_sem=y_send.at[0],
        recv_sem=y_recv.at[0],
        device_id=(pair, partner, me_x),
        device_id_type=MESH,
    )
    copy.start()
    copy.wait()
    own[...] = acc[pl.ds(pl.multiple_of(me_y * half, 8), half), :] + halves[0]

    copy = pltpu.make_async_remote_copy(
        src_ref=own,
        dst_ref=halves.at[1],
        send_sem=y_send.at[1],
        recv_sem=y_recv.at[1],
        device_id=(pair, partner, me_x),
        device_id_type=MESH,
    )
    copy.start()
    copy.wait()
    gathered[me_x, pl.ds(pl.multiple_of(me_y * half, 8), half), :] = own[...]
    gathered[me_x, pl.ds(pl.multiple_of(partner * half, 8), half), :] = halves[1]

    copies = []
    for by in range(1, inner):
        copy = pltpu.make_async_remote_copy(
            src_ref=gathered.at[me_x],
            dst_ref=gathered.at[me_x],
            send_sem=ag_send.at[by - 1],
            recv_sem=ag_recv.at[by - 1],
            device_id=(pair, me_y, (me_x + by) % inner),
            device_id_type=MESH,
        )
        copy.start()
        copies.append(copy)
    for copy in copies:
        copy.wait()
    for k in range(inner):
        out[pl.ds(k * chunk, chunk), :] = gathered[k]


def rows_sum(v, outer, inner):
    rows, width = v.shape
    chunk = rows // inner
    half = chunk // outer
    return pl.pallas_call(
        functools.partial(rows_sum_kernel, outer, inner),
        out_shape=jax.ShapeDtypeStruct(v.shape, v.dtype),
        in_specs=[pl.BlockSpec(memory_space=pltpu.VMEM)],
        out_specs=pl.BlockSpec(memory_space=pltpu.VMEM),
        scratch_shapes=[
            pltpu.VMEM((inner - 1, chunk, width), jnp.float32),
            pltpu.VMEM((chunk, width), jnp.float32),
            pltpu.VMEM((2, half, width), jnp.float32),
            pltpu.VMEM((half, width), jnp.float32),
            pltpu.VMEM((inner, chunk, width), jnp.float32),
            pltpu.SemaphoreType.DMA((inner - 1,)),
            pltpu.SemaphoreType.DMA((inner - 1,)),
            pltpu.SemaphoreType.DMA((2,)),
            pltpu.SemaphoreType.DMA((2,)),
            pltpu.SemaphoreType.DMA((inner - 1,)),
            pltpu.SemaphoreType.DMA((inner - 1,)),
        ],
        compiler_params=pltpu.CompilerParams(collective_id=0, has_side_effects=True),
    )(v)


def summed_gram(upper, lower, outer, inner):
    width = upper.shape[1]
    row = lax.broadcasted_iota(jnp.int32, (width, width), 0)
    col = lax.broadcasted_iota(jnp.int32, (width, width), 1)
    upper_gram = inner_gram(upper, upper)
    lower_gram = inner_gram(lower, lower)
    cross_gram = inner_gram(upper, lower)
    packed = jnp.where(col >= row, upper_gram, lower_gram)
    tail = jnp.zeros((64, width), jnp.float32).at[0].set(masked_diagonal(lower_gram))
    total = rows_sum(jnp.concatenate([packed, cross_gram, tail]), outer, inner)
    packed, cross_gram, lower_diagonal = total[:width], total[width : 2 * width], total[2 * width]
    strict_upper = jnp.where(col > row, packed, 0.0)
    upper_gram = jnp.where(col >= row, packed, 0.0) + strict_upper.T
    strict_lower = jnp.where(col < row, packed, 0.0)
    lower_gram = strict_lower + strict_lower.T + jnp.where(col == row, lower_diagonal[None, :], 0.0)
    return upper_gram, lower_gram, cross_gram, masked_diagonal(packed), lower_diagonal


def from_behind(x, axis, by):
    count = lax.axis_size(axis)
    pairs = [(i, i + by) for i in range(count) if 0 <= i + by < count]
    return lax.ppermute(x, axis, pairs)


def inner_gram(left, right):
    return lax.dot_general(
        left, right, (((0,), (0,)), ((), ())), precision=fast, preferred_element_type=jnp.float32
    )


def masked_diagonal(block):
    width = block.shape[0]
    eye = lax.broadcasted_iota(jnp.int32, (width, width), 0) == lax.broadcasted_iota(jnp.int32, (width, width), 1)
    return jnp.sum(jnp.where(eye, block, 0.0), axis=0)


def normalize(gram, diagonal):
    width = gram.shape[0]
    diagonal = diagonal + epsilon
    inverse = 1.0 / jnp.sqrt(diagonal)
    normed = gram * inverse[:, None] * inverse[None, :]
    spread = 1.5 * jnp.sqrt(jnp.sum(normed * normed)) / jnp.sqrt(jnp.float32(width))
    scaled_gram = normed / spread
    identity = jnp.eye(width, dtype=jnp.float32)
    first_iter = 0.5 * (3.0 * identity - scaled_gram)
    factor = 0.5 * jnp.sqrt(diagonal) / jnp.sqrt(spread)
    return (scaled_gram, first_iter, inverse, factor, identity)


def per_device(matrix, plan, outer, inner):
    local_rows = matrix.shape[0]
    blocks = matrix.reshape(local_rows, -1, BLK)
    slots = jnp.take(blocks, plan, axis=1).reshape(local_rows, -1)
    current = lax.all_to_all(slots, "pair", split_axis=1, concat_axis=0, tiled=True)
    pair_index = lax.axis_index("pair")
    pair_count = lax.axis_size("pair")
    for turn_index in range(STEPS):
        upper = current[:, :BLK]
        lower = current[:, BLK:]
        upper_gram, lower_gram, cross_gram, upper_diagonal, lower_diagonal = summed_gram(
            upper, lower, outer, inner
        )
        gram = jnp.concatenate(
            [
                jnp.concatenate([upper_gram, cross_gram], axis=1),
                jnp.concatenate([cross_gram.T, lower_gram], axis=1),
            ],
            axis=0,
        )
        diagonal = jnp.concatenate([upper_diagonal, lower_diagonal])
        scaled_gram, first_iter, inverse, factor, identity = normalize(gram, diagonal)
        weighted = current * inverse[None, :]
        applied = jnp.dot(weighted, first_iter, precision=fast, preferred_element_type=jnp.float32)
        chain = jnp.dot(applied, scaled_gram, precision=fast, preferred_element_type=jnp.float32)
        chain = jnp.dot(chain, first_iter, precision=fast, preferred_element_type=jnp.float32)
        chain = jnp.dot(chain, first_iter, precision=fast, preferred_element_type=jnp.float32)
        current = (3.0 * applied - chain) * factor[None, :]
        upper = current[:, :BLK]
        lower = current[:, BLK:]
        outgoing = jnp.where(pair_index == 0, lower, upper)
        arrived_up = from_behind(outgoing, "pair", 1)
        arrived_down = from_behind(lower, "pair", -1)
        new_upper = jnp.where(pair_index == 0, upper, arrived_up)
        new_lower = jnp.where(pair_index == pair_count - 1, upper, arrived_down)
        current = jnp.concatenate([new_upper, new_lower], axis=1)
    return current


def solution(mesh):
    pairs, rows = mesh.shape["pair"], mesh.shape["rows"]
    inner = 4
    outer = rows // inner
    split = jax.sharding.Mesh(mesh.devices.reshape(pairs, outer, inner), ("pair", "ylo", "x"))
    placed = (P(("ylo", "x", "pair"), None), P())
    return jax.shard_map(
        functools.partial(per_device, outer=outer, inner=inner),
        mesh=split,
        in_specs=placed,
        out_specs=P(("ylo", "x"), "pair"),
        check_vma=False,
    )
```

```python
import functools

import jax
import jax.numpy as jnp
from jax import lax
from jax.experimental import pallas as pl
from jax.experimental.pallas import tpu as pltpu
from jax.sharding import PartitionSpec as P

MESH = pl.DeviceIdType.MESH

BLK = 512
STEPS = 2


epsilon = 1e-06
high = lax.Precision.HIGHEST
fast = lax.Precision.HIGH


def shifted(v, axis, count, by):
    return lax.ppermute(v, axis, [(i, (i + by) % count) for i in range(count)])


def scatter_sum(v, axis, count):
    me = lax.axis_index(axis)
    chunks = v.reshape(count, v.shape[0] // count, *v.shape[1:])
    total = lax.dynamic_index_in_dim(chunks, me, keepdims=False)
    for by in range(1, count):
        piece = lax.dynamic_index_in_dim(chunks, (me + by) % count, keepdims=False)
        total = total + shifted(piece, axis, count, by)
    return total


def gather_all(v, axis, count):
    me = lax.axis_index(axis)
    out = jnp.zeros((count,) + v.shape, v.dtype)
    out = lax.dynamic_update_index_in_dim(out, v, me, 0)
    for by in range(1, count):
        out = lax.dynamic_update_index_in_dim(out, shifted(v, axis, count, by), (me - by) % count, 0)
    return out.reshape(count * v.shape[0], *v.shape[1:])


def remote(src, dst, sends, recvs, slot, device):
    copy = pltpu.make_async_remote_copy(
        src_ref=src,
        dst_ref=dst,
        send_sem=sends.at[slot],
        recv_sem=recvs.at[slot],
        device_id=device,
        device_id_type=MESH,
    )
    copy.start()
    return copy


def rows_sum_kernel(
    outer, inner, payload, out, a_in, a_acc, a_halves, a_own, a_all, b_in, b_acc, b_parts, b_own, b_row, b_all, sends, recvs
):
    pair = lax.axis_index("pair")
    me_y = lax.axis_index("ylo")
    me_x = lax.axis_index("x")
    rows, width = payload.shape
    half_w = width // 2
    a_chunk = rows // inner
    a_half = a_chunk // outer
    b_half = rows // outer
    b_chunk = b_half // inner
    partner = (me_y + 1) % outer
    cols_a = pl.ds(0, half_w)
    cols_b = pl.ds(half_w, half_w)

    def x_peer(by):
        return (pair, me_y, (me_x + by) % inner)

    y_peer = (pair, partner, me_x)

    barrier = pltpu.get_barrier_semaphore()
    for by in range(1, inner):
        pl.semaphore_signal(barrier, inc=1, device_id=x_peer(by), device_id_type=MESH)
    pl.semaphore_signal(barrier, inc=1, device_id=y_peer, device_id_type=MESH)
    pl.semaphore_wait(barrier, inner)

    copies = []
    for by in range(1, inner):
        target = (me_x + by) % inner
        rows_k = pl.ds(pl.multiple_of(target * a_chunk, 8), a_chunk)
        copies.append(remote(payload.at[rows_k, cols_a], a_in.at[by - 1], sends, recvs, by - 1, x_peer(by)))
    rows_k = pl.ds(pl.multiple_of(partner * b_half, 8), b_half)
    copies.append(remote(payload.at[rows_k, cols_b], b_in, sends, recvs, 8, y_peer))
    for copy in copies:
        copy.wait()
    total = payload[pl.ds(pl.multiple_of(me_x * a_chunk, 8), a_chunk), cols_a]
    for by in range(1, inner):
        total = total + a_in[by - 1]
    a_acc[...] = total
    b_acc[...] = payload[pl.ds(pl.multiple_of(me_y * b_half, 8), b_half), cols_b] + b_in[...]

    copies = [
        remote(a_acc.at[pl.ds(pl.multiple_of(partner * a_half, 8), a_half)], a_halves.at[0], sends, recvs, 3, y_peer)
    ]
    for by in range(1, inner):
        target = (me_x + by) % inner
        rows_k = pl.ds(pl.multiple_of(target * b_chunk, 8), b_chunk)
        copies.append(remote(b_acc.at[rows_k], b_parts.at[by - 1], sends, recvs, 8 + by, x_peer(by)))
    for copy in copies:
        copy.wait()
    a_own[...] = a_acc[pl.ds(pl.multiple_of(me_y * a_half, 8), a_half), :] + a_halves[0]
    total = b_acc[pl.ds(pl.multiple_of(me_x * b_chunk, 8), b_chunk), :]
    for by in range(1, inner):
        total = total + b_parts[by - 1]
    b_own[...] = total

    copies = [remote(a_own, a_halves.at[1], sends, recvs, 4, y_peer)]
    for by in range(1, inner):
        copies.append(remote(b_own, b_row.at[me_x], sends, recvs, 11 + by, x_peer(by)))
    for copy in copies:
        copy.wait()
    a_all[me_x, pl.ds(pl.multiple_of(me_y * a_half, 8), a_half), :] = a_own[...]
    a_all[me_x, pl.ds(pl.multiple_of(partner * a_half, 8), a_half), :] = a_halves[1]
    b_row[me_x] = b_own[...]
    b_all[me_y] = b_row[...]

    copies = []
    for by in range(1, inner):
        copies.append(remote(a_all.at[me_x], a_all.at[me_x], sends, recvs, 4 + by, x_peer(by)))
    copies.append(remote(b_row, b_all.at[me_y], sends, recvs, 15, y_peer))
    for copy in copies:
        copy.wait()
    for k in range(inner):
        out[pl.ds(k * a_chunk, a_chunk), cols_a] = a_all[k]
    for j in range(outer):
        for k in range(inner):
            out[pl.ds(j * b_half + k * b_chunk, b_chunk), cols_b] = b_all[j, k]


def rows_sum(v, outer, inner):
    rows, width = v.shape
    half_w = width // 2
    a_chunk = rows // inner
    a_half = a_chunk // outer
    b_half = rows // outer
    b_chunk = b_half // inner
    return pl.pallas_call(
        functools.partial(rows_sum_kernel, outer, inner),
        out_shape=jax.ShapeDtypeStruct(v.shape, v.dtype),
        in_specs=[pl.BlockSpec(memory_space=pltpu.VMEM)],
        out_specs=pl.BlockSpec(memory_space=pltpu.VMEM),
        scratch_shapes=[
            pltpu.VMEM((inner - 1, a_chunk, half_w), jnp.float32),
            pltpu.VMEM((a_chunk, half_w), jnp.float32),
            pltpu.VMEM((2, a_half, half_w), jnp.float32),
            pltpu.VMEM((a_half, half_w), jnp.float32),
            pltpu.VMEM((inner, a_chunk, half_w), jnp.float32),
            pltpu.VMEM((b_half, half_w), jnp.float32),
            pltpu.VMEM((b_half, half_w), jnp.float32),
            pltpu.VMEM((inner - 1, b_chunk, half_w), jnp.float32),
            pltpu.VMEM((b_chunk, half_w), jnp.float32),
            pltpu.VMEM((inner, b_chunk, half_w), jnp.float32),
            pltpu.VMEM((outer, inner, b_chunk, half_w), jnp.float32),
            pltpu.SemaphoreType.DMA((16,)),
            pltpu.SemaphoreType.DMA((16,)),
        ],
        compiler_params=pltpu.CompilerParams(collective_id=0, has_side_effects=True),
    )(v)


def summed_gram(upper, lower, outer, inner):
    width = upper.shape[1]
    row = lax.broadcasted_iota(jnp.int32, (width, width), 0)
    col = lax.broadcasted_iota(jnp.int32, (width, width), 1)
    upper_gram = inner_gram(upper, upper)
    lower_gram = inner_gram(lower, lower)
    cross_gram = inner_gram(upper, lower)
    packed = jnp.where(col >= row, upper_gram, lower_gram)
    tail = jnp.zeros((64, width), jnp.float32).at[0].set(masked_diagonal(lower_gram))
    total = rows_sum(jnp.concatenate([packed, cross_gram, tail]), outer, inner)
    packed, cross_gram, lower_diagonal = total[:width], total[width : 2 * width], total[2 * width]
    strict_upper = jnp.where(col > row, packed, 0.0)
    upper_gram = jnp.where(col >= row, packed, 0.0) + strict_upper.T
    strict_lower = jnp.where(col < row, packed, 0.0)
    lower_gram = strict_lower + strict_lower.T + jnp.where(col == row, lower_diagonal[None, :], 0.0)
    return upper_gram, lower_gram, cross_gram, masked_diagonal(packed), lower_diagonal


def from_behind(x, axis, by):
    count = lax.axis_size(axis)
    pairs = [(i, i + by) for i in range(count) if 0 <= i + by < count]
    return lax.ppermute(x, axis, pairs)


def inner_gram(left, right):
    return lax.dot_general(
        left, right, (((0,), (0,)), ((), ())), precision=fast, preferred_element_type=jnp.float32
    )


def masked_diagonal(block):
    width = block.shape[0]
    eye = lax.broadcasted_iota(jnp.int32, (width, width), 0) == lax.broadcasted_iota(jnp.int32, (width, width), 1)
    return jnp.sum(jnp.where(eye, block, 0.0), axis=0)


def normalize(gram, diagonal):
    width = gram.shape[0]
    diagonal = diagonal + epsilon
    inverse = 1.0 / jnp.sqrt(diagonal)
    normed = gram * inverse[:, None] * inverse[None, :]
    spread = 1.5 * jnp.sqrt(jnp.sum(normed * normed)) / jnp.sqrt(jnp.float32(width))
    scaled_gram = normed / spread
    identity = jnp.eye(width, dtype=jnp.float32)
    first_iter = 0.5 * (3.0 * identity - scaled_gram)
    factor = 0.5 * jnp.sqrt(diagonal) / jnp.sqrt(spread)
    return (scaled_gram, first_iter, inverse, factor, identity)


def per_device(matrix, plan, outer, inner):
    local_rows = matrix.shape[0]
    blocks = matrix.reshape(local_rows, -1, BLK)
    slots = jnp.take(blocks, plan, axis=1).reshape(local_rows, -1)
    current = lax.all_to_all(slots, "pair", split_axis=1, concat_axis=0, tiled=True)
    pair_index = lax.axis_index("pair")
    pair_count = lax.axis_size("pair")
    for turn_index in range(STEPS):
        upper = current[:, :BLK]
        lower = current[:, BLK:]
        upper_gram, lower_gram, cross_gram, upper_diagonal, lower_diagonal = summed_gram(
            upper, lower, outer, inner
        )
        gram = jnp.concatenate(
            [
                jnp.concatenate([upper_gram, cross_gram], axis=1),
                jnp.concatenate([cross_gram.T, lower_gram], axis=1),
            ],
            axis=0,
        )
        diagonal = jnp.concatenate([upper_diagonal, lower_diagonal])
        scaled_gram, first_iter, inverse, factor, identity = normalize(gram, diagonal)
        weighted = current * inverse[None, :]
        applied = jnp.dot(weighted, first_iter, precision=fast, preferred_element_type=jnp.float32)
        chain = jnp.dot(applied, scaled_gram, precision=fast, preferred_element_type=jnp.float32)
        chain = jnp.dot(chain, first_iter, precision=fast, preferred_element_type=jnp.float32)
        chain = jnp.dot(chain, first_iter, precision=fast, preferred_element_type=jnp.float32)
        current = (3.0 * applied - chain) * factor[None, :]
        upper = current[:, :BLK]
        lower = current[:, BLK:]
        outgoing = jnp.where(pair_index == 0, lower, upper)
        arrived_up = from_behind(outgoing, "pair", 1)
        arrived_down = from_behind(lower, "pair", -1)
        new_upper = jnp.where(pair_index == 0, upper, arrived_up)
        new_lower = jnp.where(pair_index == pair_count - 1, upper, arrived_down)
        current = jnp.concatenate([new_upper, new_lower], axis=1)
    return current


def solution(mesh):
    pairs, rows = mesh.shape["pair"], mesh.shape["rows"]
    inner = 4
    outer = rows // inner
    split = jax.sharding.Mesh(mesh.devices.reshape(pairs, outer, inner), ("pair", "ylo", "x"))
    placed = (P(("ylo", "x", "pair"), None), P())
    return jax.shard_map(
        functools.partial(per_device, outer=outer, inner=inner),
        mesh=split,
        in_specs=placed,
        out_specs=P(("ylo", "x"), "pair"),
        check_vma=False,
    )
```

```python
import functools

import jax
import jax.numpy as jnp
from jax import lax
from jax.experimental import pallas as pl
from jax.experimental.pallas import tpu as pltpu
from jax.sharding import PartitionSpec as P

MESH = pl.DeviceIdType.MESH

BLK = 512
STEPS = 2


epsilon = 1e-06
high = lax.Precision.HIGHEST
fast = lax.Precision.HIGH


def shifted(v, axis, count, by):
    return lax.ppermute(v, axis, [(i, (i + by) % count) for i in range(count)])


def scatter_sum(v, axis, count):
    me = lax.axis_index(axis)
    chunks = v.reshape(count, v.shape[0] // count, *v.shape[1:])
    total = lax.dynamic_index_in_dim(chunks, me, keepdims=False)
    for by in range(1, count):
        piece = lax.dynamic_index_in_dim(chunks, (me + by) % count, keepdims=False)
        total = total + shifted(piece, axis, count, by)
    return total


def gather_all(v, axis, count):
    me = lax.axis_index(axis)
    out = jnp.zeros((count,) + v.shape, v.dtype)
    out = lax.dynamic_update_index_in_dim(out, v, me, 0)
    for by in range(1, count):
        out = lax.dynamic_update_index_in_dim(out, shifted(v, axis, count, by), (me - by) % count, 0)
    return out.reshape(count * v.shape[0], *v.shape[1:])


def remote(src, dst, sends, recvs, slot, device):
    copy = pltpu.make_async_remote_copy(
        src_ref=src,
        dst_ref=dst,
        send_sem=sends.at[slot],
        recv_sem=recvs.at[slot],
        device_id=device,
        device_id_type=MESH,
    )
    copy.start()
    return copy


def rows_sum_kernel(
    outer, inner, payload, out, a_in, a_acc, a_halves, a_own, a_all, b_in, b_acc, b_parts, b_own, b_row, b_all, sends, recvs
):
    pair = lax.axis_index("pair")
    me_y = lax.axis_index("ylo")
    me_x = lax.axis_index("x")
    rows, width = payload.shape
    half_w = width // 2
    a_chunk = rows // inner
    a_half = a_chunk // outer
    b_half = rows // outer
    b_chunk = b_half // inner
    partner = (me_y + 1) % outer
    cols_a = pl.ds(0, half_w)
    cols_b = pl.ds(half_w, half_w)

    def x_peer(by):
        return (pair, me_y, (me_x + by) % inner)

    y_peer = (pair, partner, me_x)

    barrier = pltpu.get_barrier_semaphore()
    for by in range(1, inner):
        pl.semaphore_signal(barrier, inc=1, device_id=x_peer(by), device_id_type=MESH)
    pl.semaphore_signal(barrier, inc=1, device_id=y_peer, device_id_type=MESH)
    pl.semaphore_wait(barrier, inner)

    copies = []
    for by in range(1, inner):
        target = (me_x + by) % inner
        rows_k = pl.ds(pl.multiple_of(target * a_chunk, 8), a_chunk)
        copies.append(remote(payload.at[rows_k, cols_a], a_in.at[by - 1], sends, recvs, by - 1, x_peer(by)))
    rows_k = pl.ds(pl.multiple_of(partner * b_half, 8), b_half)
    copies.append(remote(payload.at[rows_k, cols_b], b_in, sends, recvs, 8, y_peer))
    for copy in copies:
        copy.wait()
    total = payload[pl.ds(pl.multiple_of(me_x * a_chunk, 8), a_chunk), cols_a]
    for by in range(1, inner):
        total = total + a_in[by - 1]
    a_acc[...] = total
    b_acc[...] = payload[pl.ds(pl.multiple_of(me_y * b_half, 8), b_half), cols_b] + b_in[...]

    copies = [
        remote(a_acc.at[pl.ds(pl.multiple_of(partner * a_half, 8), a_half)], a_halves.at[0], sends, recvs, 3, y_peer)
    ]
    for by in range(1, inner):
        target = (me_x + by) % inner
        rows_k = pl.ds(pl.multiple_of(target * b_chunk, 8), b_chunk)
        copies.append(remote(b_acc.at[rows_k], b_parts.at[by - 1], sends, recvs, 8 + by, x_peer(by)))
    for copy in copies:
        copy.wait()
    a_own[...] = a_acc[pl.ds(pl.multiple_of(me_y * a_half, 8), a_half), :] + a_halves[0]
    total = b_acc[pl.ds(pl.multiple_of(me_x * b_chunk, 8), b_chunk), :]
    for by in range(1, inner):
        total = total + b_parts[by - 1]
    b_own[...] = total

    copies = [remote(a_own, a_halves.at[1], sends, recvs, 4, y_peer)]
    for by in range(1, inner):
        copies.append(remote(b_own, b_row.at[me_x], sends, recvs, 11 + by, x_peer(by)))
    for copy in copies:
        copy.wait()
    a_all[me_x, pl.ds(pl.multiple_of(me_y * a_half, 8), a_half), :] = a_own[...]
    a_all[me_x, pl.ds(pl.multiple_of(partner * a_half, 8), a_half), :] = a_halves[1]
    b_row[me_x] = b_own[...]
    b_all[me_y] = b_row[...]

    copies = []
    for by in range(1, inner):
        copies.append(remote(a_all.at[me_x], a_all.at[me_x], sends, recvs, 4 + by, x_peer(by)))
    copies.append(remote(b_row, b_all.at[me_y], sends, recvs, 15, y_peer))
    for copy in copies:
        copy.wait()
    for k in range(inner):
        out[pl.ds(k * a_chunk, a_chunk), cols_a] = a_all[k]
    for j in range(outer):
        for k in range(inner):
            out[pl.ds(j * b_half + k * b_chunk, b_chunk), cols_b] = b_all[j, k]


def rows_sum(v, outer, inner):
    rows, width = v.shape
    half_w = width // 2
    a_chunk = rows // inner
    a_half = a_chunk // outer
    b_half = rows // outer
    b_chunk = b_half // inner
    return pl.pallas_call(
        functools.partial(rows_sum_kernel, outer, inner),
        out_shape=jax.ShapeDtypeStruct(v.shape, v.dtype),
        in_specs=[pl.BlockSpec(memory_space=pltpu.VMEM)],
        out_specs=pl.BlockSpec(memory_space=pltpu.VMEM),
        scratch_shapes=[
            pltpu.VMEM((inner - 1, a_chunk, half_w), jnp.float32),
            pltpu.VMEM((a_chunk, half_w), jnp.float32),
            pltpu.VMEM((2, a_half, half_w), jnp.float32),
            pltpu.VMEM((a_half, half_w), jnp.float32),
            pltpu.VMEM((inner, a_chunk, half_w), jnp.float32),
            pltpu.VMEM((b_half, half_w), jnp.float32),
            pltpu.VMEM((b_half, half_w), jnp.float32),
            pltpu.VMEM((inner - 1, b_chunk, half_w), jnp.float32),
            pltpu.VMEM((b_chunk, half_w), jnp.float32),
            pltpu.VMEM((inner, b_chunk, half_w), jnp.float32),
            pltpu.VMEM((outer, inner, b_chunk, half_w), jnp.float32),
            pltpu.SemaphoreType.DMA((16,)),
            pltpu.SemaphoreType.DMA((16,)),
        ],
        compiler_params=pltpu.CompilerParams(collective_id=0, has_side_effects=True),
    )(v)


def exchange_kernel(count, slots, out, landing, sends, recvs):
    me = lax.axis_index("pair")
    me_y = lax.axis_index("ylo")
    me_x = lax.axis_index("x")
    rows = slots.shape[0]
    width = out.shape[1]
    barrier = pltpu.get_barrier_semaphore()
    for by in range(1, count):
        pl.semaphore_signal(barrier, inc=1, device_id=((me + by) % count, me_y, me_x), device_id_type=MESH)
    pl.semaphore_wait(barrier, count - 1)
    copies = []
    for by in range(1, count):
        target = (me + by) % count
        copies.append(
            remote(
                slots.at[:, pl.ds(pl.multiple_of(target * width, width), width)],
                landing.at[pl.ds(pl.multiple_of(me * rows, 8), rows)],
                sends,
                recvs,
                by,
                (target, me_y, me_x),
            )
        )
    landing[pl.ds(pl.multiple_of(me * rows, 8), rows), :] = slots[:, pl.ds(pl.multiple_of(me * width, width), width)]
    for copy in copies:
        copy.wait()
    out[...] = landing[...]


def exchange(slots, count):
    rows, columns = slots.shape
    width = columns // count
    return pl.pallas_call(
        functools.partial(exchange_kernel, count),
        out_shape=jax.ShapeDtypeStruct((rows * count, width), slots.dtype),
        in_specs=[pl.BlockSpec(memory_space=pltpu.VMEM)],
        out_specs=pl.BlockSpec(memory_space=pltpu.VMEM),
        scratch_shapes=[
            pltpu.VMEM((rows * count, width), jnp.float32),
            pltpu.SemaphoreType.DMA((count,)),
            pltpu.SemaphoreType.DMA((count,)),
        ],
        compiler_params=pltpu.CompilerParams(collective_id=1, has_side_effects=True),
    )(slots)


def summed_gram(upper, lower, outer, inner):
    width = upper.shape[1]
    row = lax.broadcasted_iota(jnp.int32, (width, width), 0)
    col = lax.broadcasted_iota(jnp.int32, (width, width), 1)
    upper_gram = inner_gram(upper, upper)
    lower_gram = inner_gram(lower, lower)
    cross_gram = inner_gram(upper, lower)
    packed = jnp.where(col >= row, upper_gram, lower_gram)
    tail = jnp.zeros((64, width), jnp.float32).at[0].set(masked_diagonal(lower_gram))
    total = rows_sum(jnp.concatenate([packed, cross_gram, tail]), outer, inner)
    packed, cross_gram, lower_diagonal = total[:width], total[width : 2 * width], total[2 * width]
    strict_upper = jnp.where(col > row, packed, 0.0)
    upper_gram = jnp.where(col >= row, packed, 0.0) + strict_upper.T
    strict_lower = jnp.where(col < row, packed, 0.0)
    lower_gram = strict_lower + strict_lower.T + jnp.where(col == row, lower_diagonal[None, :], 0.0)
    return upper_gram, lower_gram, cross_gram, masked_diagonal(packed), lower_diagonal


def from_behind(x, axis, by):
    count = lax.axis_size(axis)
    pairs = [(i, i + by) for i in range(count) if 0 <= i + by < count]
    return lax.ppermute(x, axis, pairs)


def inner_gram(left, right):
    return lax.dot_general(
        left, right, (((0,), (0,)), ((), ())), precision=fast, preferred_element_type=jnp.float32
    )


def masked_diagonal(block):
    width = block.shape[0]
    eye = lax.broadcasted_iota(jnp.int32, (width, width), 0) == lax.broadcasted_iota(jnp.int32, (width, width), 1)
    return jnp.sum(jnp.where(eye, block, 0.0), axis=0)


def normalize(gram, diagonal):
    width = gram.shape[0]
    diagonal = diagonal + epsilon
    inverse = 1.0 / jnp.sqrt(diagonal)
    normed = gram * inverse[:, None] * inverse[None, :]
    spread = 1.5 * jnp.sqrt(jnp.sum(normed * normed)) / jnp.sqrt(jnp.float32(width))
    scaled_gram = normed / spread
    identity = jnp.eye(width, dtype=jnp.float32)
    first_iter = 0.5 * (3.0 * identity - scaled_gram)
    factor = 0.5 * jnp.sqrt(diagonal) / jnp.sqrt(spread)
    return (scaled_gram, first_iter, inverse, factor, identity)


def per_device(matrix, plan, outer, inner):
    local_rows = matrix.shape[0]
    blocks = matrix.reshape(local_rows, -1, BLK)
    slots = jnp.take(blocks, plan, axis=1).reshape(local_rows, -1)
    current = exchange(slots, lax.axis_size("pair"))
    pair_index = lax.axis_index("pair")
    pair_count = lax.axis_size("pair")
    for turn_index in range(STEPS):
        upper = current[:, :BLK]
        lower = current[:, BLK:]
        upper_gram, lower_gram, cross_gram, upper_diagonal, lower_diagonal = summed_gram(
            upper, lower, outer, inner
        )
        gram = jnp.concatenate(
            [
                jnp.concatenate([upper_gram, cross_gram], axis=1),
                jnp.concatenate([cross_gram.T, lower_gram], axis=1),
            ],
            axis=0,
        )
        diagonal = jnp.concatenate([upper_diagonal, lower_diagonal])
        scaled_gram, first_iter, inverse, factor, identity = normalize(gram, diagonal)
        weighted = current * inverse[None, :]
        applied = jnp.dot(weighted, first_iter, precision=fast, preferred_element_type=jnp.float32)
        chain = jnp.dot(applied, scaled_gram, precision=fast, preferred_element_type=jnp.float32)
        chain = jnp.dot(chain, first_iter, precision=fast, preferred_element_type=jnp.float32)
        chain = jnp.dot(chain, first_iter, precision=fast, preferred_element_type=jnp.float32)
        current = (3.0 * applied - chain) * factor[None, :]
        upper = current[:, :BLK]
        lower = current[:, BLK:]
        outgoing = jnp.where(pair_index == 0, lower, upper)
        arrived_up = from_behind(outgoing, "pair", 1)
        arrived_down = from_behind(lower, "pair", -1)
        new_upper = jnp.where(pair_index == 0, upper, arrived_up)
        new_lower = jnp.where(pair_index == pair_count - 1, upper, arrived_down)
        current = jnp.concatenate([new_upper, new_lower], axis=1)
    return current


def solution(mesh):
    pairs, rows = mesh.shape["pair"], mesh.shape["rows"]
    inner = 4
    outer = rows // inner
    split = jax.sharding.Mesh(mesh.devices.reshape(pairs, outer, inner), ("pair", "ylo", "x"))
    placed = (P(("ylo", "x", "pair"), None), P())
    return jax.shard_map(
        functools.partial(per_device, outer=outer, inner=inner),
        mesh=split,
        in_specs=placed,
        out_specs=P(("ylo", "x"), "pair"),
        check_vma=False,
    )
```

```python
import functools

import jax
import jax.numpy as jnp
from jax import lax
from jax.experimental import pallas as pl
from jax.experimental.pallas import tpu as pltpu
from jax.sharding import PartitionSpec as P

MESH = pl.DeviceIdType.MESH

BLK = 512
STEPS = 2


epsilon = 1e-06
high = lax.Precision.HIGHEST
fast = lax.Precision.HIGH


def shifted(v, axis, count, by):
    return lax.ppermute(v, axis, [(i, (i + by) % count) for i in range(count)])


def scatter_sum(v, axis, count):
    me = lax.axis_index(axis)
    chunks = v.reshape(count, v.shape[0] // count, *v.shape[1:])
    total = lax.dynamic_index_in_dim(chunks, me, keepdims=False)
    for by in range(1, count):
        piece = lax.dynamic_index_in_dim(chunks, (me + by) % count, keepdims=False)
        total = total + shifted(piece, axis, count, by)
    return total


def gather_all(v, axis, count):
    me = lax.axis_index(axis)
    out = jnp.zeros((count,) + v.shape, v.dtype)
    out = lax.dynamic_update_index_in_dim(out, v, me, 0)
    for by in range(1, count):
        out = lax.dynamic_update_index_in_dim(out, shifted(v, axis, count, by), (me - by) % count, 0)
    return out.reshape(count * v.shape[0], *v.shape[1:])


def remote(src, dst, sends, recvs, slot, device):
    copy = pltpu.make_async_remote_copy(
        src_ref=src,
        dst_ref=dst,
        send_sem=sends.at[slot],
        recv_sem=recvs.at[slot],
        device_id=device,
        device_id_type=MESH,
    )
    copy.start()
    return copy


def rows_sum_kernel(
    outer,
    inner,
    payload,
    scaled_out,
    first_out,
    inverse_out,
    factor_out,
    a_in,
    a_acc,
    a_halves,
    a_own,
    a_all,
    b_in,
    b_acc,
    b_parts,
    b_own,
    b_row,
    b_all,
    out,
    sends,
    recvs,
):
    pair = lax.axis_index("pair")
    me_y = lax.axis_index("ylo")
    me_x = lax.axis_index("x")
    rows, width = payload.shape
    half_w = width // 2
    a_chunk = rows // inner
    a_half = a_chunk // outer
    b_half = rows // outer
    b_chunk = b_half // inner
    partner = (me_y + 1) % outer
    cols_a = pl.ds(0, half_w)
    cols_b = pl.ds(half_w, half_w)

    def x_peer(by):
        return (pair, me_y, (me_x + by) % inner)

    y_peer = (pair, partner, me_x)

    barrier = pltpu.get_barrier_semaphore()
    for by in range(1, inner):
        pl.semaphore_signal(barrier, inc=1, device_id=x_peer(by), device_id_type=MESH)
    pl.semaphore_signal(barrier, inc=1, device_id=y_peer, device_id_type=MESH)
    pl.semaphore_wait(barrier, inner)

    copies = []
    for by in range(1, inner):
        target = (me_x + by) % inner
        rows_k = pl.ds(pl.multiple_of(target * a_chunk, 8), a_chunk)
        copies.append(remote(payload.at[rows_k, cols_a], a_in.at[by - 1], sends, recvs, by - 1, x_peer(by)))
    rows_k = pl.ds(pl.multiple_of(partner * b_half, 8), b_half)
    copies.append(remote(payload.at[rows_k, cols_b], b_in, sends, recvs, 8, y_peer))
    for copy in copies:
        copy.wait()
    total = payload[pl.ds(pl.multiple_of(me_x * a_chunk, 8), a_chunk), cols_a]
    for by in range(1, inner):
        total = total + a_in[by - 1]
    a_acc[...] = total
    b_acc[...] = payload[pl.ds(pl.multiple_of(me_y * b_half, 8), b_half), cols_b] + b_in[...]

    copies = [
        remote(a_acc.at[pl.ds(pl.multiple_of(partner * a_half, 8), a_half)], a_halves.at[0], sends, recvs, 3, y_peer)
    ]
    for by in range(1, inner):
        target = (me_x + by) % inner
        rows_k = pl.ds(pl.multiple_of(target * b_chunk, 8), b_chunk)
        copies.append(remote(b_acc.at[rows_k], b_parts.at[by - 1], sends, recvs, 8 + by, x_peer(by)))
    for copy in copies:
        copy.wait()
    a_own[...] = a_acc[pl.ds(pl.multiple_of(me_y * a_half, 8), a_half), :] + a_halves[0]
    total = b_acc[pl.ds(pl.multiple_of(me_x * b_chunk, 8), b_chunk), :]
    for by in range(1, inner):
        total = total + b_parts[by - 1]
    b_own[...] = total

    copies = [remote(a_own, a_halves.at[1], sends, recvs, 4, y_peer)]
    for by in range(1, inner):
        copies.append(remote(b_own, b_row.at[me_x], sends, recvs, 11 + by, x_peer(by)))
    for copy in copies:
        copy.wait()
    a_all[me_x, pl.ds(pl.multiple_of(me_y * a_half, 8), a_half), :] = a_own[...]
    a_all[me_x, pl.ds(pl.multiple_of(partner * a_half, 8), a_half), :] = a_halves[1]
    b_row[me_x] = b_own[...]
    b_all[me_y] = b_row[...]

    copies = []
    for by in range(1, inner):
        copies.append(remote(a_all.at[me_x], a_all.at[me_x], sends, recvs, 4 + by, x_peer(by)))
    copies.append(remote(b_row, b_all.at[me_y], sends, recvs, 15, y_peer))
    for copy in copies:
        copy.wait()
    for k in range(inner):
        out[pl.ds(k * a_chunk, a_chunk), cols_a] = a_all[k]
    for j in range(outer):
        for k in range(inner):
            out[pl.ds(j * b_half + k * b_chunk, b_chunk), cols_b] = b_all[j, k]
    normalize_packed(out, scaled_out, first_out, inverse_out, factor_out)


def normalize_packed(packed, scaled_out, first_out, inverse_out, factor_out):
    width = packed.shape[1]
    row = lax.broadcasted_iota(jnp.int32, (width, width), 0)
    col = lax.broadcasted_iota(jnp.int32, (width, width), 1)
    eye = row == col
    top = packed[pl.ds(0, width), :]
    cross = packed[pl.ds(width, width), :]
    lower_diagonal = packed[pl.ds(2 * width, 1), :]
    strict_upper = jnp.where(col > row, top, 0.0)
    upper = jnp.where(col >= row, top, 0.0) + strict_upper.T
    strict_lower = jnp.where(col < row, top, 0.0)
    lower = strict_lower + strict_lower.T + jnp.where(eye, lower_diagonal, 0.0)
    upper_row = jnp.sum(jnp.where(eye, top, 0.0), axis=0, keepdims=True) + epsilon
    upper_col = jnp.sum(jnp.where(eye, top, 0.0), axis=1, keepdims=True) + epsilon
    lower_row = lower_diagonal + epsilon
    lower_col = jnp.sum(jnp.where(eye, lower, 0.0), axis=1, keepdims=True) + epsilon
    inv_upper_row, inv_upper_col = 1.0 / jnp.sqrt(upper_row), 1.0 / jnp.sqrt(upper_col)
    inv_lower_row, inv_lower_col = 1.0 / jnp.sqrt(lower_row), 1.0 / jnp.sqrt(lower_col)
    upper = upper * inv_upper_col * inv_upper_row
    lower = lower * inv_lower_col * inv_lower_row
    cross = cross * inv_upper_col * inv_lower_row

    def total(v):
        return jnp.sum(jnp.sum(v * v, axis=0, keepdims=True), axis=1, keepdims=True)

    squares = total(upper) + total(lower) + 2.0 * total(cross)
    spread = 1.5 * jnp.sqrt(squares) / jnp.sqrt(jnp.float32(2 * width))
    upper = upper / spread
    lower = lower / spread
    cross = cross / spread
    three = jnp.where(eye, 3.0, 0.0)
    near, far = pl.ds(0, width), pl.ds(width, width)
    scaled_out[near, near] = upper
    scaled_out[near, far] = cross
    scaled_out[far, near] = cross.T
    scaled_out[far, far] = lower
    first_out[near, near] = 0.5 * (three - upper)
    first_out[near, far] = 0.5 * (0.0 - cross)
    first_out[far, near] = 0.5 * (0.0 - cross.T)
    first_out[far, far] = 0.5 * (three - lower)
    inverse_out[:, near] = inv_upper_row
    inverse_out[:, far] = inv_lower_row
    factor_out[:, near] = 0.5 * jnp.sqrt(upper_row) / jnp.sqrt(spread)
    factor_out[:, far] = 0.5 * jnp.sqrt(lower_row) / jnp.sqrt(spread)


def rows_sum(v, outer, inner):
    rows, width = v.shape
    half_w = width // 2
    a_chunk = rows // inner
    a_half = a_chunk // outer
    b_half = rows // outer
    b_chunk = b_half // inner
    return pl.pallas_call(
        functools.partial(rows_sum_kernel, outer, inner),
        out_shape=(
            jax.ShapeDtypeStruct((2 * width, 2 * width), jnp.float32),
            jax.ShapeDtypeStruct((2 * width, 2 * width), jnp.float32),
            jax.ShapeDtypeStruct((1, 2 * width), jnp.float32),
            jax.ShapeDtypeStruct((1, 2 * width), jnp.float32),
        ),
        in_specs=[pl.BlockSpec(memory_space=pltpu.VMEM)],
        out_specs=[pl.BlockSpec(memory_space=pltpu.VMEM)] * 4,
        scratch_shapes=[
            pltpu.VMEM((inner - 1, a_chunk, half_w), jnp.float32),
            pltpu.VMEM((a_chunk, half_w), jnp.float32),
            pltpu.VMEM((2, a_half, half_w), jnp.float32),
            pltpu.VMEM((a_half, half_w), jnp.float32),
            pltpu.VMEM((inner, a_chunk, half_w), jnp.float32),
            pltpu.VMEM((b_half, half_w), jnp.float32),
            pltpu.VMEM((b_half, half_w), jnp.float32),
            pltpu.VMEM((inner - 1, b_chunk, half_w), jnp.float32),
            pltpu.VMEM((b_chunk, half_w), jnp.float32),
            pltpu.VMEM((inner, b_chunk, half_w), jnp.float32),
            pltpu.VMEM((outer, inner, b_chunk, half_w), jnp.float32),
            pltpu.VMEM((rows, width), jnp.float32),
            pltpu.SemaphoreType.DMA((16,)),
            pltpu.SemaphoreType.DMA((16,)),
        ],
        compiler_params=pltpu.CompilerParams(collective_id=0, has_side_effects=True),
    )(v)


def summed_gram(upper, lower, outer, inner):
    width = upper.shape[1]
    row = lax.broadcasted_iota(jnp.int32, (width, width), 0)
    col = lax.broadcasted_iota(jnp.int32, (width, width), 1)
    upper_gram = inner_gram(upper, upper)
    lower_gram = inner_gram(lower, lower)
    cross_gram = inner_gram(upper, lower)
    packed = jnp.where(col >= row, upper_gram, lower_gram)
    tail = jnp.zeros((64, width), jnp.float32).at[0].set(masked_diagonal(lower_gram))
    return rows_sum(jnp.concatenate([packed, cross_gram, tail]), outer, inner)


def from_behind(x, axis, by):
    count = lax.axis_size(axis)
    pairs = [(i, i + by) for i in range(count) if 0 <= i + by < count]
    return lax.ppermute(x, axis, pairs)


def inner_gram(left, right):
    return lax.dot_general(
        left, right, (((0,), (0,)), ((), ())), precision=fast, preferred_element_type=jnp.float32
    )


def masked_diagonal(block):
    width = block.shape[0]
    eye = lax.broadcasted_iota(jnp.int32, (width, width), 0) == lax.broadcasted_iota(jnp.int32, (width, width), 1)
    return jnp.sum(jnp.where(eye, block, 0.0), axis=0)


def normalize(gram, diagonal):
    width = gram.shape[0]
    diagonal = diagonal + epsilon
    inverse = 1.0 / jnp.sqrt(diagonal)
    normed = gram * inverse[:, None] * inverse[None, :]
    spread = 1.5 * jnp.sqrt(jnp.sum(normed * normed)) / jnp.sqrt(jnp.float32(width))
    scaled_gram = normed / spread
    identity = jnp.eye(width, dtype=jnp.float32)
    first_iter = 0.5 * (3.0 * identity - scaled_gram)
    factor = 0.5 * jnp.sqrt(diagonal) / jnp.sqrt(spread)
    return (scaled_gram, first_iter, inverse, factor, identity)


def per_device(matrix, plan, outer, inner):
    local_rows = matrix.shape[0]
    blocks = matrix.reshape(local_rows, -1, BLK)
    slots = jnp.take(blocks, plan, axis=1).reshape(local_rows, -1)
    current = lax.all_to_all(slots, "pair", split_axis=1, concat_axis=0, tiled=True)
    pair_index = lax.axis_index("pair")
    pair_count = lax.axis_size("pair")
    for turn_index in range(STEPS):
        upper = current[:, :BLK]
        lower = current[:, BLK:]
        scaled_gram, first_iter, inverse, factor = summed_gram(upper, lower, outer, inner)
        weighted = current * inverse
        applied = jnp.dot(weighted, first_iter, precision=fast, preferred_element_type=jnp.float32)
        chain = jnp.dot(applied, scaled_gram, precision=fast, preferred_element_type=jnp.float32)
        chain = jnp.dot(chain, first_iter, precision=fast, preferred_element_type=jnp.float32)
        chain = jnp.dot(chain, first_iter, precision=fast, preferred_element_type=jnp.float32)
        current = (3.0 * applied - chain) * factor
        upper = current[:, :BLK]
        lower = current[:, BLK:]
        outgoing = jnp.where(pair_index == 0, lower, upper)
        arrived_up = from_behind(outgoing, "pair", 1)
        arrived_down = from_behind(lower, "pair", -1)
        new_upper = jnp.where(pair_index == 0, upper, arrived_up)
        new_lower = jnp.where(pair_index == pair_count - 1, upper, arrived_down)
        current = jnp.concatenate([new_upper, new_lower], axis=1)
    return current


def solution(mesh):
    pairs, rows = mesh.shape["pair"], mesh.shape["rows"]
    inner = 4
    outer = rows // inner
    split = jax.sharding.Mesh(mesh.devices.reshape(pairs, outer, inner), ("pair", "ylo", "x"))
    placed = (P(("ylo", "x", "pair"), None), P())
    return jax.shard_map(
        functools.partial(per_device, outer=outer, inner=inner),
        mesh=split,
        in_specs=placed,
        out_specs=P(("ylo", "x"), "pair"),
        check_vma=False,
    )
```

```python
import functools

import jax
import jax.numpy as jnp
from jax import lax
from jax.experimental import pallas as pl
from jax.experimental.pallas import tpu as pltpu
from jax.sharding import PartitionSpec as P

MESH = pl.DeviceIdType.MESH

BLK = 512
STEPS = 2


epsilon = 1e-06
high = lax.Precision.HIGHEST
fast = lax.Precision.HIGH


def shifted(v, axis, count, by):
    return lax.ppermute(v, axis, [(i, (i + by) % count) for i in range(count)])


def scatter_sum(v, axis, count):
    me = lax.axis_index(axis)
    chunks = v.reshape(count, v.shape[0] // count, *v.shape[1:])
    total = lax.dynamic_index_in_dim(chunks, me, keepdims=False)
    for by in range(1, count):
        piece = lax.dynamic_index_in_dim(chunks, (me + by) % count, keepdims=False)
        total = total + shifted(piece, axis, count, by)
    return total


def gather_all(v, axis, count):
    me = lax.axis_index(axis)
    out = jnp.zeros((count,) + v.shape, v.dtype)
    out = lax.dynamic_update_index_in_dim(out, v, me, 0)
    for by in range(1, count):
        out = lax.dynamic_update_index_in_dim(out, shifted(v, axis, count, by), (me - by) % count, 0)
    return out.reshape(count * v.shape[0], *v.shape[1:])


def remote(src, dst, sends, recvs, slot, device):
    copy = pltpu.make_async_remote_copy(
        src_ref=src,
        dst_ref=dst,
        send_sem=sends.at[slot],
        recv_sem=recvs.at[slot],
        device_id=device,
        device_id_type=MESH,
    )
    copy.start()
    return copy


def rows_sum_kernel(
    outer,
    inner,
    payload,
    scaled_out,
    first_out,
    inverse_out,
    factor_out,
    a_in,
    a_acc,
    a_halves,
    a_own,
    a_all,
    b_in,
    b_acc,
    b_parts,
    b_own,
    b_row,
    b_all,
    out,
    sends,
    recvs,
):
    pair = lax.axis_index("pair")
    me_y = lax.axis_index("ylo")
    me_x = lax.axis_index("x")
    rows, width = payload.shape
    half_w = width // 2
    a_chunk = rows // inner
    a_half = a_chunk // outer
    b_half = rows // outer
    b_chunk = b_half // inner
    partner = (me_y + 1) % outer
    cols_a = pl.ds(0, half_w)
    cols_b = pl.ds(half_w, half_w)

    def x_peer(by):
        return (pair, me_y, (me_x + by) % inner)

    y_peer = (pair, partner, me_x)

    barrier = pltpu.get_barrier_semaphore()
    for by in range(1, inner):
        pl.semaphore_signal(barrier, inc=1, device_id=x_peer(by), device_id_type=MESH)
    pl.semaphore_signal(barrier, inc=1, device_id=y_peer, device_id_type=MESH)
    pl.semaphore_wait(barrier, inner)

    copies = []
    for by in range(1, inner):
        target = (me_x + by) % inner
        rows_k = pl.ds(pl.multiple_of(target * a_chunk, 8), a_chunk)
        copies.append(remote(payload.at[rows_k, cols_a], a_in.at[by - 1], sends, recvs, by - 1, x_peer(by)))
    rows_k = pl.ds(pl.multiple_of(partner * b_half, 8), b_half)
    copies.append(remote(payload.at[rows_k, cols_b], b_in, sends, recvs, 8, y_peer))
    for copy in copies:
        copy.wait()
    total = payload[pl.ds(pl.multiple_of(me_x * a_chunk, 8), a_chunk), cols_a]
    for by in range(1, inner):
        total = total + a_in[by - 1]
    a_acc[...] = total
    b_acc[...] = payload[pl.ds(pl.multiple_of(me_y * b_half, 8), b_half), cols_b] + b_in[...]

    copies = [
        remote(a_acc.at[pl.ds(pl.multiple_of(partner * a_half, 8), a_half)], a_halves.at[0], sends, recvs, 3, y_peer)
    ]
    for by in range(1, inner):
        target = (me_x + by) % inner
        rows_k = pl.ds(pl.multiple_of(target * b_chunk, 8), b_chunk)
        copies.append(remote(b_acc.at[rows_k], b_parts.at[by - 1], sends, recvs, 8 + by, x_peer(by)))
    for copy in copies:
        copy.wait()
    a_own[...] = a_acc[pl.ds(pl.multiple_of(me_y * a_half, 8), a_half), :] + a_halves[0]
    total = b_acc[pl.ds(pl.multiple_of(me_x * b_chunk, 8), b_chunk), :]
    for by in range(1, inner):
        total = total + b_parts[by - 1]
    b_own[...] = total

    copies = [remote(a_own, a_halves.at[1], sends, recvs, 4, y_peer)]
    for by in range(1, inner):
        copies.append(remote(b_own, b_row.at[me_x], sends, recvs, 11 + by, x_peer(by)))
    for copy in copies:
        copy.wait()
    a_all[me_x, pl.ds(pl.multiple_of(me_y * a_half, 8), a_half), :] = a_own[...]
    a_all[me_x, pl.ds(pl.multiple_of(partner * a_half, 8), a_half), :] = a_halves[1]
    b_row[me_x] = b_own[...]
    b_all[me_y] = b_row[...]

    copies = []
    for by in range(1, inner):
        copies.append(remote(a_all.at[me_x], a_all.at[me_x], sends, recvs, 4 + by, x_peer(by)))
    copies.append(remote(b_row, b_all.at[me_y], sends, recvs, 15, y_peer))
    for copy in copies:
        copy.wait()
    for k in range(inner):
        out[pl.ds(k * a_chunk, a_chunk), cols_a] = a_all[k]
    for j in range(outer):
        for k in range(inner):
            out[pl.ds(j * b_half + k * b_chunk, b_chunk), cols_b] = b_all[j, k]
    normalize_packed(out, scaled_out, first_out, inverse_out, factor_out)


def normalize_packed(packed, scaled_out, first_out, inverse_out, factor_out):
    width = packed.shape[1]
    row = lax.broadcasted_iota(jnp.int32, (width, width), 0)
    col = lax.broadcasted_iota(jnp.int32, (width, width), 1)
    eye = row == col
    top = packed[pl.ds(0, width), :]
    cross = packed[pl.ds(width, width), :]
    lower_diagonal = packed[pl.ds(2 * width, 1), :]
    strict_upper = jnp.where(col > row, top, 0.0)
    upper = jnp.where(col >= row, top, 0.0) + strict_upper.T
    strict_lower = jnp.where(col < row, top, 0.0)
    lower = strict_lower + strict_lower.T + jnp.where(eye, lower_diagonal, 0.0)
    upper_row = jnp.sum(jnp.where(eye, top, 0.0), axis=0, keepdims=True) + epsilon
    upper_col = jnp.sum(jnp.where(eye, top, 0.0), axis=1, keepdims=True) + epsilon
    lower_row = lower_diagonal + epsilon
    lower_col = jnp.sum(jnp.where(eye, lower, 0.0), axis=1, keepdims=True) + epsilon
    inv_upper_row, inv_upper_col = 1.0 / jnp.sqrt(upper_row), 1.0 / jnp.sqrt(upper_col)
    inv_lower_row, inv_lower_col = 1.0 / jnp.sqrt(lower_row), 1.0 / jnp.sqrt(lower_col)
    upper = upper * inv_upper_col * inv_upper_row
    lower = lower * inv_lower_col * inv_lower_row
    cross = cross * inv_upper_col * inv_lower_row

    def total(v):
        return jnp.sum(jnp.sum(v * v, axis=0, keepdims=True), axis=1, keepdims=True)

    squares = total(upper) + total(lower) + 2.0 * total(cross)
    spread = 1.5 * jnp.sqrt(squares) / jnp.sqrt(jnp.float32(2 * width))
    upper = upper / spread
    lower = lower / spread
    cross = cross / spread
    three = jnp.where(eye, 3.0, 0.0)
    near, far = pl.ds(0, width), pl.ds(width, width)
    scaled_out[near, near] = upper
    scaled_out[near, far] = cross
    scaled_out[far, near] = cross.T
    scaled_out[far, far] = lower
    first_out[near, near] = 0.5 * (three - upper)
    first_out[near, far] = 0.5 * (0.0 - cross)
    first_out[far, near] = 0.5 * (0.0 - cross.T)
    first_out[far, far] = 0.5 * (three - lower)
    inverse_out[:, near] = inv_upper_row
    inverse_out[:, far] = inv_lower_row
    factor_out[:, near] = 0.5 * jnp.sqrt(upper_row) / jnp.sqrt(spread)
    factor_out[:, far] = 0.5 * jnp.sqrt(lower_row) / jnp.sqrt(spread)


def rows_sum(v, outer, inner):
    rows, width = v.shape
    half_w = width // 2
    a_chunk = rows // inner
    a_half = a_chunk // outer
    b_half = rows // outer
    b_chunk = b_half // inner
    return pl.pallas_call(
        functools.partial(rows_sum_kernel, outer, inner),
        out_shape=(
            jax.ShapeDtypeStruct((2 * width, 2 * width), jnp.float32),
            jax.ShapeDtypeStruct((2 * width, 2 * width), jnp.float32),
            jax.ShapeDtypeStruct((1, 2 * width), jnp.float32),
            jax.ShapeDtypeStruct((1, 2 * width), jnp.float32),
        ),
        in_specs=[pl.BlockSpec(memory_space=pltpu.VMEM)],
        out_specs=[pl.BlockSpec(memory_space=pltpu.VMEM)] * 4,
        scratch_shapes=[
            pltpu.VMEM((inner - 1, a_chunk, half_w), jnp.float32),
            pltpu.VMEM((a_chunk, half_w), jnp.float32),
            pltpu.VMEM((2, a_half, half_w), jnp.float32),
            pltpu.VMEM((a_half, half_w), jnp.float32),
            pltpu.VMEM((inner, a_chunk, half_w), jnp.float32),
            pltpu.VMEM((b_half, half_w), jnp.float32),
            pltpu.VMEM((b_half, half_w), jnp.float32),
            pltpu.VMEM((inner - 1, b_chunk, half_w), jnp.float32),
            pltpu.VMEM((b_chunk, half_w), jnp.float32),
            pltpu.VMEM((inner, b_chunk, half_w), jnp.float32),
            pltpu.VMEM((outer, inner, b_chunk, half_w), jnp.float32),
            pltpu.VMEM((rows, width), jnp.float32),
            pltpu.SemaphoreType.DMA((16,)),
            pltpu.SemaphoreType.DMA((16,)),
        ],
        compiler_params=pltpu.CompilerParams(collective_id=0, has_side_effects=True),
    )(v)


def summed_gram(upper, lower, outer, inner):
    width = upper.shape[1]
    row = lax.broadcasted_iota(jnp.int32, (width, width), 0)
    col = lax.broadcasted_iota(jnp.int32, (width, width), 1)
    upper_gram = inner_gram(upper, upper)
    lower_gram = inner_gram(lower, lower)
    cross_gram = inner_gram(upper, lower)
    packed = jnp.where(col >= row, upper_gram, lower_gram)
    tail = jnp.zeros((64, width), jnp.float32).at[0].set(masked_diagonal(lower_gram))
    return rows_sum(jnp.concatenate([packed, cross_gram, tail]), outer, inner)


def from_behind(x, axis, by):
    count = lax.axis_size(axis)
    pairs = [(i, i + by) for i in range(count) if 0 <= i + by < count]
    return lax.ppermute(x, axis, pairs)


def inner_gram(left, right):
    return lax.dot_general(
        left, right, (((0,), (0,)), ((), ())), precision=fast, preferred_element_type=jnp.float32
    )


def masked_diagonal(block):
    width = block.shape[0]
    eye = lax.broadcasted_iota(jnp.int32, (width, width), 0) == lax.broadcasted_iota(jnp.int32, (width, width), 1)
    return jnp.sum(jnp.where(eye, block, 0.0), axis=0)


def normalize(gram, diagonal):
    width = gram.shape[0]
    diagonal = diagonal + epsilon
    inverse = 1.0 / jnp.sqrt(diagonal)
    normed = gram * inverse[:, None] * inverse[None, :]
    spread = 1.5 * jnp.sqrt(jnp.sum(normed * normed)) / jnp.sqrt(jnp.float32(width))
    scaled_gram = normed / spread
    identity = jnp.eye(width, dtype=jnp.float32)
    first_iter = 0.5 * (3.0 * identity - scaled_gram)
    factor = 0.5 * jnp.sqrt(diagonal) / jnp.sqrt(spread)
    return (scaled_gram, first_iter, inverse, factor, identity)


def per_device(matrix, plan, outer, inner):
    local_rows = matrix.shape[0]
    blocks = matrix.reshape(local_rows, -1, BLK)
    slots = jnp.take(blocks, plan, axis=1, mode="clip").reshape(local_rows, -1)
    current = lax.all_to_all(slots, "pair", split_axis=1, concat_axis=0, tiled=True)
    pair_index = lax.axis_index("pair")
    pair_count = lax.axis_size("pair")
    def turn(turn_index, current):
        upper = current[:, :BLK]
        lower = current[:, BLK:]
        scaled_gram, first_iter, inverse, factor = summed_gram(upper, lower, outer, inner)
        weighted = current * inverse
        applied = jnp.dot(weighted, first_iter, precision=fast, preferred_element_type=jnp.float32)
        chain = jnp.dot(applied, scaled_gram, precision=fast, preferred_element_type=jnp.float32)
        chain = jnp.dot(chain, first_iter, precision=fast, preferred_element_type=jnp.float32)
        chain = jnp.dot(chain, first_iter, precision=fast, preferred_element_type=jnp.float32)
        current = (3.0 * applied - chain) * factor
        upper = current[:, :BLK]
        lower = current[:, BLK:]
        outgoing = jnp.where(pair_index == 0, lower, upper)
        arrived_up = from_behind(outgoing, "pair", 1)
        arrived_down = from_behind(lower, "pair", -1)
        new_upper = jnp.where(pair_index == 0, upper, arrived_up)
        new_lower = jnp.where(pair_index == pair_count - 1, upper, arrived_down)
        current = jnp.concatenate([new_upper, new_lower], axis=1)
        return current

    current = lax.fori_loop(0, STEPS, turn, current)
    return current


def solution(mesh):
    pairs, rows = mesh.shape["pair"], mesh.shape["rows"]
    inner = 4
    outer = rows // inner
    split = jax.sharding.Mesh(mesh.devices.reshape(pairs, outer, inner), ("pair", "ylo", "x"))
    placed = (P(("ylo", "x", "pair"), None), P())
    return jax.shard_map(
        functools.partial(per_device, outer=outer, inner=inner),
        mesh=split,
        in_specs=placed,
        out_specs=P(("ylo", "x"), "pair"),
        check_vma=False,
    )
```

```python
import functools

import jax
import jax.numpy as jnp
from jax import lax
from jax.experimental import pallas as pl
from jax.experimental.pallas import tpu as pltpu
from jax.sharding import PartitionSpec as P

MESH = pl.DeviceIdType.MESH

BLK = 512
STEPS = 2


epsilon = 1e-06
high = lax.Precision.HIGHEST
fast = lax.Precision.HIGH


def shifted(v, axis, count, by):
    return lax.ppermute(v, axis, [(i, (i + by) % count) for i in range(count)])


def scatter_sum(v, axis, count):
    me = lax.axis_index(axis)
    chunks = v.reshape(count, v.shape[0] // count, *v.shape[1:])
    total = lax.dynamic_index_in_dim(chunks, me, keepdims=False)
    for by in range(1, count):
        piece = lax.dynamic_index_in_dim(chunks, (me + by) % count, keepdims=False)
        total = total + shifted(piece, axis, count, by)
    return total


def gather_all(v, axis, count):
    me = lax.axis_index(axis)
    out = jnp.zeros((count,) + v.shape, v.dtype)
    out = lax.dynamic_update_index_in_dim(out, v, me, 0)
    for by in range(1, count):
        out = lax.dynamic_update_index_in_dim(out, shifted(v, axis, count, by), (me - by) % count, 0)
    return out.reshape(count * v.shape[0], *v.shape[1:])


def remote(src, dst, sends, recvs, slot, device):
    copy = pltpu.make_async_remote_copy(
        src_ref=src,
        dst_ref=dst,
        send_sem=sends.at[slot],
        recv_sem=recvs.at[slot],
        device_id=device,
        device_id_type=MESH,
    )
    copy.start()
    return copy


def rows_sum_kernel(
    outer,
    inner,
    payload,
    scaled_out,
    first_out,
    inverse_out,
    factor_out,
    a_in,
    a_acc,
    a_halves,
    a_own,
    a_all,
    b_in,
    b_acc,
    b_parts,
    b_own,
    b_row,
    b_all,
    out,
    sends,
    recvs,
):
    pair = lax.axis_index("pair")
    me_y = lax.axis_index("ylo")
    me_x = lax.axis_index("x")
    rows, width = payload.shape
    half_w = width // 2
    a_chunk = rows // inner
    a_half = a_chunk // outer
    b_half = rows // outer
    b_chunk = b_half // inner
    partner = (me_y + 1) % outer
    cols_a = pl.ds(0, half_w)
    cols_b = pl.ds(half_w, half_w)

    def x_peer(by):
        return (pair, me_y, (me_x + by) % inner)

    y_peer = (pair, partner, me_x)

    barrier = pltpu.get_barrier_semaphore()
    for by in range(1, inner):
        pl.semaphore_signal(barrier, inc=1, device_id=x_peer(by), device_id_type=MESH)
    pl.semaphore_signal(barrier, inc=1, device_id=y_peer, device_id_type=MESH)
    pl.semaphore_wait(barrier, inner)

    copies = []
    for by in range(1, inner):
        target = (me_x + by) % inner
        rows_k = pl.ds(pl.multiple_of(target * a_chunk, 8), a_chunk)
        copies.append(remote(payload.at[rows_k, cols_a], a_in.at[by - 1], sends, recvs, by - 1, x_peer(by)))
    rows_k = pl.ds(pl.multiple_of(partner * b_half, 8), b_half)
    copies.append(remote(payload.at[rows_k, cols_b], b_in, sends, recvs, 8, y_peer))
    for copy in copies:
        copy.wait()
    total = payload[pl.ds(pl.multiple_of(me_x * a_chunk, 8), a_chunk), cols_a]
    for by in range(1, inner):
        total = total + a_in[by - 1]
    a_acc[...] = total
    b_acc[...] = payload[pl.ds(pl.multiple_of(me_y * b_half, 8), b_half), cols_b] + b_in[...]

    copies = [
        remote(a_acc.at[pl.ds(pl.multiple_of(partner * a_half, 8), a_half)], a_halves.at[0], sends, recvs, 3, y_peer)
    ]
    for by in range(1, inner):
        target = (me_x + by) % inner
        rows_k = pl.ds(pl.multiple_of(target * b_chunk, 8), b_chunk)
        copies.append(remote(b_acc.at[rows_k], b_parts.at[by - 1], sends, recvs, 8 + by, x_peer(by)))
    for copy in copies:
        copy.wait()
    a_own[...] = a_acc[pl.ds(pl.multiple_of(me_y * a_half, 8), a_half), :] + a_halves[0]
    total = b_acc[pl.ds(pl.multiple_of(me_x * b_chunk, 8), b_chunk), :]
    for by in range(1, inner):
        total = total + b_parts[by - 1]
    b_own[...] = total

    copies = [remote(a_own, a_halves.at[1], sends, recvs, 4, y_peer)]
    for by in range(1, inner):
        copies.append(remote(b_own, b_row.at[me_x], sends, recvs, 11 + by, x_peer(by)))
    for copy in copies:
        copy.wait()
    a_all[me_x, pl.ds(pl.multiple_of(me_y * a_half, 8), a_half), :] = a_own[...]
    a_all[me_x, pl.ds(pl.multiple_of(partner * a_half, 8), a_half), :] = a_halves[1]
    b_row[me_x] = b_own[...]
    b_all[me_y] = b_row[...]

    copies = []
    for by in range(1, inner):
        copies.append(remote(a_all.at[me_x], a_all.at[me_x], sends, recvs, 4 + by, x_peer(by)))
    copies.append(remote(b_row, b_all.at[me_y], sends, recvs, 15, y_peer))
    for copy in copies:
        copy.wait()
    for k in range(inner):
        out[pl.ds(k * a_chunk, a_chunk), cols_a] = a_all[k]
    for j in range(outer):
        for k in range(inner):
            out[pl.ds(j * b_half + k * b_chunk, b_chunk), cols_b] = b_all[j, k]
    normalize_packed(out, scaled_out, first_out, inverse_out, factor_out)


def normalize_packed(packed, scaled_out, first_out, inverse_out, factor_out):
    width = packed.shape[1]
    row = lax.broadcasted_iota(jnp.int32, (width, width), 0)
    col = lax.broadcasted_iota(jnp.int32, (width, width), 1)
    eye = row == col
    top = packed[pl.ds(0, width), :]
    cross = packed[pl.ds(width, width), :]
    lower_diagonal = packed[pl.ds(2 * width, 1), :]
    strict_upper = jnp.where(col > row, top, 0.0)
    upper = jnp.where(col >= row, top, 0.0) + strict_upper.T
    strict_lower = jnp.where(col < row, top, 0.0)
    lower = strict_lower + strict_lower.T + jnp.where(eye, lower_diagonal, 0.0)
    upper_row = jnp.sum(jnp.where(eye, top, 0.0), axis=0, keepdims=True) + epsilon
    upper_col = jnp.sum(jnp.where(eye, top, 0.0), axis=1, keepdims=True) + epsilon
    lower_row = lower_diagonal + epsilon
    lower_col = jnp.sum(jnp.where(eye, lower, 0.0), axis=1, keepdims=True) + epsilon
    inv_upper_row, inv_upper_col = 1.0 / jnp.sqrt(upper_row), 1.0 / jnp.sqrt(upper_col)
    inv_lower_row, inv_lower_col = 1.0 / jnp.sqrt(lower_row), 1.0 / jnp.sqrt(lower_col)
    upper = upper * inv_upper_col * inv_upper_row
    lower = lower * inv_lower_col * inv_lower_row
    cross = cross * inv_upper_col * inv_lower_row

    def total(v):
        return jnp.sum(jnp.sum(v * v, axis=0, keepdims=True), axis=1, keepdims=True)

    squares = total(upper) + total(lower) + 2.0 * total(cross)
    spread = 1.5 * jnp.sqrt(squares) / jnp.sqrt(jnp.float32(2 * width))
    upper = upper / spread
    lower = lower / spread
    cross = cross / spread
    three = jnp.where(eye, 3.0, 0.0)
    near, far = pl.ds(0, width), pl.ds(width, width)
    scaled_out[near, near] = upper
    scaled_out[near, far] = cross
    scaled_out[far, near] = cross.T
    scaled_out[far, far] = lower
    first_out[near, near] = 0.5 * (three - upper)
    first_out[near, far] = 0.5 * (0.0 - cross)
    first_out[far, near] = 0.5 * (0.0 - cross.T)
    first_out[far, far] = 0.5 * (three - lower)
    inverse_out[:, near] = inv_upper_row
    inverse_out[:, far] = inv_lower_row
    factor_out[:, near] = 0.5 * jnp.sqrt(upper_row) / jnp.sqrt(spread)
    factor_out[:, far] = 0.5 * jnp.sqrt(lower_row) / jnp.sqrt(spread)


def rows_sum(v, outer, inner):
    rows, width = v.shape
    half_w = width // 2
    a_chunk = rows // inner
    a_half = a_chunk // outer
    b_half = rows // outer
    b_chunk = b_half // inner
    return pl.pallas_call(
        functools.partial(rows_sum_kernel, outer, inner),
        out_shape=(
            jax.ShapeDtypeStruct((2 * width, 2 * width), jnp.float32),
            jax.ShapeDtypeStruct((2 * width, 2 * width), jnp.float32),
            jax.ShapeDtypeStruct((1, 2 * width), jnp.float32),
            jax.ShapeDtypeStruct((1, 2 * width), jnp.float32),
        ),
        in_specs=[pl.BlockSpec(memory_space=pltpu.VMEM)],
        out_specs=[pl.BlockSpec(memory_space=pltpu.VMEM)] * 4,
        scratch_shapes=[
            pltpu.VMEM((inner - 1, a_chunk, half_w), jnp.float32),
            pltpu.VMEM((a_chunk, half_w), jnp.float32),
            pltpu.VMEM((2, a_half, half_w), jnp.float32),
            pltpu.VMEM((a_half, half_w), jnp.float32),
            pltpu.VMEM((inner, a_chunk, half_w), jnp.float32),
            pltpu.VMEM((b_half, half_w), jnp.float32),
            pltpu.VMEM((b_half, half_w), jnp.float32),
            pltpu.VMEM((inner - 1, b_chunk, half_w), jnp.float32),
            pltpu.VMEM((b_chunk, half_w), jnp.float32),
            pltpu.VMEM((inner, b_chunk, half_w), jnp.float32),
            pltpu.VMEM((outer, inner, b_chunk, half_w), jnp.float32),
            pltpu.VMEM((rows, width), jnp.float32),
            pltpu.SemaphoreType.DMA((16,)),
            pltpu.SemaphoreType.DMA((16,)),
        ],
        compiler_params=pltpu.CompilerParams(collective_id=0, has_side_effects=True),
    )(v)


def summed_gram(upper, lower, outer, inner):
    width = upper.shape[1]
    row = lax.broadcasted_iota(jnp.int32, (width, width), 0)
    col = lax.broadcasted_iota(jnp.int32, (width, width), 1)
    upper_gram = inner_gram(upper, upper)
    lower_gram = inner_gram(lower, lower)
    cross_gram = inner_gram(upper, lower)
    packed = jnp.where(col >= row, upper_gram, lower_gram)
    tail = jnp.zeros((64, width), jnp.float32).at[0].set(masked_diagonal(lower_gram))
    return rows_sum(jnp.concatenate([packed, cross_gram, tail]), outer, inner)


def from_behind(x, axis, by):
    count = lax.axis_size(axis)
    pairs = [(i, i + by) for i in range(count) if 0 <= i + by < count]
    return lax.ppermute(x, axis, pairs)


def inner_gram(left, right):
    return lax.dot_general(
        left, right, (((0,), (0,)), ((), ())), precision=fast, preferred_element_type=jnp.float32
    )


def masked_diagonal(block):
    width = block.shape[0]
    eye = lax.broadcasted_iota(jnp.int32, (width, width), 0) == lax.broadcasted_iota(jnp.int32, (width, width), 1)
    return jnp.sum(jnp.where(eye, block, 0.0), axis=0)


def normalize(gram, diagonal):
    width = gram.shape[0]
    diagonal = diagonal + epsilon
    inverse = 1.0 / jnp.sqrt(diagonal)
    normed = gram * inverse[:, None] * inverse[None, :]
    spread = 1.5 * jnp.sqrt(jnp.sum(normed * normed)) / jnp.sqrt(jnp.float32(width))
    scaled_gram = normed / spread
    identity = jnp.eye(width, dtype=jnp.float32)
    first_iter = 0.5 * (3.0 * identity - scaled_gram)
    factor = 0.5 * jnp.sqrt(diagonal) / jnp.sqrt(spread)
    return (scaled_gram, first_iter, inverse, factor, identity)


def per_device(matrix, plan, outer, inner):
    local_rows = matrix.shape[0]
    blocks = jnp.transpose(matrix.reshape(local_rows, -1, BLK), (1, 0, 2))
    pair_count = lax.axis_size("pair")
    slots = jnp.take(blocks, plan, axis=0, mode="clip").reshape(pair_count, 2, local_rows, BLK)
    arrived = lax.all_to_all(slots, "pair", split_axis=0, concat_axis=0, tiled=True)
    current = jnp.concatenate(
        [arrived[:, 0].reshape(-1, BLK), arrived[:, 1].reshape(-1, BLK)], axis=1
    )
    pair_index = lax.axis_index("pair")
    pair_count = lax.axis_size("pair")
    def turn(turn_index, current):
        upper = current[:, :BLK]
        lower = current[:, BLK:]
        scaled_gram, first_iter, inverse, factor = summed_gram(upper, lower, outer, inner)
        weighted = current * inverse
        applied = jnp.dot(weighted, first_iter, precision=fast, preferred_element_type=jnp.float32)
        chain = jnp.dot(applied, scaled_gram, precision=fast, preferred_element_type=jnp.float32)
        chain = jnp.dot(chain, first_iter, precision=fast, preferred_element_type=jnp.float32)
        chain = jnp.dot(chain, first_iter, precision=fast, preferred_element_type=jnp.float32)
        current = (3.0 * applied - chain) * factor
        upper = current[:, :BLK]
        lower = current[:, BLK:]
        outgoing = jnp.where(pair_index == 0, lower, upper)
        arrived_up = from_behind(outgoing, "pair", 1)
        arrived_down = from_behind(lower, "pair", -1)
        new_upper = jnp.where(pair_index == 0, upper, arrived_up)
        new_lower = jnp.where(pair_index == pair_count - 1, upper, arrived_down)
        current = jnp.concatenate([new_upper, new_lower], axis=1)
        return current

    current = lax.fori_loop(0, STEPS, turn, current)
    return current


def solution(mesh):
    pairs, rows = mesh.shape["pair"], mesh.shape["rows"]
    inner = 4
    outer = rows // inner
    split = jax.sharding.Mesh(mesh.devices.reshape(pairs, outer, inner), ("pair", "ylo", "x"))
    placed = (P(("ylo", "x", "pair"), None), P())
    return jax.shard_map(
        functools.partial(per_device, outer=outer, inner=inner),
        mesh=split,
        in_specs=placed,
        out_specs=P(("ylo", "x"), "pair"),
        check_vma=False,
    )
```

```python
import functools

import jax
import jax.numpy as jnp
from jax import lax
from jax.experimental import pallas as pl
from jax.experimental.pallas import tpu as pltpu
from jax.sharding import PartitionSpec as P

MESH = pl.DeviceIdType.MESH

BLK = 512
STEPS = 2


epsilon = 1e-06
high = lax.Precision.HIGHEST
fast = lax.Precision.HIGH


def shifted(v, axis, count, by):
    return lax.ppermute(v, axis, [(i, (i + by) % count) for i in range(count)])


def scatter_sum(v, axis, count):
    me = lax.axis_index(axis)
    chunks = v.reshape(count, v.shape[0] // count, *v.shape[1:])
    total = lax.dynamic_index_in_dim(chunks, me, keepdims=False)
    for by in range(1, count):
        piece = lax.dynamic_index_in_dim(chunks, (me + by) % count, keepdims=False)
        total = total + shifted(piece, axis, count, by)
    return total


def gather_all(v, axis, count):
    me = lax.axis_index(axis)
    out = jnp.zeros((count,) + v.shape, v.dtype)
    out = lax.dynamic_update_index_in_dim(out, v, me, 0)
    for by in range(1, count):
        out = lax.dynamic_update_index_in_dim(out, shifted(v, axis, count, by), (me - by) % count, 0)
    return out.reshape(count * v.shape[0], *v.shape[1:])


def remote(src, dst, sends, recvs, slot, device):
    copy = pltpu.make_async_remote_copy(
        src_ref=src,
        dst_ref=dst,
        send_sem=sends.at[slot],
        recv_sem=recvs.at[slot],
        device_id=device,
        device_id_type=MESH,
    )
    copy.start()
    return copy


def rows_sum_kernel(
    outer,
    inner,
    payload,
    scaled_out,
    first_out,
    weighted_out,
    factor_out,
    a_in,
    a_acc,
    a_halves,
    a_own,
    a_all,
    b_in,
    b_acc,
    b_parts,
    b_own,
    b_row,
    b_all,
    out,
    sends,
    recvs,
):
    pair = lax.axis_index("pair")
    me_y = lax.axis_index("ylo")
    me_x = lax.axis_index("x")
    rows, width = payload.shape
    half_w = width // 2
    a_chunk = rows // inner
    a_half = a_chunk // outer
    b_half = rows // outer
    b_chunk = b_half // inner
    partner = (me_y + 1) % outer
    cols_a = pl.ds(0, half_w)
    cols_b = pl.ds(half_w, half_w)

    def x_peer(by):
        return (pair, me_y, (me_x + by) % inner)

    y_peer = (pair, partner, me_x)

    barrier = pltpu.get_barrier_semaphore()
    for by in range(1, inner):
        pl.semaphore_signal(barrier, inc=1, device_id=x_peer(by), device_id_type=MESH)
    pl.semaphore_signal(barrier, inc=1, device_id=y_peer, device_id_type=MESH)
    pl.semaphore_wait(barrier, inner)

    copies = []
    for by in range(1, inner):
        target = (me_x + by) % inner
        rows_k = pl.ds(pl.multiple_of(target * a_chunk, 8), a_chunk)
        copies.append(remote(payload.at[rows_k, cols_a], a_in.at[by - 1], sends, recvs, by - 1, x_peer(by)))
    rows_k = pl.ds(pl.multiple_of(partner * b_half, 8), b_half)
    copies.append(remote(payload.at[rows_k, cols_b], b_in, sends, recvs, 8, y_peer))
    for copy in copies:
        copy.wait()
    total = payload[pl.ds(pl.multiple_of(me_x * a_chunk, 8), a_chunk), cols_a]
    for by in range(1, inner):
        total = total + a_in[by - 1]
    a_acc[...] = total
    b_acc[...] = payload[pl.ds(pl.multiple_of(me_y * b_half, 8), b_half), cols_b] + b_in[...]

    copies = [
        remote(a_acc.at[pl.ds(pl.multiple_of(partner * a_half, 8), a_half)], a_halves.at[0], sends, recvs, 3, y_peer)
    ]
    for by in range(1, inner):
        target = (me_x + by) % inner
        rows_k = pl.ds(pl.multiple_of(target * b_chunk, 8), b_chunk)
        copies.append(remote(b_acc.at[rows_k], b_parts.at[by - 1], sends, recvs, 8 + by, x_peer(by)))
    for copy in copies:
        copy.wait()
    a_own[...] = a_acc[pl.ds(pl.multiple_of(me_y * a_half, 8), a_half), :] + a_halves[0]
    total = b_acc[pl.ds(pl.multiple_of(me_x * b_chunk, 8), b_chunk), :]
    for by in range(1, inner):
        total = total + b_parts[by - 1]
    b_own[...] = total

    copies = [remote(a_own, a_halves.at[1], sends, recvs, 4, y_peer)]
    for by in range(1, inner):
        copies.append(remote(b_own, b_row.at[me_x], sends, recvs, 11 + by, x_peer(by)))
    for copy in copies:
        copy.wait()
    a_all[me_x, pl.ds(pl.multiple_of(me_y * a_half, 8), a_half), :] = a_own[...]
    a_all[me_x, pl.ds(pl.multiple_of(partner * a_half, 8), a_half), :] = a_halves[1]
    b_row[me_x] = b_own[...]
    b_all[me_y] = b_row[...]

    copies = []
    for by in range(1, inner):
        copies.append(remote(a_all.at[me_x], a_all.at[me_x], sends, recvs, 4 + by, x_peer(by)))
    copies.append(remote(b_row, b_all.at[me_y], sends, recvs, 15, y_peer))
    for copy in copies:
        copy.wait()
    for k in range(inner):
        out[pl.ds(k * a_chunk, a_chunk), cols_a] = a_all[k]
    for j in range(outer):
        for k in range(inner):
            out[pl.ds(j * b_half + k * b_chunk, b_chunk), cols_b] = b_all[j, k]
    normalize_packed(out, scaled_out, first_out, weighted_out, factor_out)


def normalize_packed(packed, scaled_out, first_out, weighted_out, factor_out):
    width = packed.shape[1]
    row = lax.broadcasted_iota(jnp.int32, (width, width), 0)
    col = lax.broadcasted_iota(jnp.int32, (width, width), 1)
    eye = row == col
    top = packed[pl.ds(0, width), :]
    cross = packed[pl.ds(width, width), :]
    lower_diagonal = packed[pl.ds(2 * width, 1), :]
    strict_upper = jnp.where(col > row, top, 0.0)
    upper = jnp.where(col >= row, top, 0.0) + strict_upper.T
    strict_lower = jnp.where(col < row, top, 0.0)
    lower = strict_lower + strict_lower.T + jnp.where(eye, lower_diagonal, 0.0)
    upper_row = jnp.sum(jnp.where(eye, top, 0.0), axis=0, keepdims=True) + epsilon
    upper_col = jnp.sum(jnp.where(eye, top, 0.0), axis=1, keepdims=True) + epsilon
    lower_row = lower_diagonal + epsilon
    lower_col = jnp.sum(jnp.where(eye, lower, 0.0), axis=1, keepdims=True) + epsilon
    inv_upper_row, inv_upper_col = 1.0 / jnp.sqrt(upper_row), 1.0 / jnp.sqrt(upper_col)
    inv_lower_row, inv_lower_col = 1.0 / jnp.sqrt(lower_row), 1.0 / jnp.sqrt(lower_col)
    upper = upper * inv_upper_col * inv_upper_row
    lower = lower * inv_lower_col * inv_lower_row
    cross = cross * inv_upper_col * inv_lower_row

    def total(v):
        return jnp.sum(jnp.sum(v * v, axis=0, keepdims=True), axis=1, keepdims=True)

    squares = total(upper) + total(lower) + 2.0 * total(cross)
    spread = 1.5 * jnp.sqrt(squares) / jnp.sqrt(jnp.float32(2 * width))
    upper = upper / spread
    lower = lower / spread
    cross = cross / spread
    three = jnp.where(eye, 3.0, 0.0)
    near, far = pl.ds(0, width), pl.ds(width, width)
    scaled_out[near, near] = upper
    scaled_out[near, far] = cross
    scaled_out[far, near] = cross.T
    scaled_out[far, far] = lower
    first_out[near, near] = 0.5 * (three - upper)
    first_out[near, far] = 0.5 * (0.0 - cross)
    first_out[far, near] = 0.5 * (0.0 - cross.T)
    first_out[far, far] = 0.5 * (three - lower)
    weighted_out[near, :] = first_out[near, :] * inv_upper_col
    weighted_out[far, :] = first_out[far, :] * inv_lower_col
    factor_out[:, near] = 0.5 * jnp.sqrt(upper_row) / jnp.sqrt(spread)
    factor_out[:, far] = 0.5 * jnp.sqrt(lower_row) / jnp.sqrt(spread)


def rows_sum(v, outer, inner):
    rows, width = v.shape
    half_w = width // 2
    a_chunk = rows // inner
    a_half = a_chunk // outer
    b_half = rows // outer
    b_chunk = b_half // inner
    return pl.pallas_call(
        functools.partial(rows_sum_kernel, outer, inner),
        out_shape=(
            jax.ShapeDtypeStruct((2 * width, 2 * width), jnp.float32),
            jax.ShapeDtypeStruct((2 * width, 2 * width), jnp.float32),
            jax.ShapeDtypeStruct((2 * width, 2 * width), jnp.float32),
            jax.ShapeDtypeStruct((1, 2 * width), jnp.float32),
        ),
        in_specs=[pl.BlockSpec(memory_space=pltpu.VMEM)],
        out_specs=[pl.BlockSpec(memory_space=pltpu.VMEM)] * 4,
        scratch_shapes=[
            pltpu.VMEM((inner - 1, a_chunk, half_w), jnp.float32),
            pltpu.VMEM((a_chunk, half_w), jnp.float32),
            pltpu.VMEM((2, a_half, half_w), jnp.float32),
            pltpu.VMEM((a_half, half_w), jnp.float32),
            pltpu.VMEM((inner, a_chunk, half_w), jnp.float32),
            pltpu.VMEM((b_half, half_w), jnp.float32),
            pltpu.VMEM((b_half, half_w), jnp.float32),
            pltpu.VMEM((inner - 1, b_chunk, half_w), jnp.float32),
            pltpu.VMEM((b_chunk, half_w), jnp.float32),
            pltpu.VMEM((inner, b_chunk, half_w), jnp.float32),
            pltpu.VMEM((outer, inner, b_chunk, half_w), jnp.float32),
            pltpu.VMEM((rows, width), jnp.float32),
            pltpu.SemaphoreType.DMA((16,)),
            pltpu.SemaphoreType.DMA((16,)),
        ],
        compiler_params=pltpu.CompilerParams(collective_id=0, has_side_effects=True),
    )(v)


def summed_gram(upper, lower, outer, inner):
    width = upper.shape[1]
    row = lax.broadcasted_iota(jnp.int32, (width, width), 0)
    col = lax.broadcasted_iota(jnp.int32, (width, width), 1)
    upper_gram = inner_gram(upper, upper)
    lower_gram = inner_gram(lower, lower)
    cross_gram = inner_gram(upper, lower)
    packed = jnp.where(col >= row, upper_gram, lower_gram)
    tail = jnp.zeros((64, width), jnp.float32).at[0].set(masked_diagonal(lower_gram))
    return rows_sum(jnp.concatenate([packed, cross_gram, tail]), outer, inner)


def from_behind(x, axis, by):
    count = lax.axis_size(axis)
    pairs = [(i, i + by) for i in range(count) if 0 <= i + by < count]
    return lax.ppermute(x, axis, pairs)


def inner_gram(left, right):
    return lax.dot_general(
        left, right, (((0,), (0,)), ((), ())), precision=fast, preferred_element_type=jnp.float32
    )


def masked_diagonal(block):
    width = block.shape[0]
    eye = lax.broadcasted_iota(jnp.int32, (width, width), 0) == lax.broadcasted_iota(jnp.int32, (width, width), 1)
    return jnp.sum(jnp.where(eye, block, 0.0), axis=0)


def normalize(gram, diagonal):
    width = gram.shape[0]
    diagonal = diagonal + epsilon
    inverse = 1.0 / jnp.sqrt(diagonal)
    normed = gram * inverse[:, None] * inverse[None, :]
    spread = 1.5 * jnp.sqrt(jnp.sum(normed * normed)) / jnp.sqrt(jnp.float32(width))
    scaled_gram = normed / spread
    identity = jnp.eye(width, dtype=jnp.float32)
    first_iter = 0.5 * (3.0 * identity - scaled_gram)
    factor = 0.5 * jnp.sqrt(diagonal) / jnp.sqrt(spread)
    return (scaled_gram, first_iter, inverse, factor, identity)


def per_device(matrix, plan, outer, inner):
    local_rows = matrix.shape[0]
    blocks = jnp.transpose(matrix.reshape(local_rows, -1, BLK), (1, 0, 2))
    pair_count = lax.axis_size("pair")
    slots = jnp.take(blocks, plan, axis=0, mode="clip").reshape(pair_count, 2, local_rows, BLK)
    arrived = lax.all_to_all(slots, "pair", split_axis=0, concat_axis=0, tiled=True)
    current = jnp.concatenate(
        [arrived[:, 0].reshape(-1, BLK), arrived[:, 1].reshape(-1, BLK)], axis=1
    )
    pair_index = lax.axis_index("pair")
    pair_count = lax.axis_size("pair")
    def turn(turn_index, current):
        upper = current[:, :BLK]
        lower = current[:, BLK:]
        scaled_gram, first_iter, weighted_first, factor = summed_gram(upper, lower, outer, inner)
        applied = jnp.dot(current, weighted_first, precision=fast, preferred_element_type=jnp.float32)
        chain = jnp.dot(applied, scaled_gram, precision=fast, preferred_element_type=jnp.float32)
        chain = jnp.dot(chain, first_iter, precision=fast, preferred_element_type=jnp.float32)
        chain = jnp.dot(chain, first_iter, precision=fast, preferred_element_type=jnp.float32)
        current = (3.0 * applied - chain) * factor
        upper = current[:, :BLK]
        lower = current[:, BLK:]
        outgoing = jnp.where(pair_index == 0, lower, upper)
        arrived_up = from_behind(outgoing, "pair", 1)
        arrived_down = from_behind(lower, "pair", -1)
        new_upper = jnp.where(pair_index == 0, upper, arrived_up)
        new_lower = jnp.where(pair_index == pair_count - 1, upper, arrived_down)
        current = jnp.concatenate([new_upper, new_lower], axis=1)
        return current

    current = lax.fori_loop(0, STEPS, turn, current)
    return current


def solution(mesh):
    pairs, rows = mesh.shape["pair"], mesh.shape["rows"]
    inner = 4
    outer = rows // inner
    split = jax.sharding.Mesh(mesh.devices.reshape(pairs, outer, inner), ("pair", "ylo", "x"))
    placed = (P(("ylo", "x", "pair"), None), P())
    return jax.shard_map(
        functools.partial(per_device, outer=outer, inner=inner),
        mesh=split,
        in_specs=placed,
        out_specs=P(("ylo", "x"), "pair"),
        check_vma=False,
    )
```

```python
import functools

import jax
import jax.numpy as jnp
from jax import lax
from jax.experimental import pallas as pl
from jax.experimental.pallas import tpu as pltpu
from jax.sharding import PartitionSpec as P

MESH = pl.DeviceIdType.MESH

BLK = 512
STEPS = 2


epsilon = 1e-06
high = lax.Precision.HIGHEST
fast = lax.Precision.HIGH


def shifted(v, axis, count, by):
    return lax.ppermute(v, axis, [(i, (i + by) % count) for i in range(count)])


def scatter_sum(v, axis, count):
    me = lax.axis_index(axis)
    chunks = v.reshape(count, v.shape[0] // count, *v.shape[1:])
    total = lax.dynamic_index_in_dim(chunks, me, keepdims=False)
    for by in range(1, count):
        piece = lax.dynamic_index_in_dim(chunks, (me + by) % count, keepdims=False)
        total = total + shifted(piece, axis, count, by)
    return total


def gather_all(v, axis, count):
    me = lax.axis_index(axis)
    out = jnp.zeros((count,) + v.shape, v.dtype)
    out = lax.dynamic_update_index_in_dim(out, v, me, 0)
    for by in range(1, count):
        out = lax.dynamic_update_index_in_dim(out, shifted(v, axis, count, by), (me - by) % count, 0)
    return out.reshape(count * v.shape[0], *v.shape[1:])


def remote(src, dst, sends, recvs, slot, device):
    copy = pltpu.make_async_remote_copy(
        src_ref=src,
        dst_ref=dst,
        send_sem=sends.at[slot],
        recv_sem=recvs.at[slot],
        device_id=device,
        device_id_type=MESH,
    )
    copy.start()
    return copy


def rows_sum_kernel(
    outer,
    inner,
    payload,
    scaled_out,
    first_out,
    inverse_out,
    factor_out,
    a_in,
    a_acc,
    a_halves,
    a_own,
    a_all,
    b_in,
    b_acc,
    b_parts,
    b_own,
    b_row,
    b_all,
    out,
    sends,
    recvs,
):
    pair = lax.axis_index("pair")
    me_y = lax.axis_index("ylo")
    me_x = lax.axis_index("x")
    rows, width = payload.shape
    half_w = width // 2
    a_chunk = rows // inner
    a_half = a_chunk // outer
    b_half = rows // outer
    b_chunk = b_half // inner
    partner = (me_y + 1) % outer
    cols_a = pl.ds(0, half_w)
    cols_b = pl.ds(half_w, half_w)

    def x_peer(by):
        return (pair, me_y, (me_x + by) % inner)

    y_peer = (pair, partner, me_x)

    barrier = pltpu.get_barrier_semaphore()
    for by in range(1, inner):
        pl.semaphore_signal(barrier, inc=1, device_id=x_peer(by), device_id_type=MESH)
    pl.semaphore_signal(barrier, inc=1, device_id=y_peer, device_id_type=MESH)
    pl.semaphore_wait(barrier, inner)

    copies = []
    for by in range(1, inner):
        target = (me_x + by) % inner
        rows_k = pl.ds(pl.multiple_of(target * a_chunk, 8), a_chunk)
        copies.append(remote(payload.at[rows_k, cols_a], a_in.at[by - 1], sends, recvs, by - 1, x_peer(by)))
    rows_k = pl.ds(pl.multiple_of(partner * b_half, 8), b_half)
    copies.append(remote(payload.at[rows_k, cols_b], b_in, sends, recvs, 8, y_peer))
    for copy in copies:
        copy.wait()
    total = payload[pl.ds(pl.multiple_of(me_x * a_chunk, 8), a_chunk), cols_a]
    for by in range(1, inner):
        total = total + a_in[by - 1]
    a_acc[...] = total
    b_acc[...] = payload[pl.ds(pl.multiple_of(me_y * b_half, 8), b_half), cols_b] + b_in[...]

    copies = [
        remote(a_acc.at[pl.ds(pl.multiple_of(partner * a_half, 8), a_half)], a_halves.at[0], sends, recvs, 3, y_peer)
    ]
    for by in range(1, inner):
        target = (me_x + by) % inner
        rows_k = pl.ds(pl.multiple_of(target * b_chunk, 8), b_chunk)
        copies.append(remote(b_acc.at[rows_k], b_parts.at[by - 1], sends, recvs, 8 + by, x_peer(by)))
    for copy in copies:
        copy.wait()
    a_own[...] = a_acc[pl.ds(pl.multiple_of(me_y * a_half, 8), a_half), :] + a_halves[0]
    total = b_acc[pl.ds(pl.multiple_of(me_x * b_chunk, 8), b_chunk), :]
    for by in range(1, inner):
        total = total + b_parts[by - 1]
    b_own[...] = total

    copies = [remote(a_own, a_halves.at[1], sends, recvs, 4, y_peer)]
    for by in range(1, inner):
        copies.append(remote(b_own, b_row.at[me_x], sends, recvs, 11 + by, x_peer(by)))
    for copy in copies:
        copy.wait()
    a_all[me_x, pl.ds(pl.multiple_of(me_y * a_half, 8), a_half), :] = a_own[...]
    a_all[me_x, pl.ds(pl.multiple_of(partner * a_half, 8), a_half), :] = a_halves[1]
    b_row[me_x] = b_own[...]
    b_all[me_y] = b_row[...]

    copies = []
    for by in range(1, inner):
        copies.append(remote(a_all.at[me_x], a_all.at[me_x], sends, recvs, 4 + by, x_peer(by)))
    copies.append(remote(b_row, b_all.at[me_y], sends, recvs, 15, y_peer))
    for copy in copies:
        copy.wait()
    for k in range(inner):
        out[pl.ds(k * a_chunk, a_chunk), cols_a] = a_all[k]
    for j in range(outer):
        for k in range(inner):
            out[pl.ds(j * b_half + k * b_chunk, b_chunk), cols_b] = b_all[j, k]
    normalize_packed(out, scaled_out, first_out, inverse_out, factor_out)


def normalize_packed(packed, scaled_out, first_out, inverse_out, factor_out):
    width = packed.shape[1]
    row = lax.broadcasted_iota(jnp.int32, (width, width), 0)
    col = lax.broadcasted_iota(jnp.int32, (width, width), 1)
    eye = row == col
    top = packed[pl.ds(0, width), :]
    cross = packed[pl.ds(width, width), :]
    lower_diagonal = packed[pl.ds(2 * width, 1), :]
    strict_upper = jnp.where(col > row, top, 0.0)
    upper = jnp.where(col >= row, top, 0.0) + strict_upper.T
    strict_lower = jnp.where(col < row, top, 0.0)
    lower = strict_lower + strict_lower.T + jnp.where(eye, lower_diagonal, 0.0)
    upper_row = jnp.sum(jnp.where(eye, top, 0.0), axis=0, keepdims=True) + epsilon
    upper_col = jnp.sum(jnp.where(eye, top, 0.0), axis=1, keepdims=True) + epsilon
    lower_row = lower_diagonal + epsilon
    lower_col = jnp.sum(jnp.where(eye, lower, 0.0), axis=1, keepdims=True) + epsilon
    inv_upper_row, inv_upper_col = 1.0 / jnp.sqrt(upper_row), 1.0 / jnp.sqrt(upper_col)
    inv_lower_row, inv_lower_col = 1.0 / jnp.sqrt(lower_row), 1.0 / jnp.sqrt(lower_col)
    upper = upper * inv_upper_col * inv_upper_row
    lower = lower * inv_lower_col * inv_lower_row
    cross = cross * inv_upper_col * inv_lower_row

    def total(v):
        return jnp.sum(jnp.sum(v * v, axis=0, keepdims=True), axis=1, keepdims=True)

    squares = total(upper) + total(lower) + 2.0 * total(cross)
    spread = 1.5 * jnp.sqrt(squares) / jnp.sqrt(jnp.float32(2 * width))
    upper = upper / spread
    lower = lower / spread
    cross = cross / spread
    three = jnp.where(eye, 3.0, 0.0)
    near, far = pl.ds(0, width), pl.ds(width, width)
    scaled_out[near, near] = upper
    scaled_out[near, far] = cross
    scaled_out[far, near] = cross.T
    scaled_out[far, far] = lower
    first_out[near, near] = 0.5 * (three - upper)
    first_out[near, far] = 0.5 * (0.0 - cross)
    first_out[far, near] = 0.5 * (0.0 - cross.T)
    first_out[far, far] = 0.5 * (three - lower)
    inverse_out[:, near] = inv_upper_row
    inverse_out[:, far] = inv_lower_row
    factor_out[:, near] = 0.5 * jnp.sqrt(upper_row) / jnp.sqrt(spread)
    factor_out[:, far] = 0.5 * jnp.sqrt(lower_row) / jnp.sqrt(spread)


def rows_sum(v, outer, inner):
    rows, width = v.shape
    half_w = width // 2
    a_chunk = rows // inner
    a_half = a_chunk // outer
    b_half = rows // outer
    b_chunk = b_half // inner
    return pl.pallas_call(
        functools.partial(rows_sum_kernel, outer, inner),
        out_shape=(
            jax.ShapeDtypeStruct((2 * width, 2 * width), jnp.float32),
            jax.ShapeDtypeStruct((2 * width, 2 * width), jnp.float32),
            jax.ShapeDtypeStruct((1, 2 * width), jnp.float32),
            jax.ShapeDtypeStruct((1, 2 * width), jnp.float32),
        ),
        in_specs=[pl.BlockSpec(memory_space=pltpu.VMEM)],
        out_specs=[pl.BlockSpec(memory_space=pltpu.VMEM)] * 4,
        scratch_shapes=[
            pltpu.VMEM((inner - 1, a_chunk, half_w), jnp.float32),
            pltpu.VMEM((a_chunk, half_w), jnp.float32),
            pltpu.VMEM((2, a_half, half_w), jnp.float32),
            pltpu.VMEM((a_half, half_w), jnp.float32),
            pltpu.VMEM((inner, a_chunk, half_w), jnp.float32),
            pltpu.VMEM((b_half, half_w), jnp.float32),
            pltpu.VMEM((b_half, half_w), jnp.float32),
            pltpu.VMEM((inner - 1, b_chunk, half_w), jnp.float32),
            pltpu.VMEM((b_chunk, half_w), jnp.float32),
            pltpu.VMEM((inner, b_chunk, half_w), jnp.float32),
            pltpu.VMEM((outer, inner, b_chunk, half_w), jnp.float32),
            pltpu.VMEM((rows, width), jnp.float32),
            pltpu.SemaphoreType.DMA((16,)),
            pltpu.SemaphoreType.DMA((16,)),
        ],
        compiler_params=pltpu.CompilerParams(collective_id=0, has_side_effects=True),
    )(v)


def rotate_kernel(count, current, out, landed, sends, recvs):
    me = lax.axis_index("pair")
    me_y = lax.axis_index("ylo")
    me_x = lax.axis_index("x")
    half = current.shape[1] // 2
    upper_cols, lower_cols = pl.ds(0, half), pl.ds(half, half)
    following = ((me + 1) % count, me_y, me_x)
    preceding = ((me + count - 1) % count, me_y, me_x)
    barrier = pltpu.get_barrier_semaphore()

    @pl.when(me < count - 1)
    def _():
        pl.semaphore_signal(barrier, inc=1, device_id=following, device_id_type=MESH)

    @pl.when(me > 0)
    def _():
        pl.semaphore_signal(barrier, inc=1, device_id=preceding, device_id_type=MESH)

    @pl.when(jnp.logical_and(me > 0, me < count - 1))
    def _():
        pl.semaphore_wait(barrier, 2)

    @pl.when(jnp.logical_or(me == 0, me == count - 1))
    def _():
        pl.semaphore_wait(barrier, 1)

    start = pl.multiple_of(jnp.where(me == 0, half, 0), 128)
    upward = pltpu.make_async_remote_copy(
        src_ref=current.at[:, pl.ds(start, half)],
        dst_ref=landed.at[:, upper_cols],
        send_sem=sends.at[0],
        recv_sem=recvs.at[0],
        device_id=following,
        device_id_type=MESH,
    )
    downward = pltpu.make_async_remote_copy(
        src_ref=current.at[:, lower_cols],
        dst_ref=landed.at[:, lower_cols],
        send_sem=sends.at[1],
        recv_sem=recvs.at[1],
        device_id=preceding,
        device_id_type=MESH,
    )

    @pl.when(me < count - 1)
    def _():
        upward.start()

    @pl.when(me > 0)
    def _():
        downward.start()

    @pl.when(me == 0)
    def _():
        landed[:, upper_cols] = current[:, upper_cols]

    @pl.when(me == count - 1)
    def _():
        landed[:, lower_cols] = current[:, upper_cols]

    @pl.when(me < count - 1)
    def _():
        upward.wait_send()
        downward.wait_recv()

    @pl.when(me > 0)
    def _():
        downward.wait_send()
        upward.wait_recv()

    out[...] = landed[...]


def rotate(current, count):
    return pl.pallas_call(
        functools.partial(rotate_kernel, count),
        out_shape=jax.ShapeDtypeStruct(current.shape, current.dtype),
        in_specs=[pl.BlockSpec(memory_space=pltpu.VMEM)],
        out_specs=pl.BlockSpec(memory_space=pltpu.VMEM),
        scratch_shapes=[
            pltpu.VMEM(current.shape, jnp.float32),
            pltpu.SemaphoreType.DMA((2,)),
            pltpu.SemaphoreType.DMA((2,)),
        ],
        compiler_params=pltpu.CompilerParams(collective_id=2, has_side_effects=True),
    )(current)


def summed_gram(upper, lower, outer, inner):
    width = upper.shape[1]
    row = lax.broadcasted_iota(jnp.int32, (width, width), 0)
    col = lax.broadcasted_iota(jnp.int32, (width, width), 1)
    upper_gram = inner_gram(upper, upper)
    lower_gram = inner_gram(lower, lower)
    cross_gram = inner_gram(upper, lower)
    packed = jnp.where(col >= row, upper_gram, lower_gram)
    tail = jnp.zeros((64, width), jnp.float32).at[0].set(masked_diagonal(lower_gram))
    return rows_sum(jnp.concatenate([packed, cross_gram, tail]), outer, inner)


def from_behind(x, axis, by):
    count = lax.axis_size(axis)
    pairs = [(i, i + by) for i in range(count) if 0 <= i + by < count]
    return lax.ppermute(x, axis, pairs)


def inner_gram(left, right):
    return lax.dot_general(
        left, right, (((0,), (0,)), ((), ())), precision=fast, preferred_element_type=jnp.float32
    )


def masked_diagonal(block):
    width = block.shape[0]
    eye = lax.broadcasted_iota(jnp.int32, (width, width), 0) == lax.broadcasted_iota(jnp.int32, (width, width), 1)
    return jnp.sum(jnp.where(eye, block, 0.0), axis=0)


def normalize(gram, diagonal):
    width = gram.shape[0]
    diagonal = diagonal + epsilon
    inverse = 1.0 / jnp.sqrt(diagonal)
    normed = gram * inverse[:, None] * inverse[None, :]
    spread = 1.5 * jnp.sqrt(jnp.sum(normed * normed)) / jnp.sqrt(jnp.float32(width))
    scaled_gram = normed / spread
    identity = jnp.eye(width, dtype=jnp.float32)
    first_iter = 0.5 * (3.0 * identity - scaled_gram)
    factor = 0.5 * jnp.sqrt(diagonal) / jnp.sqrt(spread)
    return (scaled_gram, first_iter, inverse, factor, identity)


def per_device(matrix, plan, outer, inner):
    local_rows = matrix.shape[0]
    blocks = jnp.transpose(matrix.reshape(local_rows, -1, BLK), (1, 0, 2))
    pair_count = lax.axis_size("pair")
    slots = jnp.take(blocks, plan, axis=0, mode="clip").reshape(pair_count, 2, local_rows, BLK)
    arrived = lax.all_to_all(slots, "pair", split_axis=0, concat_axis=0, tiled=True)
    current = jnp.concatenate(
        [arrived[:, 0].reshape(-1, BLK), arrived[:, 1].reshape(-1, BLK)], axis=1
    )
    pair_index = lax.axis_index("pair")
    pair_count = lax.axis_size("pair")
    def turn(turn_index, current):
        upper = current[:, :BLK]
        lower = current[:, BLK:]
        scaled_gram, first_iter, inverse, factor = summed_gram(upper, lower, outer, inner)
        weighted = current * inverse
        applied = jnp.dot(weighted, first_iter, precision=fast, preferred_element_type=jnp.float32)
        chain = jnp.dot(applied, scaled_gram, precision=fast, preferred_element_type=jnp.float32)
        chain = jnp.dot(chain, first_iter, precision=fast, preferred_element_type=jnp.float32)
        chain = jnp.dot(chain, first_iter, precision=fast, preferred_element_type=jnp.float32)
        current = (3.0 * applied - chain) * factor
        return rotate(current, pair_count)

    current = lax.fori_loop(0, STEPS, turn, current)
    return current


def solution(mesh):
    pairs, rows = mesh.shape["pair"], mesh.shape["rows"]
    inner = 4
    outer = rows // inner
    split = jax.sharding.Mesh(mesh.devices.reshape(pairs, outer, inner), ("pair", "ylo", "x"))
    placed = (P(("ylo", "x", "pair"), None), P())
    return jax.shard_map(
        functools.partial(per_device, outer=outer, inner=inner),
        mesh=split,
        in_specs=placed,
        out_specs=P(("ylo", "x"), "pair"),
        check_vma=False,
    )
```

```python
import functools

import jax
import jax.numpy as jnp
from jax import lax
from jax.experimental import pallas as pl
from jax.experimental.pallas import tpu as pltpu
from jax.sharding import PartitionSpec as P

MESH = pl.DeviceIdType.MESH

BLK = 512
STEPS = 2


epsilon = 1e-06
high = lax.Precision.HIGHEST
fast = lax.Precision.HIGH


def shifted(v, axis, count, by):
    return lax.ppermute(v, axis, [(i, (i + by) % count) for i in range(count)])


def scatter_sum(v, axis, count):
    me = lax.axis_index(axis)
    chunks = v.reshape(count, v.shape[0] // count, *v.shape[1:])
    total = lax.dynamic_index_in_dim(chunks, me, keepdims=False)
    for by in range(1, count):
        piece = lax.dynamic_index_in_dim(chunks, (me + by) % count, keepdims=False)
        total = total + shifted(piece, axis, count, by)
    return total


def gather_all(v, axis, count):
    me = lax.axis_index(axis)
    out = jnp.zeros((count,) + v.shape, v.dtype)
    out = lax.dynamic_update_index_in_dim(out, v, me, 0)
    for by in range(1, count):
        out = lax.dynamic_update_index_in_dim(out, shifted(v, axis, count, by), (me - by) % count, 0)
    return out.reshape(count * v.shape[0], *v.shape[1:])


def remote(src, dst, sends, recvs, slot, device):
    copy = pltpu.make_async_remote_copy(
        src_ref=src,
        dst_ref=dst,
        send_sem=sends.at[slot],
        recv_sem=recvs.at[slot],
        device_id=device,
        device_id_type=MESH,
    )
    copy.start()
    return copy


def rows_sum_kernel(
    outer,
    inner,
    payload,
    scaled_out,
    first_out,
    inverse_out,
    factor_out,
    a_in,
    a_acc,
    a_halves,
    a_own,
    a_all,
    b_in,
    b_acc,
    b_parts,
    b_own,
    b_row,
    b_all,
    out,
    sends,
    recvs,
):
    pair = lax.axis_index("pair")
    me_y = lax.axis_index("ylo")
    me_x = lax.axis_index("x")
    rows, width = payload.shape
    half_w = width // 2
    a_chunk = rows // inner
    a_half = a_chunk // outer
    b_half = rows // outer
    b_chunk = b_half // inner
    partner = (me_y + 1) % outer
    cols_a = pl.ds(0, half_w)
    cols_b = pl.ds(half_w, half_w)

    def x_peer(by):
        return (pair, me_y, (me_x + by) % inner)

    y_peer = (pair, partner, me_x)

    barrier = pltpu.get_barrier_semaphore()
    for by in range(1, inner):
        pl.semaphore_signal(barrier, inc=1, device_id=x_peer(by), device_id_type=MESH)
    pl.semaphore_signal(barrier, inc=1, device_id=y_peer, device_id_type=MESH)
    pl.semaphore_wait(barrier, inner)

    copies = []
    for by in range(1, inner):
        target = (me_x + by) % inner
        rows_k = pl.ds(pl.multiple_of(target * a_chunk, 8), a_chunk)
        copies.append(remote(payload.at[rows_k, cols_a], a_in.at[by - 1], sends, recvs, by - 1, x_peer(by)))
    rows_k = pl.ds(pl.multiple_of(partner * b_half, 8), b_half)
    copies.append(remote(payload.at[rows_k, cols_b], b_in, sends, recvs, 8, y_peer))
    for copy in copies:
        copy.wait()
    total = payload[pl.ds(pl.multiple_of(me_x * a_chunk, 8), a_chunk), cols_a]
    for by in range(1, inner):
        total = total + a_in[by - 1]
    a_acc[...] = total
    b_acc[...] = payload[pl.ds(pl.multiple_of(me_y * b_half, 8), b_half), cols_b] + b_in[...]

    copies = [
        remote(a_acc.at[pl.ds(pl.multiple_of(partner * a_half, 8), a_half)], a_halves.at[0], sends, recvs, 3, y_peer)
    ]
    for by in range(1, inner):
        target = (me_x + by) % inner
        rows_k = pl.ds(pl.multiple_of(target * b_chunk, 8), b_chunk)
        copies.append(remote(b_acc.at[rows_k], b_parts.at[by - 1], sends, recvs, 8 + by, x_peer(by)))
    for copy in copies:
        copy.wait()
    a_own[...] = a_acc[pl.ds(pl.multiple_of(me_y * a_half, 8), a_half), :] + a_halves[0]
    total = b_acc[pl.ds(pl.multiple_of(me_x * b_chunk, 8), b_chunk), :]
    for by in range(1, inner):
        total = total + b_parts[by - 1]
    b_own[...] = total

    copies = [remote(a_own, a_halves.at[1], sends, recvs, 4, y_peer)]
    for by in range(1, inner):
        copies.append(remote(b_own, b_row.at[me_x], sends, recvs, 11 + by, x_peer(by)))
    for copy in copies:
        copy.wait()
    a_all[me_x, pl.ds(pl.multiple_of(me_y * a_half, 8), a_half), :] = a_own[...]
    a_all[me_x, pl.ds(pl.multiple_of(partner * a_half, 8), a_half), :] = a_halves[1]
    b_row[me_x] = b_own[...]
    b_all[me_y] = b_row[...]

    copies = []
    for by in range(1, inner):
        copies.append(remote(a_all.at[me_x], a_all.at[me_x], sends, recvs, 4 + by, x_peer(by)))
    copies.append(remote(b_row, b_all.at[me_y], sends, recvs, 15, y_peer))
    for copy in copies:
        copy.wait()
    for k in range(inner):
        out[pl.ds(k * a_chunk, a_chunk), cols_a] = a_all[k]
    for j in range(outer):
        for k in range(inner):
            out[pl.ds(j * b_half + k * b_chunk, b_chunk), cols_b] = b_all[j, k]
    normalize_packed(out, scaled_out, first_out, inverse_out, factor_out)


def normalize_packed(packed, scaled_out, first_out, inverse_out, factor_out):
    width = packed.shape[1]
    row = lax.broadcasted_iota(jnp.int32, (width, width), 0)
    col = lax.broadcasted_iota(jnp.int32, (width, width), 1)
    eye = row == col
    top = packed[pl.ds(0, width), :]
    cross = packed[pl.ds(width, width), :]
    lower_diagonal = packed[pl.ds(2 * width, 1), :]
    strict_upper = jnp.where(col > row, top, 0.0)
    upper = jnp.where(col >= row, top, 0.0) + strict_upper.T
    strict_lower = jnp.where(col < row, top, 0.0)
    lower = strict_lower + strict_lower.T + jnp.where(eye, lower_diagonal, 0.0)
    upper_row = jnp.sum(jnp.where(eye, top, 0.0), axis=0, keepdims=True) + epsilon
    upper_col = jnp.sum(jnp.where(eye, top, 0.0), axis=1, keepdims=True) + epsilon
    lower_row = lower_diagonal + epsilon
    lower_col = jnp.sum(jnp.where(eye, lower, 0.0), axis=1, keepdims=True) + epsilon
    inv_upper_row, inv_upper_col = 1.0 / jnp.sqrt(upper_row), 1.0 / jnp.sqrt(upper_col)
    inv_lower_row, inv_lower_col = 1.0 / jnp.sqrt(lower_row), 1.0 / jnp.sqrt(lower_col)
    upper = upper * inv_upper_col * inv_upper_row
    lower = lower * inv_lower_col * inv_lower_row
    cross = cross * inv_upper_col * inv_lower_row

    def total(v):
        return jnp.sum(jnp.sum(v * v, axis=0, keepdims=True), axis=1, keepdims=True)

    squares = total(upper) + total(lower) + 2.0 * total(cross)
    spread = 1.5 * jnp.sqrt(squares) / jnp.sqrt(jnp.float32(2 * width))
    upper = upper / spread
    lower = lower / spread
    cross = cross / spread
    three = jnp.where(eye, 3.0, 0.0)
    near, far = pl.ds(0, width), pl.ds(width, width)
    scaled_out[near, near] = upper
    scaled_out[near, far] = cross
    scaled_out[far, near] = cross.T
    scaled_out[far, far] = lower
    first_out[near, near] = 0.5 * (three - upper)
    first_out[near, far] = 0.5 * (0.0 - cross)
    first_out[far, near] = 0.5 * (0.0 - cross.T)
    first_out[far, far] = 0.5 * (three - lower)
    inverse_out[:, near] = inv_upper_row
    inverse_out[:, far] = inv_lower_row
    factor_out[:, near] = 0.5 * jnp.sqrt(upper_row) / jnp.sqrt(spread)
    factor_out[:, far] = 0.5 * jnp.sqrt(lower_row) / jnp.sqrt(spread)


def rows_sum(v, outer, inner):
    rows, width = v.shape
    half_w = width // 2
    a_chunk = rows // inner
    a_half = a_chunk // outer
    b_half = rows // outer
    b_chunk = b_half // inner
    return pl.pallas_call(
        functools.partial(rows_sum_kernel, outer, inner),
        out_shape=(
            jax.ShapeDtypeStruct((2 * width, 2 * width), jnp.float32),
            jax.ShapeDtypeStruct((2 * width, 2 * width), jnp.float32),
            jax.ShapeDtypeStruct((1, 2 * width), jnp.float32),
            jax.ShapeDtypeStruct((1, 2 * width), jnp.float32),
        ),
        in_specs=[pl.BlockSpec(memory_space=pltpu.VMEM)],
        out_specs=[pl.BlockSpec(memory_space=pltpu.VMEM)] * 4,
        scratch_shapes=[
            pltpu.VMEM((inner - 1, a_chunk, half_w), jnp.float32),
            pltpu.VMEM((a_chunk, half_w), jnp.float32),
            pltpu.VMEM((2, a_half, half_w), jnp.float32),
            pltpu.VMEM((a_half, half_w), jnp.float32),
            pltpu.VMEM((inner, a_chunk, half_w), jnp.float32),
            pltpu.VMEM((b_half, half_w), jnp.float32),
            pltpu.VMEM((b_half, half_w), jnp.float32),
            pltpu.VMEM((inner - 1, b_chunk, half_w), jnp.float32),
            pltpu.VMEM((b_chunk, half_w), jnp.float32),
            pltpu.VMEM((inner, b_chunk, half_w), jnp.float32),
            pltpu.VMEM((outer, inner, b_chunk, half_w), jnp.float32),
            pltpu.VMEM((rows, width), jnp.float32),
            pltpu.SemaphoreType.DMA((16,)),
            pltpu.SemaphoreType.DMA((16,)),
        ],
        compiler_params=pltpu.CompilerParams(collective_id=0, has_side_effects=True),
    )(v)


def rotate_kernel(count, current, out, landed, sends, recvs):
    me = lax.axis_index("pair")
    me_y = lax.axis_index("ylo")
    me_x = lax.axis_index("x")
    half = current.shape[1] // 2
    upper_cols, lower_cols = pl.ds(0, half), pl.ds(half, half)
    following = ((me + 1) % count, me_y, me_x)
    preceding = ((me + count - 1) % count, me_y, me_x)
    barrier = pltpu.get_barrier_semaphore()

    @pl.when(me < count - 1)
    def _():
        pl.semaphore_signal(barrier, inc=1, device_id=following, device_id_type=MESH)

    @pl.when(me > 0)
    def _():
        pl.semaphore_signal(barrier, inc=1, device_id=preceding, device_id_type=MESH)

    @pl.when(jnp.logical_and(me > 0, me < count - 1))
    def _():
        pl.semaphore_wait(barrier, 2)

    @pl.when(jnp.logical_or(me == 0, me == count - 1))
    def _():
        pl.semaphore_wait(barrier, 1)

    start = pl.multiple_of(jnp.where(me == 0, half, 0), 128)
    pieces = 4
    rows = current.shape[0] // pieces
    upward, downward = [], []
    for k in range(pieces):
        band = pl.ds(k * rows, rows)
        upward.append(
            pltpu.make_async_remote_copy(
                src_ref=current.at[band, pl.ds(start, half)],
                dst_ref=landed.at[band, upper_cols],
                send_sem=sends.at[k],
                recv_sem=recvs.at[k],
                device_id=following,
                device_id_type=MESH,
            )
        )
        downward.append(
            pltpu.make_async_remote_copy(
                src_ref=current.at[band, lower_cols],
                dst_ref=landed.at[band, lower_cols],
                send_sem=sends.at[pieces + k],
                recv_sem=recvs.at[pieces + k],
                device_id=preceding,
                device_id_type=MESH,
            )
        )

    @pl.when(me < count - 1)
    def _():
        for copy in upward:
            copy.start()

    @pl.when(me > 0)
    def _():
        for copy in downward:
            copy.start()

    @pl.when(me == 0)
    def _():
        landed[:, upper_cols] = current[:, upper_cols]

    @pl.when(me == count - 1)
    def _():
        landed[:, lower_cols] = current[:, upper_cols]

    @pl.when(me < count - 1)
    def _():
        for copy in upward:
            copy.wait_send()
        for copy in downward:
            copy.wait_recv()

    @pl.when(me > 0)
    def _():
        for copy in downward:
            copy.wait_send()
        for copy in upward:
            copy.wait_recv()

    out[...] = landed[...]


def rotate(current, count):
    return pl.pallas_call(
        functools.partial(rotate_kernel, count),
        out_shape=jax.ShapeDtypeStruct(current.shape, current.dtype),
        in_specs=[pl.BlockSpec(memory_space=pltpu.VMEM)],
        out_specs=pl.BlockSpec(memory_space=pltpu.VMEM),
        scratch_shapes=[
            pltpu.VMEM(current.shape, jnp.float32),
            pltpu.SemaphoreType.DMA((8,)),
            pltpu.SemaphoreType.DMA((8,)),
        ],
        compiler_params=pltpu.CompilerParams(collective_id=2, has_side_effects=True),
    )(current)


def summed_gram(upper, lower, outer, inner):
    width = upper.shape[1]
    row = lax.broadcasted_iota(jnp.int32, (width, width), 0)
    col = lax.broadcasted_iota(jnp.int32, (width, width), 1)
    upper_gram = inner_gram(upper, upper)
    lower_gram = inner_gram(lower, lower)
    cross_gram = inner_gram(upper, lower)
    packed = jnp.where(col >= row, upper_gram, lower_gram)
    tail = jnp.zeros((64, width), jnp.float32).at[0].set(masked_diagonal(lower_gram))
    return rows_sum(jnp.concatenate([packed, cross_gram, tail]), outer, inner)


def from_behind(x, axis, by):
    count = lax.axis_size(axis)
    pairs = [(i, i + by) for i in range(count) if 0 <= i + by < count]
    return lax.ppermute(x, axis, pairs)


def inner_gram(left, right):
    return lax.dot_general(
        left, right, (((0,), (0,)), ((), ())), precision=fast, preferred_element_type=jnp.float32
    )


def masked_diagonal(block):
    width = block.shape[0]
    eye = lax.broadcasted_iota(jnp.int32, (width, width), 0) == lax.broadcasted_iota(jnp.int32, (width, width), 1)
    return jnp.sum(jnp.where(eye, block, 0.0), axis=0)


def normalize(gram, diagonal):
    width = gram.shape[0]
    diagonal = diagonal + epsilon
    inverse = 1.0 / jnp.sqrt(diagonal)
    normed = gram * inverse[:, None] * inverse[None, :]
    spread = 1.5 * jnp.sqrt(jnp.sum(normed * normed)) / jnp.sqrt(jnp.float32(width))
    scaled_gram = normed / spread
    identity = jnp.eye(width, dtype=jnp.float32)
    first_iter = 0.5 * (3.0 * identity - scaled_gram)
    factor = 0.5 * jnp.sqrt(diagonal) / jnp.sqrt(spread)
    return (scaled_gram, first_iter, inverse, factor, identity)


def per_device(matrix, plan, outer, inner):
    local_rows = matrix.shape[0]
    blocks = jnp.transpose(matrix.reshape(local_rows, -1, BLK), (1, 0, 2))
    pair_count = lax.axis_size("pair")
    slots = jnp.take(blocks, plan, axis=0, mode="clip").reshape(pair_count, 2, local_rows, BLK)
    arrived = lax.all_to_all(slots, "pair", split_axis=0, concat_axis=0, tiled=True)
    current = jnp.concatenate(
        [arrived[:, 0].reshape(-1, BLK), arrived[:, 1].reshape(-1, BLK)], axis=1
    )
    pair_index = lax.axis_index("pair")
    pair_count = lax.axis_size("pair")
    def turn(turn_index, current):
        upper = current[:, :BLK]
        lower = current[:, BLK:]
        scaled_gram, first_iter, inverse, factor = summed_gram(upper, lower, outer, inner)
        weighted = current * inverse
        applied = jnp.dot(weighted, first_iter, precision=fast, preferred_element_type=jnp.float32)
        chain = jnp.dot(applied, scaled_gram, precision=fast, preferred_element_type=jnp.float32)
        chain = jnp.dot(chain, first_iter, precision=fast, preferred_element_type=jnp.float32)
        chain = jnp.dot(chain, first_iter, precision=fast, preferred_element_type=jnp.float32)
        current = (3.0 * applied - chain) * factor
        return rotate(current, pair_count)

    current = lax.fori_loop(0, STEPS, turn, current)
    return current


def solution(mesh):
    pairs, rows = mesh.shape["pair"], mesh.shape["rows"]
    inner = 4
    outer = rows // inner
    split = jax.sharding.Mesh(mesh.devices.reshape(pairs, outer, inner), ("pair", "ylo", "x"))
    placed = (P(("ylo", "x", "pair"), None), P())
    return jax.shard_map(
        functools.partial(per_device, outer=outer, inner=inner),
        mesh=split,
        in_specs=placed,
        out_specs=P(("ylo", "x"), "pair"),
        check_vma=False,
    )
```

```python
import functools

import jax
import jax.numpy as jnp
from jax import lax
from jax.experimental import pallas as pl
from jax.experimental.pallas import tpu as pltpu
from jax.sharding import PartitionSpec as P

MESH = pl.DeviceIdType.MESH

BLK = 512
STEPS = 2


epsilon = 1e-06
high = lax.Precision.HIGHEST
fast = lax.Precision.HIGH


def shifted(v, axis, count, by):
    return lax.ppermute(v, axis, [(i, (i + by) % count) for i in range(count)])


def scatter_sum(v, axis, count):
    me = lax.axis_index(axis)
    chunks = v.reshape(count, v.shape[0] // count, *v.shape[1:])
    total = lax.dynamic_index_in_dim(chunks, me, keepdims=False)
    for by in range(1, count):
        piece = lax.dynamic_index_in_dim(chunks, (me + by) % count, keepdims=False)
        total = total + shifted(piece, axis, count, by)
    return total


def gather_all(v, axis, count):
    me = lax.axis_index(axis)
    out = jnp.zeros((count,) + v.shape, v.dtype)
    out = lax.dynamic_update_index_in_dim(out, v, me, 0)
    for by in range(1, count):
        out = lax.dynamic_update_index_in_dim(out, shifted(v, axis, count, by), (me - by) % count, 0)
    return out.reshape(count * v.shape[0], *v.shape[1:])


def remote(src, dst, sends, recvs, slot, device):
    copy = pltpu.make_async_remote_copy(
        src_ref=src,
        dst_ref=dst,
        send_sem=sends.at[slot],
        recv_sem=recvs.at[slot],
        device_id=device,
        device_id_type=MESH,
    )
    copy.start()
    return copy


def rows_sum_kernel(
    outer,
    inner,
    payload,
    first_out,
    inverse_out,
    factor_out,
    a_in,
    a_acc,
    a_halves,
    a_own,
    a_all,
    b_in,
    b_acc,
    b_parts,
    b_own,
    b_row,
    b_all,
    out,
    sends,
    recvs,
):
    pair = lax.axis_index("pair")
    me_y = lax.axis_index("ylo")
    me_x = lax.axis_index("x")
    rows, width = payload.shape
    half_w = width // 2
    a_chunk = rows // inner
    a_half = a_chunk // outer
    b_half = rows // outer
    b_chunk = b_half // inner
    partner = (me_y + 1) % outer
    cols_a = pl.ds(0, half_w)
    cols_b = pl.ds(half_w, half_w)

    def x_peer(by):
        return (pair, me_y, (me_x + by) % inner)

    y_peer = (pair, partner, me_x)

    barrier = pltpu.get_barrier_semaphore()
    for by in range(1, inner):
        pl.semaphore_signal(barrier, inc=1, device_id=x_peer(by), device_id_type=MESH)
    pl.semaphore_signal(barrier, inc=1, device_id=y_peer, device_id_type=MESH)
    pl.semaphore_wait(barrier, inner)

    copies = []
    for by in range(1, inner):
        target = (me_x + by) % inner
        rows_k = pl.ds(pl.multiple_of(target * a_chunk, 8), a_chunk)
        copies.append(remote(payload.at[rows_k, cols_a], a_in.at[by - 1], sends, recvs, by - 1, x_peer(by)))
    rows_k = pl.ds(pl.multiple_of(partner * b_half, 8), b_half)
    copies.append(remote(payload.at[rows_k, cols_b], b_in, sends, recvs, 8, y_peer))
    for copy in copies:
        copy.wait()
    total = payload[pl.ds(pl.multiple_of(me_x * a_chunk, 8), a_chunk), cols_a]
    for by in range(1, inner):
        total = total + a_in[by - 1]
    a_acc[...] = total
    b_acc[...] = payload[pl.ds(pl.multiple_of(me_y * b_half, 8), b_half), cols_b] + b_in[...]

    copies = [
        remote(a_acc.at[pl.ds(pl.multiple_of(partner * a_half, 8), a_half)], a_halves.at[0], sends, recvs, 3, y_peer)
    ]
    for by in range(1, inner):
        target = (me_x + by) % inner
        rows_k = pl.ds(pl.multiple_of(target * b_chunk, 8), b_chunk)
        copies.append(remote(b_acc.at[rows_k], b_parts.at[by - 1], sends, recvs, 8 + by, x_peer(by)))
    for copy in copies:
        copy.wait()
    a_own[...] = a_acc[pl.ds(pl.multiple_of(me_y * a_half, 8), a_half), :] + a_halves[0]
    total = b_acc[pl.ds(pl.multiple_of(me_x * b_chunk, 8), b_chunk), :]
    for by in range(1, inner):
        total = total + b_parts[by - 1]
    b_own[...] = total

    copies = [remote(a_own, a_halves.at[1], sends, recvs, 4, y_peer)]
    for by in range(1, inner):
        copies.append(remote(b_own, b_row.at[me_x], sends, recvs, 11 + by, x_peer(by)))
    for copy in copies:
        copy.wait()
    a_all[me_x, pl.ds(pl.multiple_of(me_y * a_half, 8), a_half), :] = a_own[...]
    a_all[me_x, pl.ds(pl.multiple_of(partner * a_half, 8), a_half), :] = a_halves[1]
    b_row[me_x] = b_own[...]
    b_all[me_y] = b_row[...]

    copies = []
    for by in range(1, inner):
        copies.append(remote(a_all.at[me_x], a_all.at[me_x], sends, recvs, 4 + by, x_peer(by)))
    copies.append(remote(b_row, b_all.at[me_y], sends, recvs, 15, y_peer))
    for copy in copies:
        copy.wait()
    for k in range(inner):
        out[pl.ds(k * a_chunk, a_chunk), cols_a] = a_all[k]
    for j in range(outer):
        for k in range(inner):
            out[pl.ds(j * b_half + k * b_chunk, b_chunk), cols_b] = b_all[j, k]
    normalize_packed(out, first_out, inverse_out, factor_out)


def normalize_packed(packed, first_out, inverse_out, factor_out):
    width = packed.shape[1]
    row = lax.broadcasted_iota(jnp.int32, (width, width), 0)
    col = lax.broadcasted_iota(jnp.int32, (width, width), 1)
    eye = row == col
    top = packed[pl.ds(0, width), :]
    cross = packed[pl.ds(width, width), :]
    lower_diagonal = packed[pl.ds(2 * width, 1), :]
    strict_upper = jnp.where(col > row, top, 0.0)
    upper = jnp.where(col >= row, top, 0.0) + strict_upper.T
    strict_lower = jnp.where(col < row, top, 0.0)
    lower = strict_lower + strict_lower.T + jnp.where(eye, lower_diagonal, 0.0)
    upper_row = jnp.sum(jnp.where(eye, top, 0.0), axis=0, keepdims=True) + epsilon
    upper_col = jnp.sum(jnp.where(eye, top, 0.0), axis=1, keepdims=True) + epsilon
    lower_row = lower_diagonal + epsilon
    lower_col = jnp.sum(jnp.where(eye, lower, 0.0), axis=1, keepdims=True) + epsilon
    inv_upper_row, inv_upper_col = 1.0 / jnp.sqrt(upper_row), 1.0 / jnp.sqrt(upper_col)
    inv_lower_row, inv_lower_col = 1.0 / jnp.sqrt(lower_row), 1.0 / jnp.sqrt(lower_col)
    upper = upper * inv_upper_col * inv_upper_row
    lower = lower * inv_lower_col * inv_lower_row
    cross = cross * inv_upper_col * inv_lower_row

    def total(v):
        return jnp.sum(jnp.sum(v * v, axis=0, keepdims=True), axis=1, keepdims=True)

    squares = total(upper) + total(lower) + 2.0 * total(cross)
    spread = 1.5 * jnp.sqrt(squares) / jnp.sqrt(jnp.float32(2 * width))
    upper = upper / spread
    lower = lower / spread
    cross = cross / spread
    three = jnp.where(eye, 3.0, 0.0)
    near, far = pl.ds(0, width), pl.ds(width, width)
    first_out[near, near] = 0.5 * (three - upper)
    first_out[near, far] = 0.5 * (0.0 - cross)
    first_out[far, near] = 0.5 * (0.0 - cross.T)
    first_out[far, far] = 0.5 * (three - lower)
    inverse_out[:, near] = inv_upper_row
    inverse_out[:, far] = inv_lower_row
    factor_out[:, near] = 0.5 * jnp.sqrt(upper_row) / jnp.sqrt(spread)
    factor_out[:, far] = 0.5 * jnp.sqrt(lower_row) / jnp.sqrt(spread)


def rows_sum(v, outer, inner):
    rows, width = v.shape
    half_w = width // 2
    a_chunk = rows // inner
    a_half = a_chunk // outer
    b_half = rows // outer
    b_chunk = b_half // inner
    return pl.pallas_call(
        functools.partial(rows_sum_kernel, outer, inner),
        out_shape=(
            jax.ShapeDtypeStruct((2 * width, 2 * width), jnp.float32),
            jax.ShapeDtypeStruct((1, 2 * width), jnp.float32),
            jax.ShapeDtypeStruct((1, 2 * width), jnp.float32),
        ),
        in_specs=[pl.BlockSpec(memory_space=pltpu.VMEM)],
        out_specs=[pl.BlockSpec(memory_space=pltpu.VMEM)] * 3,
        scratch_shapes=[
            pltpu.VMEM((inner - 1, a_chunk, half_w), jnp.float32),
            pltpu.VMEM((a_chunk, half_w), jnp.float32),
            pltpu.VMEM((2, a_half, half_w), jnp.float32),
            pltpu.VMEM((a_half, half_w), jnp.float32),
            pltpu.VMEM((inner, a_chunk, half_w), jnp.float32),
            pltpu.VMEM((b_half, half_w), jnp.float32),
            pltpu.VMEM((b_half, half_w), jnp.float32),
            pltpu.VMEM((inner - 1, b_chunk, half_w), jnp.float32),
            pltpu.VMEM((b_chunk, half_w), jnp.float32),
            pltpu.VMEM((inner, b_chunk, half_w), jnp.float32),
            pltpu.VMEM((outer, inner, b_chunk, half_w), jnp.float32),
            pltpu.VMEM((rows, width), jnp.float32),
            pltpu.SemaphoreType.DMA((16,)),
            pltpu.SemaphoreType.DMA((16,)),
        ],
        compiler_params=pltpu.CompilerParams(collective_id=0, has_side_effects=True),
    )(v)


def rotate_kernel(count, current, out, landed, sends, recvs):
    me = lax.axis_index("pair")
    me_y = lax.axis_index("ylo")
    me_x = lax.axis_index("x")
    half = current.shape[1] // 2
    upper_cols, lower_cols = pl.ds(0, half), pl.ds(half, half)
    following = ((me + 1) % count, me_y, me_x)
    preceding = ((me + count - 1) % count, me_y, me_x)
    barrier = pltpu.get_barrier_semaphore()

    @pl.when(me < count - 1)
    def _():
        pl.semaphore_signal(barrier, inc=1, device_id=following, device_id_type=MESH)

    @pl.when(me > 0)
    def _():
        pl.semaphore_signal(barrier, inc=1, device_id=preceding, device_id_type=MESH)

    @pl.when(jnp.logical_and(me > 0, me < count - 1))
    def _():
        pl.semaphore_wait(barrier, 2)

    @pl.when(jnp.logical_or(me == 0, me == count - 1))
    def _():
        pl.semaphore_wait(barrier, 1)

    start = pl.multiple_of(jnp.where(me == 0, half, 0), 128)
    upward = pltpu.make_async_remote_copy(
        src_ref=current.at[:, pl.ds(start, half)],
        dst_ref=landed.at[:, upper_cols],
        send_sem=sends.at[0],
        recv_sem=recvs.at[0],
        device_id=following,
        device_id_type=MESH,
    )
    downward = pltpu.make_async_remote_copy(
        src_ref=current.at[:, lower_cols],
        dst_ref=landed.at[:, lower_cols],
        send_sem=sends.at[1],
        recv_sem=recvs.at[1],
        device_id=preceding,
        device_id_type=MESH,
    )

    @pl.when(me < count - 1)
    def _():
        upward.start()

    @pl.when(me > 0)
    def _():
        downward.start()

    @pl.when(me == 0)
    def _():
        landed[:, upper_cols] = current[:, upper_cols]

    @pl.when(me == count - 1)
    def _():
        landed[:, lower_cols] = current[:, upper_cols]

    @pl.when(me < count - 1)
    def _():
        upward.wait_send()
        downward.wait_recv()

    @pl.when(me > 0)
    def _():
        downward.wait_send()
        upward.wait_recv()

    out[...] = landed[...]


def rotate(current, count):
    return pl.pallas_call(
        functools.partial(rotate_kernel, count),
        out_shape=jax.ShapeDtypeStruct(current.shape, current.dtype),
        in_specs=[pl.BlockSpec(memory_space=pltpu.VMEM)],
        out_specs=pl.BlockSpec(memory_space=pltpu.VMEM),
        scratch_shapes=[
            pltpu.VMEM(current.shape, jnp.float32),
            pltpu.SemaphoreType.DMA((2,)),
            pltpu.SemaphoreType.DMA((2,)),
        ],
        compiler_params=pltpu.CompilerParams(collective_id=2, has_side_effects=True),
    )(current)


def summed_gram(upper, lower, outer, inner):
    width = upper.shape[1]
    row = lax.broadcasted_iota(jnp.int32, (width, width), 0)
    col = lax.broadcasted_iota(jnp.int32, (width, width), 1)
    upper_gram = inner_gram(upper, upper)
    lower_gram = inner_gram(lower, lower)
    cross_gram = inner_gram(upper, lower)
    packed = jnp.where(col >= row, upper_gram, lower_gram)
    tail = jnp.zeros((64, width), jnp.float32).at[0].set(masked_diagonal(lower_gram))
    return rows_sum(jnp.concatenate([packed, cross_gram, tail]), outer, inner)


def from_behind(x, axis, by):
    count = lax.axis_size(axis)
    pairs = [(i, i + by) for i in range(count) if 0 <= i + by < count]
    return lax.ppermute(x, axis, pairs)


def inner_gram(left, right):
    return lax.dot_general(
        left, right, (((0,), (0,)), ((), ())), precision=fast, preferred_element_type=jnp.float32
    )


def masked_diagonal(block):
    width = block.shape[0]
    eye = lax.broadcasted_iota(jnp.int32, (width, width), 0) == lax.broadcasted_iota(jnp.int32, (width, width), 1)
    return jnp.sum(jnp.where(eye, block, 0.0), axis=0)


def normalize(gram, diagonal):
    width = gram.shape[0]
    diagonal = diagonal + epsilon
    inverse = 1.0 / jnp.sqrt(diagonal)
    normed = gram * inverse[:, None] * inverse[None, :]
    spread = 1.5 * jnp.sqrt(jnp.sum(normed * normed)) / jnp.sqrt(jnp.float32(width))
    scaled_gram = normed / spread
    identity = jnp.eye(width, dtype=jnp.float32)
    first_iter = 0.5 * (3.0 * identity - scaled_gram)
    factor = 0.5 * jnp.sqrt(diagonal) / jnp.sqrt(spread)
    return (scaled_gram, first_iter, inverse, factor, identity)


def per_device(matrix, plan, outer, inner):
    local_rows = matrix.shape[0]
    blocks = jnp.transpose(matrix.reshape(local_rows, -1, BLK), (1, 0, 2))
    pair_count = lax.axis_size("pair")
    slots = jnp.take(blocks, plan, axis=0, mode="clip").reshape(pair_count, 2, local_rows, BLK)
    arrived = lax.all_to_all(slots, "pair", split_axis=0, concat_axis=0, tiled=True)
    current = jnp.concatenate(
        [arrived[:, 0].reshape(-1, BLK), arrived[:, 1].reshape(-1, BLK)], axis=1
    )
    pair_index = lax.axis_index("pair")
    pair_count = lax.axis_size("pair")
    def turn(turn_index, current):
        upper = current[:, :BLK]
        lower = current[:, BLK:]
        first_iter, inverse, factor = summed_gram(upper, lower, outer, inner)
        weighted = current * inverse
        applied = jnp.dot(weighted, first_iter, precision=fast, preferred_element_type=jnp.float32)
        chain = 3.0 * applied - 2.0 * jnp.dot(
            applied, first_iter, precision=fast, preferred_element_type=jnp.float32
        )
        chain = jnp.dot(chain, first_iter, precision=fast, preferred_element_type=jnp.float32)
        chain = jnp.dot(chain, first_iter, precision=fast, preferred_element_type=jnp.float32)
        current = (3.0 * applied - chain) * factor
        return rotate(current, pair_count)

    current = lax.fori_loop(0, STEPS, turn, current)
    return current


def solution(mesh):
    pairs, rows = mesh.shape["pair"], mesh.shape["rows"]
    inner = 4
    outer = rows // inner
    split = jax.sharding.Mesh(mesh.devices.reshape(pairs, outer, inner), ("pair", "ylo", "x"))
    placed = (P(("ylo", "x", "pair"), None), P())
    return jax.shard_map(
        functools.partial(per_device, outer=outer, inner=inner),
        mesh=split,
        in_specs=placed,
        out_specs=P(("ylo", "x"), "pair"),
        check_vma=False,
    )
```

```python
import functools

import jax
import jax.numpy as jnp
from jax import lax
from jax.experimental import pallas as pl
from jax.experimental.pallas import tpu as pltpu
from jax.sharding import PartitionSpec as P

MESH = pl.DeviceIdType.MESH

BLK = 512
STEPS = 2


epsilon = 1e-06
high = lax.Precision.HIGHEST
fast = lax.Precision.HIGH


def shifted(v, axis, count, by):
    return lax.ppermute(v, axis, [(i, (i + by) % count) for i in range(count)])


def scatter_sum(v, axis, count):
    me = lax.axis_index(axis)
    chunks = v.reshape(count, v.shape[0] // count, *v.shape[1:])
    total = lax.dynamic_index_in_dim(chunks, me, keepdims=False)
    for by in range(1, count):
        piece = lax.dynamic_index_in_dim(chunks, (me + by) % count, keepdims=False)
        total = total + shifted(piece, axis, count, by)
    return total


def gather_all(v, axis, count):
    me = lax.axis_index(axis)
    out = jnp.zeros((count,) + v.shape, v.dtype)
    out = lax.dynamic_update_index_in_dim(out, v, me, 0)
    for by in range(1, count):
        out = lax.dynamic_update_index_in_dim(out, shifted(v, axis, count, by), (me - by) % count, 0)
    return out.reshape(count * v.shape[0], *v.shape[1:])


def remote(src, dst, sends, recvs, slot, device):
    copy = pltpu.make_async_remote_copy(
        src_ref=src,
        dst_ref=dst,
        send_sem=sends.at[slot],
        recv_sem=recvs.at[slot],
        device_id=device,
        device_id_type=MESH,
    )
    copy.start()
    return copy


def rows_sum_kernel(
    outer,
    inner,
    payload,
    first_out,
    inverse_out,
    factor_out,
    a_in,
    a_acc,
    a_halves,
    a_own,
    a_all,
    b_in,
    b_acc,
    b_parts,
    b_own,
    b_row,
    b_all,
    out,
    sends,
    recvs,
):
    pair = lax.axis_index("pair")
    me_y = lax.axis_index("ylo")
    me_x = lax.axis_index("x")
    a_rows = a_in.shape[1] * inner
    b_rows = b_in.shape[0] * outer
    a_chunk = a_rows // inner
    a_half = a_chunk // outer
    b_half = b_rows // outer
    b_chunk = b_half // inner
    partner = (me_y + 1) % outer
    cols_a = slice(None)
    cols_b = slice(None)

    def x_peer(by):
        return (pair, me_y, (me_x + by) % inner)

    y_peer = (pair, partner, me_x)

    barrier = pltpu.get_barrier_semaphore()
    for by in range(1, inner):
        pl.semaphore_signal(barrier, inc=1, device_id=x_peer(by), device_id_type=MESH)
    pl.semaphore_signal(barrier, inc=1, device_id=y_peer, device_id_type=MESH)
    pl.semaphore_wait(barrier, inner)

    copies = []
    for by in range(1, inner):
        target = (me_x + by) % inner
        rows_k = pl.ds(pl.multiple_of(target * a_chunk, 8), a_chunk)
        copies.append(remote(payload.at[rows_k], a_in.at[by - 1], sends, recvs, by - 1, x_peer(by)))
    rows_k = pl.ds(pl.multiple_of(a_rows + partner * b_half, 8), b_half)
    copies.append(remote(payload.at[rows_k], b_in, sends, recvs, 8, y_peer))
    for copy in copies:
        copy.wait()
    total = payload[pl.ds(pl.multiple_of(me_x * a_chunk, 8), a_chunk), :]
    for by in range(1, inner):
        total = total + a_in[by - 1]
    a_acc[...] = total
    b_acc[...] = payload[pl.ds(pl.multiple_of(a_rows + me_y * b_half, 8), b_half), :] + b_in[...]

    copies = [
        remote(a_acc.at[pl.ds(pl.multiple_of(partner * a_half, 8), a_half)], a_halves.at[0], sends, recvs, 3, y_peer)
    ]
    for by in range(1, inner):
        target = (me_x + by) % inner
        rows_k = pl.ds(pl.multiple_of(target * b_chunk, 8), b_chunk)
        copies.append(remote(b_acc.at[rows_k], b_parts.at[by - 1], sends, recvs, 8 + by, x_peer(by)))
    for copy in copies:
        copy.wait()
    a_own[...] = a_acc[pl.ds(pl.multiple_of(me_y * a_half, 8), a_half), :] + a_halves[0]
    total = b_acc[pl.ds(pl.multiple_of(me_x * b_chunk, 8), b_chunk), :]
    for by in range(1, inner):
        total = total + b_parts[by - 1]
    b_own[...] = total

    copies = [remote(a_own, a_halves.at[1], sends, recvs, 4, y_peer)]
    for by in range(1, inner):
        copies.append(remote(b_own, b_row.at[me_x], sends, recvs, 11 + by, x_peer(by)))
    for copy in copies:
        copy.wait()
    a_all[me_x, pl.ds(pl.multiple_of(me_y * a_half, 8), a_half), :] = a_own[...]
    a_all[me_x, pl.ds(pl.multiple_of(partner * a_half, 8), a_half), :] = a_halves[1]
    b_row[me_x] = b_own[...]
    b_all[me_y] = b_row[...]

    copies = []
    for by in range(1, inner):
        copies.append(remote(a_all.at[me_x], a_all.at[me_x], sends, recvs, 4 + by, x_peer(by)))
    copies.append(remote(b_row, b_all.at[me_y], sends, recvs, 15, y_peer))
    for copy in copies:
        copy.wait()
    for k in range(inner):
        out[pl.ds(k * a_chunk, a_chunk), :] = a_all[k]
    for j in range(outer):
        for k in range(inner):
            out[pl.ds(a_rows + j * b_half + k * b_chunk, b_chunk), :] = b_all[j, k]
    normalize_packed(out, first_out, inverse_out, factor_out)


def normalize_packed(packed, first_out, inverse_out, factor_out):
    width = packed.shape[1]
    row = lax.broadcasted_iota(jnp.int32, (width, width), 0)
    col = lax.broadcasted_iota(jnp.int32, (width, width), 1)
    eye = row == col
    top = packed[pl.ds(0, width), :]
    cross = packed[pl.ds(width, width), :]
    lower_diagonal = packed[pl.ds(2 * width, 1), :]
    strict_upper = jnp.where(col > row, top, 0.0)
    upper = jnp.where(col >= row, top, 0.0) + strict_upper.T
    strict_lower = jnp.where(col < row, top, 0.0)
    lower = strict_lower + strict_lower.T + jnp.where(eye, lower_diagonal, 0.0)
    upper_row = jnp.sum(jnp.where(eye, top, 0.0), axis=0, keepdims=True) + epsilon
    upper_col = jnp.sum(jnp.where(eye, top, 0.0), axis=1, keepdims=True) + epsilon
    lower_row = lower_diagonal + epsilon
    lower_col = jnp.sum(jnp.where(eye, lower, 0.0), axis=1, keepdims=True) + epsilon
    inv_upper_row, inv_upper_col = 1.0 / jnp.sqrt(upper_row), 1.0 / jnp.sqrt(upper_col)
    inv_lower_row, inv_lower_col = 1.0 / jnp.sqrt(lower_row), 1.0 / jnp.sqrt(lower_col)
    upper = upper * inv_upper_col * inv_upper_row
    lower = lower * inv_lower_col * inv_lower_row
    cross = cross * inv_upper_col * inv_lower_row

    def total(v):
        return jnp.sum(jnp.sum(v * v, axis=0, keepdims=True), axis=1, keepdims=True)

    squares = total(upper) + total(lower) + 2.0 * total(cross)
    spread = 1.5 * jnp.sqrt(squares) / jnp.sqrt(jnp.float32(2 * width))
    upper = upper / spread
    lower = lower / spread
    cross = cross / spread
    three = jnp.where(eye, 3.0, 0.0)
    near, far = pl.ds(0, width), pl.ds(width, width)
    first_out[near, near] = 0.5 * (three - upper)
    first_out[near, far] = 0.5 * (0.0 - cross)
    first_out[far, near] = 0.5 * (0.0 - cross.T)
    first_out[far, far] = 0.5 * (three - lower)
    inverse_out[:, near] = inv_upper_row
    inverse_out[:, far] = inv_lower_row
    factor_out[:, near] = 0.5 * jnp.sqrt(upper_row) / jnp.sqrt(spread)
    factor_out[:, far] = 0.5 * jnp.sqrt(lower_row) / jnp.sqrt(spread)


def rows_sum(v, outer, inner):
    rows, width = v.shape
    half_w = width
    a_rows = round(rows * 4 / 7 / 64) * 64
    a_chunk = a_rows // inner
    a_half = a_chunk // outer
    b_half = (rows - a_rows) // outer
    b_chunk = b_half // inner
    return pl.pallas_call(
        functools.partial(rows_sum_kernel, outer, inner),
        out_shape=(
            jax.ShapeDtypeStruct((2 * width, 2 * width), jnp.float32),
            jax.ShapeDtypeStruct((1, 2 * width), jnp.float32),
            jax.ShapeDtypeStruct((1, 2 * width), jnp.float32),
        ),
        in_specs=[pl.BlockSpec(memory_space=pltpu.VMEM)],
        out_specs=[pl.BlockSpec(memory_space=pltpu.VMEM)] * 3,
        scratch_shapes=[
            pltpu.VMEM((inner - 1, a_chunk, half_w), jnp.float32),
            pltpu.VMEM((a_chunk, half_w), jnp.float32),
            pltpu.VMEM((2, a_half, half_w), jnp.float32),
            pltpu.VMEM((a_half, half_w), jnp.float32),
            pltpu.VMEM((inner, a_chunk, half_w), jnp.float32),
            pltpu.VMEM((b_half, half_w), jnp.float32),
            pltpu.VMEM((b_half, half_w), jnp.float32),
            pltpu.VMEM((inner - 1, b_chunk, half_w), jnp.float32),
            pltpu.VMEM((b_chunk, half_w), jnp.float32),
            pltpu.VMEM((inner, b_chunk, half_w), jnp.float32),
            pltpu.VMEM((outer, inner, b_chunk, half_w), jnp.float32),
            pltpu.VMEM((rows, width), jnp.float32),
            pltpu.SemaphoreType.DMA((16,)),
            pltpu.SemaphoreType.DMA((16,)),
        ],
        compiler_params=pltpu.CompilerParams(collective_id=0, has_side_effects=True),
    )(v)


def rotate_kernel(count, current, out, landed, sends, recvs):
    me = lax.axis_index("pair")
    me_y = lax.axis_index("ylo")
    me_x = lax.axis_index("x")
    half = current.shape[1] // 2
    upper_cols, lower_cols = pl.ds(0, half), pl.ds(half, half)
    following = ((me + 1) % count, me_y, me_x)
    preceding = ((me + count - 1) % count, me_y, me_x)
    barrier = pltpu.get_barrier_semaphore()

    @pl.when(me < count - 1)
    def _():
        pl.semaphore_signal(barrier, inc=1, device_id=following, device_id_type=MESH)

    @pl.when(me > 0)
    def _():
        pl.semaphore_signal(barrier, inc=1, device_id=preceding, device_id_type=MESH)

    @pl.when(jnp.logical_and(me > 0, me < count - 1))
    def _():
        pl.semaphore_wait(barrier, 2)

    @pl.when(jnp.logical_or(me == 0, me == count - 1))
    def _():
        pl.semaphore_wait(barrier, 1)

    start = pl.multiple_of(jnp.where(me == 0, half, 0), 128)
    upward = pltpu.make_async_remote_copy(
        src_ref=current.at[:, pl.ds(start, half)],
        dst_ref=landed.at[:, upper_cols],
        send_sem=sends.at[0],
        recv_sem=recvs.at[0],
        device_id=following,
        device_id_type=MESH,
    )
    downward = pltpu.make_async_remote_copy(
        src_ref=current.at[:, lower_cols],
        dst_ref=landed.at[:, lower_cols],
        send_sem=sends.at[1],
        recv_sem=recvs.at[1],
        device_id=preceding,
        device_id_type=MESH,
    )

    @pl.when(me < count - 1)
    def _():
        upward.start()

    @pl.when(me > 0)
    def _():
        downward.start()

    @pl.when(me == 0)
    def _():
        landed[:, upper_cols] = current[:, upper_cols]

    @pl.when(me == count - 1)
    def _():
        landed[:, lower_cols] = current[:, upper_cols]

    @pl.when(me < count - 1)
    def _():
        upward.wait_send()
        downward.wait_recv()

    @pl.when(me > 0)
    def _():
        downward.wait_send()
        upward.wait_recv()

    out[...] = landed[...]


def rotate(current, count):
    return pl.pallas_call(
        functools.partial(rotate_kernel, count),
        out_shape=jax.ShapeDtypeStruct(current.shape, current.dtype),
        in_specs=[pl.BlockSpec(memory_space=pltpu.VMEM)],
        out_specs=pl.BlockSpec(memory_space=pltpu.VMEM),
        scratch_shapes=[
            pltpu.VMEM(current.shape, jnp.float32),
            pltpu.SemaphoreType.DMA((2,)),
            pltpu.SemaphoreType.DMA((2,)),
        ],
        compiler_params=pltpu.CompilerParams(collective_id=2, has_side_effects=True),
    )(current)


def summed_gram(upper, lower, outer, inner):
    width = upper.shape[1]
    row = lax.broadcasted_iota(jnp.int32, (width, width), 0)
    col = lax.broadcasted_iota(jnp.int32, (width, width), 1)
    upper_gram = inner_gram(upper, upper)
    lower_gram = inner_gram(lower, lower)
    cross_gram = inner_gram(upper, lower)
    packed = jnp.where(col >= row, upper_gram, lower_gram)
    tail = jnp.zeros((64, width), jnp.float32).at[0].set(masked_diagonal(lower_gram))
    return rows_sum(jnp.concatenate([packed, cross_gram, tail]), outer, inner)


def from_behind(x, axis, by):
    count = lax.axis_size(axis)
    pairs = [(i, i + by) for i in range(count) if 0 <= i + by < count]
    return lax.ppermute(x, axis, pairs)


def inner_gram(left, right):
    return lax.dot_general(
        left, right, (((0,), (0,)), ((), ())), precision=fast, preferred_element_type=jnp.float32
    )


def masked_diagonal(block):
    width = block.shape[0]
    eye = lax.broadcasted_iota(jnp.int32, (width, width), 0) == lax.broadcasted_iota(jnp.int32, (width, width), 1)
    return jnp.sum(jnp.where(eye, block, 0.0), axis=0)


def normalize(gram, diagonal):
    width = gram.shape[0]
    diagonal = diagonal + epsilon
    inverse = 1.0 / jnp.sqrt(diagonal)
    normed = gram * inverse[:, None] * inverse[None, :]
    spread = 1.5 * jnp.sqrt(jnp.sum(normed * normed)) / jnp.sqrt(jnp.float32(width))
    scaled_gram = normed / spread
    identity = jnp.eye(width, dtype=jnp.float32)
    first_iter = 0.5 * (3.0 * identity - scaled_gram)
    factor = 0.5 * jnp.sqrt(diagonal) / jnp.sqrt(spread)
    return (scaled_gram, first_iter, inverse, factor, identity)


def per_device(matrix, plan, outer, inner):
    local_rows = matrix.shape[0]
    blocks = jnp.transpose(matrix.reshape(local_rows, -1, BLK), (1, 0, 2))
    pair_count = lax.axis_size("pair")
    slots = jnp.take(blocks, plan, axis=0, mode="clip").reshape(pair_count, 2, local_rows, BLK)
    arrived = lax.all_to_all(slots, "pair", split_axis=0, concat_axis=0, tiled=True)
    current = jnp.concatenate(
        [arrived[:, 0].reshape(-1, BLK), arrived[:, 1].reshape(-1, BLK)], axis=1
    )
    pair_index = lax.axis_index("pair")
    pair_count = lax.axis_size("pair")
    def turn(turn_index, current):
        upper = current[:, :BLK]
        lower = current[:, BLK:]
        first_iter, inverse, factor = summed_gram(upper, lower, outer, inner)
        weighted = current * inverse
        applied = jnp.dot(weighted, first_iter, precision=fast, preferred_element_type=jnp.float32)
        chain = 3.0 * applied - 2.0 * jnp.dot(
            applied, first_iter, precision=fast, preferred_element_type=jnp.float32
        )
        chain = jnp.dot(chain, first_iter, precision=fast, preferred_element_type=jnp.float32)
        chain = jnp.dot(chain, first_iter, precision=fast, preferred_element_type=jnp.float32)
        current = (3.0 * applied - chain) * factor
        return rotate(current, pair_count)

    current = lax.fori_loop(0, STEPS, turn, current)
    return current


def solution(mesh):
    pairs, rows = mesh.shape["pair"], mesh.shape["rows"]
    inner = 4
    outer = rows // inner
    split = jax.sharding.Mesh(mesh.devices.reshape(pairs, outer, inner), ("pair", "ylo", "x"))
    placed = (P(("ylo", "x", "pair"), None), P())
    return jax.shard_map(
        functools.partial(per_device, outer=outer, inner=inner),
        mesh=split,
        in_specs=placed,
        out_specs=P(("ylo", "x"), "pair"),
        check_vma=False,
    )
```

```python
import functools

import jax
import jax.numpy as jnp
from jax import lax
from jax.experimental import pallas as pl
from jax.experimental.pallas import tpu as pltpu
from jax.sharding import PartitionSpec as P

MESH = pl.DeviceIdType.MESH

BLK = 512
STEPS = 2


epsilon = 1e-06
high = lax.Precision.HIGHEST
fast = lax.Precision.HIGH


def shifted(v, axis, count, by):
    return lax.ppermute(v, axis, [(i, (i + by) % count) for i in range(count)])


def scatter_sum(v, axis, count):
    me = lax.axis_index(axis)
    chunks = v.reshape(count, v.shape[0] // count, *v.shape[1:])
    total = lax.dynamic_index_in_dim(chunks, me, keepdims=False)
    for by in range(1, count):
        piece = lax.dynamic_index_in_dim(chunks, (me + by) % count, keepdims=False)
        total = total + shifted(piece, axis, count, by)
    return total


def gather_all(v, axis, count):
    me = lax.axis_index(axis)
    out = jnp.zeros((count,) + v.shape, v.dtype)
    out = lax.dynamic_update_index_in_dim(out, v, me, 0)
    for by in range(1, count):
        out = lax.dynamic_update_index_in_dim(out, shifted(v, axis, count, by), (me - by) % count, 0)
    return out.reshape(count * v.shape[0], *v.shape[1:])


def remote(src, dst, sends, recvs, slot, device):
    copy = pltpu.make_async_remote_copy(
        src_ref=src,
        dst_ref=dst,
        send_sem=sends.at[slot],
        recv_sem=recvs.at[slot],
        device_id=device,
        device_id_type=MESH,
    )
    copy.start()
    return copy


def rows_sum_kernel(
    outer,
    inner,
    payload,
    first_out,
    inverse_out,
    factor_out,
    a_in,
    a_acc,
    a_halves,
    a_own,
    a_all,
    b_in,
    b_acc,
    b_parts,
    b_own,
    b_row,
    b_all,
    out,
    sends,
    recvs,
):
    pair = lax.axis_index("pair")
    me_y = lax.axis_index("ylo")
    me_x = lax.axis_index("x")
    a_rows = a_in.shape[1] * inner
    b_rows = b_in.shape[0] * outer
    a_chunk = a_rows // inner
    a_half = a_chunk // outer
    b_half = b_rows // outer
    b_chunk = b_half // inner
    partner = (me_y + 1) % outer
    cols_a = slice(None)
    cols_b = slice(None)

    def x_peer(by):
        return (pair, me_y, (me_x + by) % inner)

    y_peer = (pair, partner, me_x)

    barrier = pltpu.get_barrier_semaphore()
    for by in range(1, inner):
        pl.semaphore_signal(barrier, inc=1, device_id=x_peer(by), device_id_type=MESH)
    pl.semaphore_signal(barrier, inc=1, device_id=y_peer, device_id_type=MESH)
    pl.semaphore_wait(barrier, inner)

    copies = []
    for by in range(1, inner):
        target = (me_x + by) % inner
        rows_k = pl.ds(pl.multiple_of(target * a_chunk, 8), a_chunk)
        copies.append(remote(payload.at[rows_k], a_in.at[by - 1], sends, recvs, by - 1, x_peer(by)))
    rows_k = pl.ds(pl.multiple_of(a_rows + partner * b_half, 8), b_half)
    copies.append(remote(payload.at[rows_k], b_in, sends, recvs, 8, y_peer))
    for copy in copies:
        copy.wait()
    total = payload[pl.ds(pl.multiple_of(me_x * a_chunk, 8), a_chunk), :]
    for by in range(1, inner):
        total = total + a_in[by - 1]
    a_acc[...] = total
    b_acc[...] = payload[pl.ds(pl.multiple_of(a_rows + me_y * b_half, 8), b_half), :] + b_in[...]

    copies = [
        remote(a_acc.at[pl.ds(pl.multiple_of(partner * a_half, 8), a_half)], a_halves.at[0], sends, recvs, 3, y_peer)
    ]
    for by in range(1, inner):
        target = (me_x + by) % inner
        rows_k = pl.ds(pl.multiple_of(target * b_chunk, 8), b_chunk)
        copies.append(remote(b_acc.at[rows_k], b_parts.at[by - 1], sends, recvs, 8 + by, x_peer(by)))
    for copy in copies:
        copy.wait()
    a_own[...] = a_acc[pl.ds(pl.multiple_of(me_y * a_half, 8), a_half), :] + a_halves[0]
    total = b_acc[pl.ds(pl.multiple_of(me_x * b_chunk, 8), b_chunk), :]
    for by in range(1, inner):
        total = total + b_parts[by - 1]
    b_own[...] = total

    copies = [remote(a_own, a_halves.at[1], sends, recvs, 4, y_peer)]
    for by in range(1, inner):
        copies.append(remote(b_own, b_row.at[me_x], sends, recvs, 11 + by, x_peer(by)))
    for copy in copies:
        copy.wait()
    a_all[me_x, pl.ds(pl.multiple_of(me_y * a_half, 8), a_half), :] = a_own[...]
    a_all[me_x, pl.ds(pl.multiple_of(partner * a_half, 8), a_half), :] = a_halves[1]
    b_row[me_x] = b_own[...]
    b_all[me_y] = b_row[...]

    copies = []
    for by in range(1, inner):
        copies.append(remote(a_all.at[me_x], a_all.at[me_x], sends, recvs, 4 + by, x_peer(by)))
    copies.append(remote(b_row, b_all.at[me_y], sends, recvs, 15, y_peer))
    for copy in copies:
        copy.wait()
    for k in range(inner):
        out[pl.ds(k * a_chunk, a_chunk), :] = a_all[k]
    for j in range(outer):
        for k in range(inner):
            out[pl.ds(a_rows + j * b_half + k * b_chunk, b_chunk), :] = b_all[j, k]
    normalize_packed(out, first_out, inverse_out, factor_out)


def normalize_packed(packed, first_out, inverse_out, factor_out):
    width = packed.shape[1]
    row = lax.broadcasted_iota(jnp.int32, (width, width), 0)
    col = lax.broadcasted_iota(jnp.int32, (width, width), 1)
    eye = row == col
    top = packed[pl.ds(0, width), :]
    cross = packed[pl.ds(width, width), :]
    lower_diagonal = packed[pl.ds(2 * width, 1), :]
    strict_upper = jnp.where(col > row, top, 0.0)
    upper = jnp.where(col >= row, top, 0.0) + strict_upper.T
    strict_lower = jnp.where(col < row, top, 0.0)
    lower = strict_lower + strict_lower.T + jnp.where(eye, lower_diagonal, 0.0)
    upper_row = jnp.sum(jnp.where(eye, top, 0.0), axis=0, keepdims=True) + epsilon
    upper_col = jnp.sum(jnp.where(eye, top, 0.0), axis=1, keepdims=True) + epsilon
    lower_row = lower_diagonal + epsilon
    lower_col = jnp.sum(jnp.where(eye, lower, 0.0), axis=1, keepdims=True) + epsilon
    inv_upper_row, inv_upper_col = 1.0 / jnp.sqrt(upper_row), 1.0 / jnp.sqrt(upper_col)
    inv_lower_row, inv_lower_col = 1.0 / jnp.sqrt(lower_row), 1.0 / jnp.sqrt(lower_col)
    upper = upper * inv_upper_col * inv_upper_row
    lower = lower * inv_lower_col * inv_lower_row
    cross = cross * inv_upper_col * inv_lower_row

    def total(v):
        return jnp.sum(jnp.sum(v * v, axis=0, keepdims=True), axis=1, keepdims=True)

    squares = total(upper) + total(lower) + 2.0 * total(cross)
    spread = 1.5 * jnp.sqrt(squares) / jnp.sqrt(jnp.float32(2 * width))
    upper = upper / spread
    lower = lower / spread
    cross = cross / spread
    three = jnp.where(eye, 3.0, 0.0)
    near, far = pl.ds(0, width), pl.ds(width, width)
    first_out[near, near] = 0.5 * (three - upper)
    first_out[near, far] = 0.5 * (0.0 - cross)
    first_out[far, near] = 0.5 * (0.0 - cross.T)
    first_out[far, far] = 0.5 * (three - lower)
    inverse_out[:, near] = inv_upper_row
    inverse_out[:, far] = inv_lower_row
    factor_out[:, near] = 0.5 * jnp.sqrt(upper_row) / jnp.sqrt(spread)
    factor_out[:, far] = 0.5 * jnp.sqrt(lower_row) / jnp.sqrt(spread)


def rows_sum(v, outer, inner):
    rows, width = v.shape
    half_w = width
    a_rows = round(rows * 3 / 7 / 64) * 64
    a_chunk = a_rows // inner
    a_half = a_chunk // outer
    b_half = (rows - a_rows) // outer
    b_chunk = b_half // inner
    return pl.pallas_call(
        functools.partial(rows_sum_kernel, outer, inner),
        out_shape=(
            jax.ShapeDtypeStruct((2 * width, 2 * width), jnp.float32),
            jax.ShapeDtypeStruct((1, 2 * width), jnp.float32),
            jax.ShapeDtypeStruct((1, 2 * width), jnp.float32),
        ),
        in_specs=[pl.BlockSpec(memory_space=pltpu.VMEM)],
        out_specs=[pl.BlockSpec(memory_space=pltpu.VMEM)] * 3,
        scratch_shapes=[
            pltpu.VMEM((inner - 1, a_chunk, half_w), jnp.float32),
            pltpu.VMEM((a_chunk, half_w), jnp.float32),
            pltpu.VMEM((2, a_half, half_w), jnp.float32),
            pltpu.VMEM((a_half, half_w), jnp.float32),
            pltpu.VMEM((inner, a_chunk, half_w), jnp.float32),
            pltpu.VMEM((b_half, half_w), jnp.float32),
            pltpu.VMEM((b_half, half_w), jnp.float32),
            pltpu.VMEM((inner - 1, b_chunk, half_w), jnp.float32),
            pltpu.VMEM((b_chunk, half_w), jnp.float32),
            pltpu.VMEM((inner, b_chunk, half_w), jnp.float32),
            pltpu.VMEM((outer, inner, b_chunk, half_w), jnp.float32),
            pltpu.VMEM((rows, width), jnp.float32),
            pltpu.SemaphoreType.DMA((16,)),
            pltpu.SemaphoreType.DMA((16,)),
        ],
        compiler_params=pltpu.CompilerParams(collective_id=0, has_side_effects=True),
    )(v)


def rotate_kernel(count, current, out, landed, sends, recvs):
    me = lax.axis_index("pair")
    me_y = lax.axis_index("ylo")
    me_x = lax.axis_index("x")
    half = current.shape[1] // 2
    upper_cols, lower_cols = pl.ds(0, half), pl.ds(half, half)
    following = ((me + 1) % count, me_y, me_x)
    preceding = ((me + count - 1) % count, me_y, me_x)
    barrier = pltpu.get_barrier_semaphore()

    @pl.when(me < count - 1)
    def _():
        pl.semaphore_signal(barrier, inc=1, device_id=following, device_id_type=MESH)

    @pl.when(me > 0)
    def _():
        pl.semaphore_signal(barrier, inc=1, device_id=preceding, device_id_type=MESH)

    @pl.when(jnp.logical_and(me > 0, me < count - 1))
    def _():
        pl.semaphore_wait(barrier, 2)

    @pl.when(jnp.logical_or(me == 0, me == count - 1))
    def _():
        pl.semaphore_wait(barrier, 1)

    start = pl.multiple_of(jnp.where(me == 0, half, 0), 128)
    upward = pltpu.make_async_remote_copy(
        src_ref=current.at[:, pl.ds(start, half)],
        dst_ref=landed.at[:, upper_cols],
        send_sem=sends.at[0],
        recv_sem=recvs.at[0],
        device_id=following,
        device_id_type=MESH,
    )
    downward = pltpu.make_async_remote_copy(
        src_ref=current.at[:, lower_cols],
        dst_ref=landed.at[:, lower_cols],
        send_sem=sends.at[1],
        recv_sem=recvs.at[1],
        device_id=preceding,
        device_id_type=MESH,
    )

    @pl.when(me < count - 1)
    def _():
        upward.start()

    @pl.when(me > 0)
    def _():
        downward.start()

    @pl.when(me == 0)
    def _():
        landed[:, upper_cols] = current[:, upper_cols]

    @pl.when(me == count - 1)
    def _():
        landed[:, lower_cols] = current[:, upper_cols]

    @pl.when(me < count - 1)
    def _():
        upward.wait_send()
        downward.wait_recv()

    @pl.when(me > 0)
    def _():
        downward.wait_send()
        upward.wait_recv()

    out[...] = landed[...]


def rotate(current, count):
    return pl.pallas_call(
        functools.partial(rotate_kernel, count),
        out_shape=jax.ShapeDtypeStruct(current.shape, current.dtype),
        in_specs=[pl.BlockSpec(memory_space=pltpu.VMEM)],
        out_specs=pl.BlockSpec(memory_space=pltpu.VMEM),
        scratch_shapes=[
            pltpu.VMEM(current.shape, jnp.float32),
            pltpu.SemaphoreType.DMA((2,)),
            pltpu.SemaphoreType.DMA((2,)),
        ],
        compiler_params=pltpu.CompilerParams(collective_id=2, has_side_effects=True),
    )(current)


def summed_gram(upper, lower, outer, inner):
    width = upper.shape[1]
    row = lax.broadcasted_iota(jnp.int32, (width, width), 0)
    col = lax.broadcasted_iota(jnp.int32, (width, width), 1)
    upper_gram = inner_gram(upper, upper)
    lower_gram = inner_gram(lower, lower)
    cross_gram = inner_gram(upper, lower)
    packed = jnp.where(col >= row, upper_gram, lower_gram)
    tail = jnp.zeros((64, width), jnp.float32).at[0].set(masked_diagonal(lower_gram))
    return rows_sum(jnp.concatenate([packed, cross_gram, tail]), outer, inner)


def from_behind(x, axis, by):
    count = lax.axis_size(axis)
    pairs = [(i, i + by) for i in range(count) if 0 <= i + by < count]
    return lax.ppermute(x, axis, pairs)


def inner_gram(left, right):
    return lax.dot_general(
        left, right, (((0,), (0,)), ((), ())), precision=fast, preferred_element_type=jnp.float32
    )


def masked_diagonal(block):
    width = block.shape[0]
    eye = lax.broadcasted_iota(jnp.int32, (width, width), 0) == lax.broadcasted_iota(jnp.int32, (width, width), 1)
    return jnp.sum(jnp.where(eye, block, 0.0), axis=0)


def normalize(gram, diagonal):
    width = gram.shape[0]
    diagonal = diagonal + epsilon
    inverse = 1.0 / jnp.sqrt(diagonal)
    normed = gram * inverse[:, None] * inverse[None, :]
    spread = 1.5 * jnp.sqrt(jnp.sum(normed * normed)) / jnp.sqrt(jnp.float32(width))
    scaled_gram = normed / spread
    identity = jnp.eye(width, dtype=jnp.float32)
    first_iter = 0.5 * (3.0 * identity - scaled_gram)
    factor = 0.5 * jnp.sqrt(diagonal) / jnp.sqrt(spread)
    return (scaled_gram, first_iter, inverse, factor, identity)


def per_device(matrix, plan, outer, inner):
    local_rows = matrix.shape[0]
    blocks = jnp.transpose(matrix.reshape(local_rows, -1, BLK), (1, 0, 2))
    pair_count = lax.axis_size("pair")
    slots = jnp.take(blocks, plan, axis=0, mode="clip").reshape(pair_count, 2, local_rows, BLK)
    arrived = lax.all_to_all(slots, "pair", split_axis=0, concat_axis=0, tiled=True)
    current = jnp.concatenate(
        [arrived[:, 0].reshape(-1, BLK), arrived[:, 1].reshape(-1, BLK)], axis=1
    )
    pair_index = lax.axis_index("pair")
    pair_count = lax.axis_size("pair")
    def turn(turn_index, current):
        upper = current[:, :BLK]
        lower = current[:, BLK:]
        first_iter, inverse, factor = summed_gram(upper, lower, outer, inner)
        weighted = current * inverse
        applied = jnp.dot(weighted, first_iter, precision=fast, preferred_element_type=jnp.float32)
        chain = 3.0 * applied - 2.0 * jnp.dot(
            applied, first_iter, precision=fast, preferred_element_type=jnp.float32
        )
        chain = jnp.dot(chain, first_iter, precision=fast, preferred_element_type=jnp.float32)
        chain = jnp.dot(chain, first_iter, precision=fast, preferred_element_type=jnp.float32)
        current = (3.0 * applied - chain) * factor
        return rotate(current, pair_count)

    current = lax.fori_loop(0, STEPS, turn, current)
    return current


def solution(mesh):
    pairs, rows = mesh.shape["pair"], mesh.shape["rows"]
    inner = 4
    outer = rows // inner
    split = jax.sharding.Mesh(mesh.devices.reshape(pairs, outer, inner), ("pair", "ylo", "x"))
    placed = (P(("ylo", "x", "pair"), None), P())
    return jax.shard_map(
        functools.partial(per_device, outer=outer, inner=inner),
        mesh=split,
        in_specs=placed,
        out_specs=P(("ylo", "x"), "pair"),
        check_vma=False,
    )
```

```python
import functools

import jax
import jax.numpy as jnp
from jax import lax
from jax.experimental import pallas as pl
from jax.experimental.pallas import tpu as pltpu
from jax.sharding import PartitionSpec as P

MESH = pl.DeviceIdType.MESH

BLK = 512
STEPS = 2


epsilon = 1e-06
high = lax.Precision.HIGHEST
fast = lax.Precision.HIGH


def shifted(v, axis, count, by):
    return lax.ppermute(v, axis, [(i, (i + by) % count) for i in range(count)])


def scatter_sum(v, axis, count):
    me = lax.axis_index(axis)
    chunks = v.reshape(count, v.shape[0] // count, *v.shape[1:])
    total = lax.dynamic_index_in_dim(chunks, me, keepdims=False)
    for by in range(1, count):
        piece = lax.dynamic_index_in_dim(chunks, (me + by) % count, keepdims=False)
        total = total + shifted(piece, axis, count, by)
    return total


def gather_all(v, axis, count):
    me = lax.axis_index(axis)
    out = jnp.zeros((count,) + v.shape, v.dtype)
    out = lax.dynamic_update_index_in_dim(out, v, me, 0)
    for by in range(1, count):
        out = lax.dynamic_update_index_in_dim(out, shifted(v, axis, count, by), (me - by) % count, 0)
    return out.reshape(count * v.shape[0], *v.shape[1:])


def remote(src, dst, sends, recvs, slot, device):
    copy = pltpu.make_async_remote_copy(
        src_ref=src,
        dst_ref=dst,
        send_sem=sends.at[slot],
        recv_sem=recvs.at[slot],
        device_id=device,
        device_id_type=MESH,
    )
    copy.start()
    return copy


def rows_sum_kernel(
    outer,
    inner,
    payload,
    first_out,
    inverse_out,
    factor_out,
    a_in,
    a_acc,
    a_halves,
    a_own,
    a_all,
    b_in,
    b_acc,
    b_parts,
    b_own,
    b_row,
    b_all,
    out,
    sends,
    recvs,
):
    pair = lax.axis_index("pair")
    me_y = lax.axis_index("ylo")
    me_x = lax.axis_index("x")
    rows, width = payload.shape
    half_w = width // 2
    a_chunk = rows // inner
    a_half = a_chunk // outer
    b_half = rows // outer
    b_chunk = b_half // inner
    partner = (me_y + 1) % outer
    cols_a = pl.ds(0, half_w)
    cols_b = pl.ds(half_w, half_w)

    def x_peer(by):
        return (pair, me_y, (me_x + by) % inner)

    y_peer = (pair, partner, me_x)

    barrier = pltpu.get_barrier_semaphore()
    for by in range(1, inner):
        pl.semaphore_signal(barrier, inc=1, device_id=x_peer(by), device_id_type=MESH)
    pl.semaphore_signal(barrier, inc=1, device_id=y_peer, device_id_type=MESH)
    pl.semaphore_wait(barrier, inner)

    a_copies = []
    for by in range(1, inner):
        target = (me_x + by) % inner
        rows_k = pl.ds(pl.multiple_of(target * a_chunk, 8), a_chunk)
        a_copies.append(remote(payload.at[rows_k, cols_a], a_in.at[by - 1], sends, recvs, by - 1, x_peer(by)))
    rows_k = pl.ds(pl.multiple_of(partner * b_half, 8), b_half)
    b_copies = [remote(payload.at[rows_k, cols_b], b_in, sends, recvs, 8, y_peer)]

    for copy in a_copies:
        copy.wait()
    total = payload[pl.ds(pl.multiple_of(me_x * a_chunk, 8), a_chunk), cols_a]
    for by in range(1, inner):
        total = total + a_in[by - 1]
    a_acc[...] = total
    a_copies = [
        remote(a_acc.at[pl.ds(pl.multiple_of(partner * a_half, 8), a_half)], a_halves.at[0], sends, recvs, 3, y_peer)
    ]

    for copy in b_copies:
        copy.wait()
    b_acc[...] = payload[pl.ds(pl.multiple_of(me_y * b_half, 8), b_half), cols_b] + b_in[...]
    b_copies = []
    for by in range(1, inner):
        target = (me_x + by) % inner
        rows_k = pl.ds(pl.multiple_of(target * b_chunk, 8), b_chunk)
        b_copies.append(remote(b_acc.at[rows_k], b_parts.at[by - 1], sends, recvs, 8 + by, x_peer(by)))

    for copy in a_copies:
        copy.wait()
    a_own[...] = a_acc[pl.ds(pl.multiple_of(me_y * a_half, 8), a_half), :] + a_halves[0]
    a_copies = [remote(a_own, a_halves.at[1], sends, recvs, 4, y_peer)]

    for copy in b_copies:
        copy.wait()
    total = b_acc[pl.ds(pl.multiple_of(me_x * b_chunk, 8), b_chunk), :]
    for by in range(1, inner):
        total = total + b_parts[by - 1]
    b_own[...] = total
    b_copies = [remote(b_own, b_row.at[me_x], sends, recvs, 11 + by, x_peer(by)) for by in range(1, inner)]

    for copy in a_copies:
        copy.wait()
    a_all[me_x, pl.ds(pl.multiple_of(me_y * a_half, 8), a_half), :] = a_own[...]
    a_all[me_x, pl.ds(pl.multiple_of(partner * a_half, 8), a_half), :] = a_halves[1]
    a_copies = [remote(a_all.at[me_x], a_all.at[me_x], sends, recvs, 4 + by, x_peer(by)) for by in range(1, inner)]

    b_row[me_x] = b_own[...]
    for copy in b_copies:
        copy.wait()
    b_all[me_y] = b_row[...]
    b_copies = [remote(b_row, b_all.at[me_y], sends, recvs, 15, y_peer)]

    for copy in a_copies + b_copies:
        copy.wait()
    for k in range(inner):
        out[pl.ds(k * a_chunk, a_chunk), cols_a] = a_all[k]
    for j in range(outer):
        for k in range(inner):
            out[pl.ds(j * b_half + k * b_chunk, b_chunk), cols_b] = b_all[j, k]
    normalize_packed(out, first_out, inverse_out, factor_out)


def normalize_packed(packed, first_out, inverse_out, factor_out):
    width = packed.shape[1]
    row = lax.broadcasted_iota(jnp.int32, (width, width), 0)
    col = lax.broadcasted_iota(jnp.int32, (width, width), 1)
    eye = row == col
    top = packed[pl.ds(0, width), :]
    cross = packed[pl.ds(width, width), :]
    lower_diagonal = packed[pl.ds(2 * width, 1), :]
    strict_upper = jnp.where(col > row, top, 0.0)
    upper = jnp.where(col >= row, top, 0.0) + strict_upper.T
    strict_lower = jnp.where(col < row, top, 0.0)
    lower = strict_lower + strict_lower.T + jnp.where(eye, lower_diagonal, 0.0)
    upper_row = jnp.sum(jnp.where(eye, top, 0.0), axis=0, keepdims=True) + epsilon
    upper_col = jnp.sum(jnp.where(eye, top, 0.0), axis=1, keepdims=True) + epsilon
    lower_row = lower_diagonal + epsilon
    lower_col = jnp.sum(jnp.where(eye, lower, 0.0), axis=1, keepdims=True) + epsilon
    inv_upper_row, inv_upper_col = 1.0 / jnp.sqrt(upper_row), 1.0 / jnp.sqrt(upper_col)
    inv_lower_row, inv_lower_col = 1.0 / jnp.sqrt(lower_row), 1.0 / jnp.sqrt(lower_col)
    upper = upper * inv_upper_col * inv_upper_row
    lower = lower * inv_lower_col * inv_lower_row
    cross = cross * inv_upper_col * inv_lower_row

    def total(v):
        return jnp.sum(jnp.sum(v * v, axis=0, keepdims=True), axis=1, keepdims=True)

    squares = total(upper) + total(lower) + 2.0 * total(cross)
    spread = 1.5 * jnp.sqrt(squares) / jnp.sqrt(jnp.float32(2 * width))
    upper = upper / spread
    lower = lower / spread
    cross = cross / spread
    three = jnp.where(eye, 3.0, 0.0)
    near, far = pl.ds(0, width), pl.ds(width, width)
    first_out[near, near] = 0.5 * (three - upper)
    first_out[near, far] = 0.5 * (0.0 - cross)
    first_out[far, near] = 0.5 * (0.0 - cross.T)
    first_out[far, far] = 0.5 * (three - lower)
    inverse_out[:, near] = inv_upper_row
    inverse_out[:, far] = inv_lower_row
    factor_out[:, near] = 0.5 * jnp.sqrt(upper_row) / jnp.sqrt(spread)
    factor_out[:, far] = 0.5 * jnp.sqrt(lower_row) / jnp.sqrt(spread)


def rows_sum(v, outer, inner):
    rows, width = v.shape
    half_w = width // 2
    a_chunk = rows // inner
    a_half = a_chunk // outer
    b_half = rows // outer
    b_chunk = b_half // inner
    return pl.pallas_call(
        functools.partial(rows_sum_kernel, outer, inner),
        out_shape=(
            jax.ShapeDtypeStruct((2 * width, 2 * width), jnp.float32),
            jax.ShapeDtypeStruct((1, 2 * width), jnp.float32),
            jax.ShapeDtypeStruct((1, 2 * width), jnp.float32),
        ),
        in_specs=[pl.BlockSpec(memory_space=pltpu.VMEM)],
        out_specs=[pl.BlockSpec(memory_space=pltpu.VMEM)] * 3,
        scratch_shapes=[
            pltpu.VMEM((inner - 1, a_chunk, half_w), jnp.float32),
            pltpu.VMEM((a_chunk, half_w), jnp.float32),
            pltpu.VMEM((2, a_half, half_w), jnp.float32),
            pltpu.VMEM((a_half, half_w), jnp.float32),
            pltpu.VMEM((inner, a_chunk, half_w), jnp.float32),
            pltpu.VMEM((b_half, half_w), jnp.float32),
            pltpu.VMEM((b_half, half_w), jnp.float32),
            pltpu.VMEM((inner - 1, b_chunk, half_w), jnp.float32),
            pltpu.VMEM((b_chunk, half_w), jnp.float32),
            pltpu.VMEM((inner, b_chunk, half_w), jnp.float32),
            pltpu.VMEM((outer, inner, b_chunk, half_w), jnp.float32),
            pltpu.VMEM((rows, width), jnp.float32),
            pltpu.SemaphoreType.DMA((16,)),
            pltpu.SemaphoreType.DMA((16,)),
        ],
        compiler_params=pltpu.CompilerParams(collective_id=0, has_side_effects=True),
    )(v)


def rotate_kernel(count, current, out, landed, sends, recvs):
    me = lax.axis_index("pair")
    me_y = lax.axis_index("ylo")
    me_x = lax.axis_index("x")
    half = current.shape[1] // 2
    upper_cols, lower_cols = pl.ds(0, half), pl.ds(half, half)
    following = ((me + 1) % count, me_y, me_x)
    preceding = ((me + count - 1) % count, me_y, me_x)
    barrier = pltpu.get_barrier_semaphore()

    @pl.when(me < count - 1)
    def _():
        pl.semaphore_signal(barrier, inc=1, device_id=following, device_id_type=MESH)

    @pl.when(me > 0)
    def _():
        pl.semaphore_signal(barrier, inc=1, device_id=preceding, device_id_type=MESH)

    @pl.when(jnp.logical_and(me > 0, me < count - 1))
    def _():
        pl.semaphore_wait(barrier, 2)

    @pl.when(jnp.logical_or(me == 0, me == count - 1))
    def _():
        pl.semaphore_wait(barrier, 1)

    start = pl.multiple_of(jnp.where(me == 0, half, 0), 128)
    upward = pltpu.make_async_remote_copy(
        src_ref=current.at[:, pl.ds(start, half)],
        dst_ref=landed.at[:, upper_cols],
        send_sem=sends.at[0],
        recv_sem=recvs.at[0],
        device_id=following,
        device_id_type=MESH,
    )
    downward = pltpu.make_async_remote_copy(
        src_ref=current.at[:, lower_cols],
        dst_ref=landed.at[:, lower_cols],
        send_sem=sends.at[1],
        recv_sem=recvs.at[1],
        device_id=preceding,
        device_id_type=MESH,
    )

    @pl.when(me < count - 1)
    def _():
        upward.start()

    @pl.when(me > 0)
    def _():
        downward.start()

    @pl.when(me == 0)
    def _():
        landed[:, upper_cols] = current[:, upper_cols]

    @pl.when(me == count - 1)
    def _():
        landed[:, lower_cols] = current[:, upper_cols]

    @pl.when(me < count - 1)
    def _():
        upward.wait_send()
        downward.wait_recv()

    @pl.when(me > 0)
    def _():
        downward.wait_send()
        upward.wait_recv()

    out[...] = landed[...]


def rotate(current, count):
    return pl.pallas_call(
        functools.partial(rotate_kernel, count),
        out_shape=jax.ShapeDtypeStruct(current.shape, current.dtype),
        in_specs=[pl.BlockSpec(memory_space=pltpu.VMEM)],
        out_specs=pl.BlockSpec(memory_space=pltpu.VMEM),
        scratch_shapes=[
            pltpu.VMEM(current.shape, jnp.float32),
            pltpu.SemaphoreType.DMA((2,)),
            pltpu.SemaphoreType.DMA((2,)),
        ],
        compiler_params=pltpu.CompilerParams(collective_id=2, has_side_effects=True),
    )(current)


def summed_gram(upper, lower, outer, inner):
    width = upper.shape[1]
    row = lax.broadcasted_iota(jnp.int32, (width, width), 0)
    col = lax.broadcasted_iota(jnp.int32, (width, width), 1)
    upper_gram = inner_gram(upper, upper)
    lower_gram = inner_gram(lower, lower)
    cross_gram = inner_gram(upper, lower)
    packed = jnp.where(col >= row, upper_gram, lower_gram)
    tail = jnp.zeros((64, width), jnp.float32).at[0].set(masked_diagonal(lower_gram))
    return rows_sum(jnp.concatenate([packed, cross_gram, tail]), outer, inner)


def from_behind(x, axis, by):
    count = lax.axis_size(axis)
    pairs = [(i, i + by) for i in range(count) if 0 <= i + by < count]
    return lax.ppermute(x, axis, pairs)


def inner_gram(left, right):
    return lax.dot_general(
        left, right, (((0,), (0,)), ((), ())), precision=fast, preferred_element_type=jnp.float32
    )


def masked_diagonal(block):
    width = block.shape[0]
    eye = lax.broadcasted_iota(jnp.int32, (width, width), 0) == lax.broadcasted_iota(jnp.int32, (width, width), 1)
    return jnp.sum(jnp.where(eye, block, 0.0), axis=0)


def normalize(gram, diagonal):
    width = gram.shape[0]
    diagonal = diagonal + epsilon
    inverse = 1.0 / jnp.sqrt(diagonal)
    normed = gram * inverse[:, None] * inverse[None, :]
    spread = 1.5 * jnp.sqrt(jnp.sum(normed * normed)) / jnp.sqrt(jnp.float32(width))
    scaled_gram = normed / spread
    identity = jnp.eye(width, dtype=jnp.float32)
    first_iter = 0.5 * (3.0 * identity - scaled_gram)
    factor = 0.5 * jnp.sqrt(diagonal) / jnp.sqrt(spread)
    return (scaled_gram, first_iter, inverse, factor, identity)


def per_device(matrix, plan, outer, inner):
    local_rows = matrix.shape[0]
    blocks = jnp.transpose(matrix.reshape(local_rows, -1, BLK), (1, 0, 2))
    pair_count = lax.axis_size("pair")
    slots = jnp.take(blocks, plan, axis=0, mode="clip").reshape(pair_count, 2, local_rows, BLK)
    arrived = lax.all_to_all(slots, "pair", split_axis=0, concat_axis=0, tiled=True)
    current = jnp.concatenate(
        [arrived[:, 0].reshape(-1, BLK), arrived[:, 1].reshape(-1, BLK)], axis=1
    )
    pair_index = lax.axis_index("pair")
    pair_count = lax.axis_size("pair")
    def turn(turn_index, current):
        upper = current[:, :BLK]
        lower = current[:, BLK:]
        first_iter, inverse, factor = summed_gram(upper, lower, outer, inner)
        weighted = current * inverse
        applied = jnp.dot(weighted, first_iter, precision=fast, preferred_element_type=jnp.float32)
        chain = 3.0 * applied - 2.0 * jnp.dot(
            applied, first_iter, precision=fast, preferred_element_type=jnp.float32
        )
        chain = jnp.dot(chain, first_iter, precision=fast, preferred_element_type=jnp.float32)
        chain = jnp.dot(chain, first_iter, precision=fast, preferred_element_type=jnp.float32)
        current = (3.0 * applied - chain) * factor
        return rotate(current, pair_count)

    current = lax.fori_loop(0, STEPS, turn, current)
    return current


def solution(mesh):
    pairs, rows = mesh.shape["pair"], mesh.shape["rows"]
    inner = 4
    outer = rows // inner
    split = jax.sharding.Mesh(mesh.devices.reshape(pairs, outer, inner), ("pair", "ylo", "x"))
    placed = (P(("ylo", "x", "pair"), None), P())
    return jax.shard_map(
        functools.partial(per_device, outer=outer, inner=inner),
        mesh=split,
        in_specs=placed,
        out_specs=P(("ylo", "x"), "pair"),
        check_vma=False,
    )
```

```python
import functools

import jax
import jax.numpy as jnp
from jax import lax
from jax.experimental import pallas as pl
from jax.experimental.pallas import tpu as pltpu
from jax.sharding import PartitionSpec as P

MESH = pl.DeviceIdType.MESH

BLK = 512
STEPS = 2


epsilon = 1e-06
high = lax.Precision.HIGHEST
fast = lax.Precision.HIGH


def shifted(v, axis, count, by):
    return lax.ppermute(v, axis, [(i, (i + by) % count) for i in range(count)])


def scatter_sum(v, axis, count):
    me = lax.axis_index(axis)
    chunks = v.reshape(count, v.shape[0] // count, *v.shape[1:])
    total = lax.dynamic_index_in_dim(chunks, me, keepdims=False)
    for by in range(1, count):
        piece = lax.dynamic_index_in_dim(chunks, (me + by) % count, keepdims=False)
        total = total + shifted(piece, axis, count, by)
    return total


def gather_all(v, axis, count):
    me = lax.axis_index(axis)
    out = jnp.zeros((count,) + v.shape, v.dtype)
    out = lax.dynamic_update_index_in_dim(out, v, me, 0)
    for by in range(1, count):
        out = lax.dynamic_update_index_in_dim(out, shifted(v, axis, count, by), (me - by) % count, 0)
    return out.reshape(count * v.shape[0], *v.shape[1:])


def remote(src, dst, sends, recvs, slot, device):
    copy = pltpu.make_async_remote_copy(
        src_ref=src,
        dst_ref=dst,
        send_sem=sends.at[slot],
        recv_sem=recvs.at[slot],
        device_id=device,
        device_id_type=MESH,
    )
    copy.start()
    return copy


def rows_sum_kernel(
    outer,
    inner,
    payload,
    first_out,
    inverse_out,
    factor_out,
    a_in,
    a_acc,
    a_halves,
    a_own,
    a_all,
    b_in,
    b_acc,
    b_parts,
    b_own,
    b_row,
    b_all,
    out,
    sends,
    recvs,
):
    pair = lax.axis_index("pair")
    me_y = lax.axis_index("ylo")
    me_x = lax.axis_index("x")
    rows, width = payload.shape
    half_w = width // 2
    a_chunk = rows // inner
    a_half = a_chunk // outer
    b_half = rows // outer
    b_chunk = b_half // inner
    partner = (me_y + 1) % outer
    cols_a = pl.ds(0, half_w)
    cols_b = pl.ds(half_w, half_w)

    def x_peer(by):
        return (pair, me_y, (me_x + by) % inner)

    y_peer = (pair, partner, me_x)

    barrier = pltpu.get_barrier_semaphore()
    for by in range(1, inner):
        pl.semaphore_signal(barrier, inc=1, device_id=x_peer(by), device_id_type=MESH)
    pl.semaphore_signal(barrier, inc=1, device_id=y_peer, device_id_type=MESH)
    pl.semaphore_wait(barrier, inner)

    rows_k = pl.ds(pl.multiple_of(partner * b_half, 8), b_half)
    b_copies = [remote(payload.at[rows_k, cols_b], b_in, sends, recvs, 8, y_peer)]
    a_copies = []
    for by in range(1, inner):
        target = (me_x + by) % inner
        rows_k = pl.ds(pl.multiple_of(target * a_chunk, 8), a_chunk)
        a_copies.append(remote(payload.at[rows_k, cols_a], a_in.at[by - 1], sends, recvs, by - 1, x_peer(by)))

    for copy in a_copies:
        copy.wait()
    total = payload[pl.ds(pl.multiple_of(me_x * a_chunk, 8), a_chunk), cols_a]
    for by in range(1, inner):
        total = total + a_in[by - 1]
    a_acc[...] = total
    a_copies = [
        remote(a_acc.at[pl.ds(pl.multiple_of(partner * a_half, 8), a_half)], a_halves.at[0], sends, recvs, 3, y_peer)
    ]

    for copy in b_copies:
        copy.wait()
    b_acc[...] = payload[pl.ds(pl.multiple_of(me_y * b_half, 8), b_half), cols_b] + b_in[...]
    b_copies = []
    for by in range(1, inner):
        target = (me_x + by) % inner
        rows_k = pl.ds(pl.multiple_of(target * b_chunk, 8), b_chunk)
        b_copies.append(remote(b_acc.at[rows_k], b_parts.at[by - 1], sends, recvs, 8 + by, x_peer(by)))

    for copy in a_copies:
        copy.wait()
    a_own[...] = a_acc[pl.ds(pl.multiple_of(me_y * a_half, 8), a_half), :] + a_halves[0]
    a_copies = [remote(a_own, a_halves.at[1], sends, recvs, 4, y_peer)]

    for copy in b_copies:
        copy.wait()
    total = b_acc[pl.ds(pl.multiple_of(me_x * b_chunk, 8), b_chunk), :]
    for by in range(1, inner):
        total = total + b_parts[by - 1]
    b_own[...] = total
    b_copies = [remote(b_own, b_row.at[me_x], sends, recvs, 11 + by, x_peer(by)) for by in range(1, inner)]

    for copy in a_copies:
        copy.wait()
    a_all[me_x, pl.ds(pl.multiple_of(me_y * a_half, 8), a_half), :] = a_own[...]
    a_all[me_x, pl.ds(pl.multiple_of(partner * a_half, 8), a_half), :] = a_halves[1]
    a_copies = [remote(a_all.at[me_x], a_all.at[me_x], sends, recvs, 4 + by, x_peer(by)) for by in range(1, inner)]

    b_row[me_x] = b_own[...]
    for copy in b_copies:
        copy.wait()
    b_all[me_y] = b_row[...]
    b_copies = [remote(b_row, b_all.at[me_y], sends, recvs, 15, y_peer)]

    for copy in a_copies:
        copy.wait()
    for k in range(inner):
        out[pl.ds(k * a_chunk, a_chunk), cols_a] = a_all[k]
    for copy in b_copies:
        copy.wait()
    for j in range(outer):
        for k in range(inner):
            out[pl.ds(j * b_half + k * b_chunk, b_chunk), cols_b] = b_all[j, k]
    normalize_packed(out, first_out, inverse_out, factor_out)


def normalize_packed(packed, first_out, inverse_out, factor_out):
    width = packed.shape[1]
    row = lax.broadcasted_iota(jnp.int32, (width, width), 0)
    col = lax.broadcasted_iota(jnp.int32, (width, width), 1)
    eye = row == col
    top = packed[pl.ds(0, width), :]
    cross = packed[pl.ds(width, width), :]
    lower_diagonal = packed[pl.ds(2 * width, 1), :]
    strict_upper = jnp.where(col > row, top, 0.0)
    upper = jnp.where(col >= row, top, 0.0) + strict_upper.T
    strict_lower = jnp.where(col < row, top, 0.0)
    lower = strict_lower + strict_lower.T + jnp.where(eye, lower_diagonal, 0.0)
    upper_row = jnp.sum(jnp.where(eye, top, 0.0), axis=0, keepdims=True) + epsilon
    upper_col = jnp.sum(jnp.where(eye, top, 0.0), axis=1, keepdims=True) + epsilon
    lower_row = lower_diagonal + epsilon
    lower_col = jnp.sum(jnp.where(eye, lower, 0.0), axis=1, keepdims=True) + epsilon
    inv_upper_row, inv_upper_col = 1.0 / jnp.sqrt(upper_row), 1.0 / jnp.sqrt(upper_col)
    inv_lower_row, inv_lower_col = 1.0 / jnp.sqrt(lower_row), 1.0 / jnp.sqrt(lower_col)
    upper = upper * inv_upper_col * inv_upper_row
    lower = lower * inv_lower_col * inv_lower_row
    cross = cross * inv_upper_col * inv_lower_row

    def total(v):
        return jnp.sum(jnp.sum(v * v, axis=0, keepdims=True), axis=1, keepdims=True)

    squares = total(upper) + total(lower) + 2.0 * total(cross)
    spread = 1.5 * jnp.sqrt(squares) / jnp.sqrt(jnp.float32(2 * width))
    upper = upper / spread
    lower = lower / spread
    cross = cross / spread
    three = jnp.where(eye, 3.0, 0.0)
    near, far = pl.ds(0, width), pl.ds(width, width)
    first_out[near, near] = 0.5 * (three - upper)
    first_out[near, far] = 0.5 * (0.0 - cross)
    first_out[far, near] = 0.5 * (0.0 - cross.T)
    first_out[far, far] = 0.5 * (three - lower)
    inverse_out[:, near] = inv_upper_row
    inverse_out[:, far] = inv_lower_row
    factor_out[:, near] = 0.5 * jnp.sqrt(upper_row) / jnp.sqrt(spread)
    factor_out[:, far] = 0.5 * jnp.sqrt(lower_row) / jnp.sqrt(spread)


def rows_sum(v, outer, inner):
    rows, width = v.shape
    half_w = width // 2
    a_chunk = rows // inner
    a_half = a_chunk // outer
    b_half = rows // outer
    b_chunk = b_half // inner
    return pl.pallas_call(
        functools.partial(rows_sum_kernel, outer, inner),
        out_shape=(
            jax.ShapeDtypeStruct((2 * width, 2 * width), jnp.float32),
            jax.ShapeDtypeStruct((1, 2 * width), jnp.float32),
            jax.ShapeDtypeStruct((1, 2 * width), jnp.float32),
        ),
        in_specs=[pl.BlockSpec(memory_space=pltpu.VMEM)],
        out_specs=[pl.BlockSpec(memory_space=pltpu.VMEM)] * 3,
        scratch_shapes=[
            pltpu.VMEM((inner - 1, a_chunk, half_w), jnp.float32),
            pltpu.VMEM((a_chunk, half_w), jnp.float32),
            pltpu.VMEM((2, a_half, half_w), jnp.float32),
            pltpu.VMEM((a_half, half_w), jnp.float32),
            pltpu.VMEM((inner, a_chunk, half_w), jnp.float32),
            pltpu.VMEM((b_half, half_w), jnp.float32),
            pltpu.VMEM((b_half, half_w), jnp.float32),
            pltpu.VMEM((inner - 1, b_chunk, half_w), jnp.float32),
            pltpu.VMEM((b_chunk, half_w), jnp.float32),
            pltpu.VMEM((inner, b_chunk, half_w), jnp.float32),
            pltpu.VMEM((outer, inner, b_chunk, half_w), jnp.float32),
            pltpu.VMEM((rows, width), jnp.float32),
            pltpu.SemaphoreType.DMA((16,)),
            pltpu.SemaphoreType.DMA((16,)),
        ],
        compiler_params=pltpu.CompilerParams(collective_id=0, has_side_effects=True),
    )(v)


def rotate_kernel(count, current, out, landed, sends, recvs):
    me = lax.axis_index("pair")
    me_y = lax.axis_index("ylo")
    me_x = lax.axis_index("x")
    half = current.shape[1] // 2
    upper_cols, lower_cols = pl.ds(0, half), pl.ds(half, half)
    following = ((me + 1) % count, me_y, me_x)
    preceding = ((me + count - 1) % count, me_y, me_x)
    barrier = pltpu.get_barrier_semaphore()

    @pl.when(me < count - 1)
    def _():
        pl.semaphore_signal(barrier, inc=1, device_id=following, device_id_type=MESH)

    @pl.when(me > 0)
    def _():
        pl.semaphore_signal(barrier, inc=1, device_id=preceding, device_id_type=MESH)

    @pl.when(jnp.logical_and(me > 0, me < count - 1))
    def _():
        pl.semaphore_wait(barrier, 2)

    @pl.when(jnp.logical_or(me == 0, me == count - 1))
    def _():
        pl.semaphore_wait(barrier, 1)

    start = pl.multiple_of(jnp.where(me == 0, half, 0), 128)
    upward = pltpu.make_async_remote_copy(
        src_ref=current.at[:, pl.ds(start, half)],
        dst_ref=landed.at[:, upper_cols],
        send_sem=sends.at[0],
        recv_sem=recvs.at[0],
        device_id=following,
        device_id_type=MESH,
    )
    downward = pltpu.make_async_remote_copy(
        src_ref=current.at[:, lower_cols],
        dst_ref=landed.at[:, lower_cols],
        send_sem=sends.at[1],
        recv_sem=recvs.at[1],
        device_id=preceding,
        device_id_type=MESH,
    )

    @pl.when(me < count - 1)
    def _():
        upward.start()

    @pl.when(me > 0)
    def _():
        downward.start()

    @pl.when(me == 0)
    def _():
        landed[:, upper_cols] = current[:, upper_cols]

    @pl.when(me == count - 1)
    def _():
        landed[:, lower_cols] = current[:, upper_cols]

    @pl.when(me < count - 1)
    def _():
        upward.wait_send()
        downward.wait_recv()

    @pl.when(me > 0)
    def _():
        downward.wait_send()
        upward.wait_recv()

    out[...] = landed[...]


def rotate(current, count):
    return pl.pallas_call(
        functools.partial(rotate_kernel, count),
        out_shape=jax.ShapeDtypeStruct(current.shape, current.dtype),
        in_specs=[pl.BlockSpec(memory_space=pltpu.VMEM)],
        out_specs=pl.BlockSpec(memory_space=pltpu.VMEM),
        scratch_shapes=[
            pltpu.VMEM(current.shape, jnp.float32),
            pltpu.SemaphoreType.DMA((2,)),
            pltpu.SemaphoreType.DMA((2,)),
        ],
        compiler_params=pltpu.CompilerParams(collective_id=2, has_side_effects=True),
    )(current)


def summed_gram(upper, lower, outer, inner):
    width = upper.shape[1]
    row = lax.broadcasted_iota(jnp.int32, (width, width), 0)
    col = lax.broadcasted_iota(jnp.int32, (width, width), 1)
    upper_gram = inner_gram(upper, upper)
    lower_gram = inner_gram(lower, lower)
    cross_gram = inner_gram(upper, lower)
    packed = jnp.where(col >= row, upper_gram, lower_gram)
    tail = jnp.zeros((64, width), jnp.float32).at[0].set(masked_diagonal(lower_gram))
    return rows_sum(jnp.concatenate([packed, cross_gram, tail]), outer, inner)


def from_behind(x, axis, by):
    count = lax.axis_size(axis)
    pairs = [(i, i + by) for i in range(count) if 0 <= i + by < count]
    return lax.ppermute(x, axis, pairs)


def inner_gram(left, right):
    return lax.dot_general(
        left, right, (((0,), (0,)), ((), ())), precision=fast, preferred_element_type=jnp.float32
    )


def masked_diagonal(block):
    width = block.shape[0]
    eye = lax.broadcasted_iota(jnp.int32, (width, width), 0) == lax.broadcasted_iota(jnp.int32, (width, width), 1)
    return jnp.sum(jnp.where(eye, block, 0.0), axis=0)


def normalize(gram, diagonal):
    width = gram.shape[0]
    diagonal = diagonal + epsilon
    inverse = 1.0 / jnp.sqrt(diagonal)
    normed = gram * inverse[:, None] * inverse[None, :]
    spread = 1.5 * jnp.sqrt(jnp.sum(normed * normed)) / jnp.sqrt(jnp.float32(width))
    scaled_gram = normed / spread
    identity = jnp.eye(width, dtype=jnp.float32)
    first_iter = 0.5 * (3.0 * identity - scaled_gram)
    factor = 0.5 * jnp.sqrt(diagonal) / jnp.sqrt(spread)
    return (scaled_gram, first_iter, inverse, factor, identity)


def per_device(matrix, plan, outer, inner):
    local_rows = matrix.shape[0]
    blocks = jnp.transpose(matrix.reshape(local_rows, -1, BLK), (1, 0, 2))
    pair_count = lax.axis_size("pair")
    slots = jnp.take(blocks, plan, axis=0, mode="clip").reshape(pair_count, 2, local_rows, BLK)
    arrived = lax.all_to_all(slots, "pair", split_axis=0, concat_axis=0, tiled=True)
    current = jnp.concatenate(
        [arrived[:, 0].reshape(-1, BLK), arrived[:, 1].reshape(-1, BLK)], axis=1
    )
    pair_index = lax.axis_index("pair")
    pair_count = lax.axis_size("pair")
    def turn(turn_index, current):
        upper = current[:, :BLK]
        lower = current[:, BLK:]
        first_iter, inverse, factor = summed_gram(upper, lower, outer, inner)
        weighted = current * inverse
        applied = jnp.dot(weighted, first_iter, precision=fast, preferred_element_type=jnp.float32)
        chain = 3.0 * applied - 2.0 * jnp.dot(
            applied, first_iter, precision=fast, preferred_element_type=jnp.float32
        )
        chain = jnp.dot(chain, first_iter, precision=fast, preferred_element_type=jnp.float32)
        chain = jnp.dot(chain, first_iter, precision=fast, preferred_element_type=jnp.float32)
        current = (3.0 * applied - chain) * factor
        return rotate(current, pair_count)

    current = lax.fori_loop(0, STEPS, turn, current)
    return current


def solution(mesh):
    pairs, rows = mesh.shape["pair"], mesh.shape["rows"]
    inner = 4
    outer = rows // inner
    split = jax.sharding.Mesh(mesh.devices.reshape(pairs, outer, inner), ("pair", "ylo", "x"))
    placed = (P(("ylo", "x", "pair"), None), P())
    return jax.shard_map(
        functools.partial(per_device, outer=outer, inner=inner),
        mesh=split,
        in_specs=placed,
        out_specs=P(("ylo", "x"), "pair"),
        check_vma=False,
    )
```

```python
import functools

import jax
import jax.numpy as jnp
from jax import lax
from jax.experimental import pallas as pl
from jax.experimental.pallas import tpu as pltpu
from jax.sharding import PartitionSpec as P

MESH = pl.DeviceIdType.MESH

BLK = 512
STEPS = 2


epsilon = 1e-06
high = lax.Precision.HIGHEST
fast = lax.Precision.HIGH


def shifted(v, axis, count, by):
    return lax.ppermute(v, axis, [(i, (i + by) % count) for i in range(count)])


def scatter_sum(v, axis, count):
    me = lax.axis_index(axis)
    chunks = v.reshape(count, v.shape[0] // count, *v.shape[1:])
    total = lax.dynamic_index_in_dim(chunks, me, keepdims=False)
    for by in range(1, count):
        piece = lax.dynamic_index_in_dim(chunks, (me + by) % count, keepdims=False)
        total = total + shifted(piece, axis, count, by)
    return total


def gather_all(v, axis, count):
    me = lax.axis_index(axis)
    out = jnp.zeros((count,) + v.shape, v.dtype)
    out = lax.dynamic_update_index_in_dim(out, v, me, 0)
    for by in range(1, count):
        out = lax.dynamic_update_index_in_dim(out, shifted(v, axis, count, by), (me - by) % count, 0)
    return out.reshape(count * v.shape[0], *v.shape[1:])


def remote(src, dst, sends, recvs, slot, device):
    copy = pltpu.make_async_remote_copy(
        src_ref=src,
        dst_ref=dst,
        send_sem=sends.at[slot],
        recv_sem=recvs.at[slot],
        device_id=device,
        device_id_type=MESH,
    )
    copy.start()
    return copy


def rows_sum_kernel(
    outer,
    inner,
    payload,
    first_out,
    inverse_out,
    factor_out,
    a_in,
    a_acc,
    a_halves,
    a_own,
    a_all,
    b_in,
    b_acc,
    b_parts,
    b_own,
    b_row,
    b_all,
    out,
    sends,
    recvs,
):
    pair = lax.axis_index("pair")
    me_y = lax.axis_index("ylo")
    me_x = lax.axis_index("x")
    rows, width = payload.shape
    half_w = width // 2
    a_chunk = rows // inner
    a_half = a_chunk // outer
    b_half = rows // outer
    b_chunk = b_half // inner
    partner = (me_y + 1) % outer
    cols_a = pl.ds(0, half_w)
    cols_b = pl.ds(half_w, half_w)

    def x_peer(by):
        return (pair, me_y, (me_x + by) % inner)

    y_peer = (pair, partner, me_x)

    barrier = pltpu.get_barrier_semaphore()
    for by in range(1, inner):
        pl.semaphore_signal(barrier, inc=1, device_id=x_peer(by), device_id_type=MESH)
    pl.semaphore_signal(barrier, inc=1, device_id=y_peer, device_id_type=MESH)
    pl.semaphore_wait(barrier, inner)

    a_copies = []
    for by in range(1, inner):
        target = (me_x + by) % inner
        rows_k = pl.ds(pl.multiple_of(target * a_chunk, 8), a_chunk)
        a_copies.append(remote(payload.at[rows_k, cols_a], a_in.at[by - 1], sends, recvs, by - 1, x_peer(by)))
    rows_k = pl.ds(pl.multiple_of(partner * b_half, 8), b_half)
    b_copies = [remote(payload.at[rows_k, cols_b], b_in, sends, recvs, 8, y_peer)]

    for copy in a_copies:
        copy.wait()
    total = payload[pl.ds(pl.multiple_of(me_x * a_chunk, 8), a_chunk), cols_a]
    for by in range(1, inner):
        total = total + a_in[by - 1]
    a_acc[...] = total
    a_copies = [
        remote(a_acc.at[pl.ds(pl.multiple_of(partner * a_half, 8), a_half)], a_halves.at[0], sends, recvs, 3, y_peer)
    ]

    for copy in b_copies:
        copy.wait()
    b_acc[...] = payload[pl.ds(pl.multiple_of(me_y * b_half, 8), b_half), cols_b] + b_in[...]
    b_copies = []
    for by in range(1, inner):
        target = (me_x + by) % inner
        rows_k = pl.ds(pl.multiple_of(target * b_chunk, 8), b_chunk)
        b_copies.append(remote(b_acc.at[rows_k], b_parts.at[by - 1], sends, recvs, 8 + by, x_peer(by)))

    for copy in a_copies:
        copy.wait()
    a_own[...] = a_acc[pl.ds(pl.multiple_of(me_y * a_half, 8), a_half), :] + a_halves[0]
    a_copies = [remote(a_own, a_halves.at[1], sends, recvs, 4, y_peer)]

    for copy in b_copies:
        copy.wait()
    total = b_acc[pl.ds(pl.multiple_of(me_x * b_chunk, 8), b_chunk), :]
    for by in range(1, inner):
        total = total + b_parts[by - 1]
    b_own[...] = total
    b_copies = [remote(b_own, b_row.at[me_x], sends, recvs, 11 + by, x_peer(by)) for by in range(1, inner)]

    for copy in a_copies:
        copy.wait()
    a_all[me_x, pl.ds(pl.multiple_of(me_y * a_half, 8), a_half), :] = a_own[...]
    a_all[me_x, pl.ds(pl.multiple_of(partner * a_half, 8), a_half), :] = a_halves[1]
    a_copies = [remote(a_all.at[me_x], a_all.at[me_x], sends, recvs, 4 + by, x_peer(by)) for by in range(1, inner)]

    b_row[me_x] = b_own[...]
    for copy in b_copies:
        copy.wait()
    b_all[me_y] = b_row[...]
    b_copies = [remote(b_row, b_all.at[me_y], sends, recvs, 15, y_peer)]

    for copy in a_copies + b_copies:
        copy.wait()
    for k in range(inner):
        out[pl.ds(k * a_chunk, a_chunk), cols_a] = a_all[k]
    for j in range(outer):
        for k in range(inner):
            out[pl.ds(j * b_half + k * b_chunk, b_chunk), cols_b] = b_all[j, k]
    normalize_packed(out, first_out, inverse_out, factor_out)


def normalize_packed(packed, first_out, inverse_out, factor_out):
    width = packed.shape[1]
    row = lax.broadcasted_iota(jnp.int32, (width, width), 0)
    col = lax.broadcasted_iota(jnp.int32, (width, width), 1)
    eye = row == col
    top = packed[pl.ds(0, width), :]
    cross = packed[pl.ds(width, width), :]
    lower_diagonal = packed[pl.ds(2 * width, 1), :]
    strict_upper = jnp.where(col > row, top, 0.0)
    upper = jnp.where(col >= row, top, 0.0) + strict_upper.T
    strict_lower = jnp.where(col < row, top, 0.0)
    lower = strict_lower + strict_lower.T + jnp.where(eye, lower_diagonal, 0.0)
    upper_row = jnp.sum(jnp.where(eye, top, 0.0), axis=0, keepdims=True) + epsilon
    upper_col = jnp.sum(jnp.where(eye, top, 0.0), axis=1, keepdims=True) + epsilon
    lower_row = lower_diagonal + epsilon
    lower_col = jnp.sum(jnp.where(eye, lower, 0.0), axis=1, keepdims=True) + epsilon
    inv_upper_row, inv_upper_col = 1.0 / jnp.sqrt(upper_row), 1.0 / jnp.sqrt(upper_col)
    inv_lower_row, inv_lower_col = 1.0 / jnp.sqrt(lower_row), 1.0 / jnp.sqrt(lower_col)
    upper = upper * inv_upper_col * inv_upper_row
    lower = lower * inv_lower_col * inv_lower_row
    cross = cross * inv_upper_col * inv_lower_row

    def total(v):
        return jnp.sum(jnp.sum(v * v, axis=0, keepdims=True), axis=1, keepdims=True)

    squares = total(upper) + total(lower) + 2.0 * total(cross)
    spread = 1.5 * jnp.sqrt(squares) / jnp.sqrt(jnp.float32(2 * width))
    upper = upper / spread
    lower = lower / spread
    cross = cross / spread
    three = jnp.where(eye, 3.0, 0.0)
    near, far = pl.ds(0, width), pl.ds(width, width)
    first_out[near, near] = 0.5 * (three - upper)
    first_out[near, far] = 0.5 * (0.0 - cross)
    first_out[far, near] = 0.5 * (0.0 - cross.T)
    first_out[far, far] = 0.5 * (three - lower)
    inverse_out[:, near] = inv_upper_row
    inverse_out[:, far] = inv_lower_row
    factor_out[:, near] = 0.5 * jnp.sqrt(upper_row) / jnp.sqrt(spread)
    factor_out[:, far] = 0.5 * jnp.sqrt(lower_row) / jnp.sqrt(spread)


def rows_sum(v, outer, inner):
    rows, width = v.shape
    half_w = width // 2
    a_chunk = rows // inner
    a_half = a_chunk // outer
    b_half = rows // outer
    b_chunk = b_half // inner
    return pl.pallas_call(
        functools.partial(rows_sum_kernel, outer, inner),
        out_shape=(
            jax.ShapeDtypeStruct((2 * width, 2 * width), jnp.float32),
            jax.ShapeDtypeStruct((1, 2 * width), jnp.float32),
            jax.ShapeDtypeStruct((1, 2 * width), jnp.float32),
        ),
        in_specs=[pl.BlockSpec(memory_space=pltpu.VMEM)],
        out_specs=[pl.BlockSpec(memory_space=pltpu.VMEM)] * 3,
        scratch_shapes=[
            pltpu.VMEM((inner - 1, a_chunk, half_w), jnp.float32),
            pltpu.VMEM((a_chunk, half_w), jnp.float32),
            pltpu.VMEM((2, a_half, half_w), jnp.float32),
            pltpu.VMEM((a_half, half_w), jnp.float32),
            pltpu.VMEM((inner, a_chunk, half_w), jnp.float32),
            pltpu.VMEM((b_half, half_w), jnp.float32),
            pltpu.VMEM((b_half, half_w), jnp.float32),
            pltpu.VMEM((inner - 1, b_chunk, half_w), jnp.float32),
            pltpu.VMEM((b_chunk, half_w), jnp.float32),
            pltpu.VMEM((inner, b_chunk, half_w), jnp.float32),
            pltpu.VMEM((outer, inner, b_chunk, half_w), jnp.float32),
            pltpu.VMEM((rows, width), jnp.float32),
            pltpu.SemaphoreType.DMA((16,)),
            pltpu.SemaphoreType.DMA((16,)),
        ],
        compiler_params=pltpu.CompilerParams(collective_id=0, has_side_effects=True),
    )(v)


def rotate_kernel(count, current, out, landed, sends, recvs):
    me = lax.axis_index("pair")
    me_y = lax.axis_index("ylo")
    me_x = lax.axis_index("x")
    half = current.shape[1] // 2
    upper_cols, lower_cols = pl.ds(0, half), pl.ds(half, half)
    following = ((me + 1) % count, me_y, me_x)
    preceding = ((me + count - 1) % count, me_y, me_x)
    barrier = pltpu.get_barrier_semaphore()

    @pl.when(me < count - 1)
    def _():
        pl.semaphore_signal(barrier, inc=1, device_id=following, device_id_type=MESH)

    @pl.when(me > 0)
    def _():
        pl.semaphore_signal(barrier, inc=1, device_id=preceding, device_id_type=MESH)

    @pl.when(jnp.logical_and(me > 0, me < count - 1))
    def _():
        pl.semaphore_wait(barrier, 2)

    @pl.when(jnp.logical_or(me == 0, me == count - 1))
    def _():
        pl.semaphore_wait(barrier, 1)

    start = pl.multiple_of(jnp.where(me == 0, half, 0), 128)
    upward = pltpu.make_async_remote_copy(
        src_ref=current.at[:, pl.ds(start, half)],
        dst_ref=landed.at[:, upper_cols],
        send_sem=sends.at[0],
        recv_sem=recvs.at[0],
        device_id=following,
        device_id_type=MESH,
    )
    downward = pltpu.make_async_remote_copy(
        src_ref=current.at[:, lower_cols],
        dst_ref=landed.at[:, lower_cols],
        send_sem=sends.at[1],
        recv_sem=recvs.at[1],
        device_id=preceding,
        device_id_type=MESH,
    )

    @pl.when(me < count - 1)
    def _():
        upward.start()

    @pl.when(me > 0)
    def _():
        downward.start()

    @pl.when(me == 0)
    def _():
        landed[:, upper_cols] = current[:, upper_cols]

    @pl.when(me == count - 1)
    def _():
        landed[:, lower_cols] = current[:, upper_cols]

    @pl.when(me < count - 1)
    def _():
        upward.wait_send()
        downward.wait_recv()

    @pl.when(me > 0)
    def _():
        downward.wait_send()
        upward.wait_recv()

    out[...] = landed[...]


def rotate(current, count):
    return pl.pallas_call(
        functools.partial(rotate_kernel, count),
        out_shape=jax.ShapeDtypeStruct(current.shape, current.dtype),
        in_specs=[pl.BlockSpec(memory_space=pltpu.VMEM)],
        out_specs=pl.BlockSpec(memory_space=pltpu.VMEM),
        scratch_shapes=[
            pltpu.VMEM(current.shape, jnp.float32),
            pltpu.SemaphoreType.DMA((2,)),
            pltpu.SemaphoreType.DMA((2,)),
        ],
        compiler_params=pltpu.CompilerParams(collective_id=2, has_side_effects=True),
    )(current)


def summed_gram(upper, lower, outer, inner):
    width = upper.shape[1]
    row = lax.broadcasted_iota(jnp.int32, (width, width), 0)
    col = lax.broadcasted_iota(jnp.int32, (width, width), 1)
    top = inner_gram(upper, jnp.concatenate([upper, lower], axis=1))
    upper_gram, cross_gram = top[:, :width], top[:, width:]
    lower_gram = inner_gram(lower, lower)
    packed = jnp.where(col >= row, upper_gram, lower_gram)
    tail = jnp.zeros((64, width), jnp.float32).at[0].set(masked_diagonal(lower_gram))
    return rows_sum(jnp.concatenate([packed, cross_gram, tail]), outer, inner)


def from_behind(x, axis, by):
    count = lax.axis_size(axis)
    pairs = [(i, i + by) for i in range(count) if 0 <= i + by < count]
    return lax.ppermute(x, axis, pairs)


def inner_gram(left, right):
    return lax.dot_general(
        left, right, (((0,), (0,)), ((), ())), precision=fast, preferred_element_type=jnp.float32
    )


def masked_diagonal(block):
    width = block.shape[0]
    eye = lax.broadcasted_iota(jnp.int32, (width, width), 0) == lax.broadcasted_iota(jnp.int32, (width, width), 1)
    return jnp.sum(jnp.where(eye, block, 0.0), axis=0)


def normalize(gram, diagonal):
    width = gram.shape[0]
    diagonal = diagonal + epsilon
    inverse = 1.0 / jnp.sqrt(diagonal)
    normed = gram * inverse[:, None] * inverse[None, :]
    spread = 1.5 * jnp.sqrt(jnp.sum(normed * normed)) / jnp.sqrt(jnp.float32(width))
    scaled_gram = normed / spread
    identity = jnp.eye(width, dtype=jnp.float32)
    first_iter = 0.5 * (3.0 * identity - scaled_gram)
    factor = 0.5 * jnp.sqrt(diagonal) / jnp.sqrt(spread)
    return (scaled_gram, first_iter, inverse, factor, identity)


def per_device(matrix, plan, outer, inner):
    local_rows = matrix.shape[0]
    blocks = jnp.transpose(matrix.reshape(local_rows, -1, BLK), (1, 0, 2))
    pair_count = lax.axis_size("pair")
    slots = jnp.take(blocks, plan, axis=0, mode="clip").reshape(pair_count, 2, local_rows, BLK)
    arrived = lax.all_to_all(slots, "pair", split_axis=0, concat_axis=0, tiled=True)
    current = jnp.concatenate(
        [arrived[:, 0].reshape(-1, BLK), arrived[:, 1].reshape(-1, BLK)], axis=1
    )
    pair_index = lax.axis_index("pair")
    pair_count = lax.axis_size("pair")
    def turn(turn_index, current):
        upper = current[:, :BLK]
        lower = current[:, BLK:]
        first_iter, inverse, factor = summed_gram(upper, lower, outer, inner)
        weighted = current * inverse
        applied = jnp.dot(weighted, first_iter, precision=fast, preferred_element_type=jnp.float32)
        chain = 3.0 * applied - 2.0 * jnp.dot(
            applied, first_iter, precision=fast, preferred_element_type=jnp.float32
        )
        chain = jnp.dot(chain, first_iter, precision=fast, preferred_element_type=jnp.float32)
        chain = jnp.dot(chain, first_iter, precision=fast, preferred_element_type=jnp.float32)
        current = (3.0 * applied - chain) * factor
        return rotate(current, pair_count)

    current = lax.fori_loop(0, STEPS, turn, current)
    return current


def solution(mesh):
    pairs, rows = mesh.shape["pair"], mesh.shape["rows"]
    inner = 4
    outer = rows // inner
    split = jax.sharding.Mesh(mesh.devices.reshape(pairs, outer, inner), ("pair", "ylo", "x"))
    placed = (P(("ylo", "x", "pair"), None), P())
    return jax.shard_map(
        functools.partial(per_device, outer=outer, inner=inner),
        mesh=split,
        in_specs=placed,
        out_specs=P(("ylo", "x"), "pair"),
        check_vma=False,
    )
```

```python
import functools

import jax
import jax.numpy as jnp
from jax import lax
from jax.experimental import pallas as pl
from jax.experimental.pallas import tpu as pltpu
from jax.sharding import PartitionSpec as P

MESH = pl.DeviceIdType.MESH

BLK = 512
STEPS = 2


epsilon = 1e-06
high = lax.Precision.HIGHEST
fast = lax.Precision.HIGH


def shifted(v, axis, count, by):
    return lax.ppermute(v, axis, [(i, (i + by) % count) for i in range(count)])


def scatter_sum(v, axis, count):
    me = lax.axis_index(axis)
    chunks = v.reshape(count, v.shape[0] // count, *v.shape[1:])
    total = lax.dynamic_index_in_dim(chunks, me, keepdims=False)
    for by in range(1, count):
        piece = lax.dynamic_index_in_dim(chunks, (me + by) % count, keepdims=False)
        total = total + shifted(piece, axis, count, by)
    return total


def gather_all(v, axis, count):
    me = lax.axis_index(axis)
    out = jnp.zeros((count,) + v.shape, v.dtype)
    out = lax.dynamic_update_index_in_dim(out, v, me, 0)
    for by in range(1, count):
        out = lax.dynamic_update_index_in_dim(out, shifted(v, axis, count, by), (me - by) % count, 0)
    return out.reshape(count * v.shape[0], *v.shape[1:])


def remote(src, dst, sends, recvs, slot, device):
    copy = pltpu.make_async_remote_copy(
        src_ref=src,
        dst_ref=dst,
        send_sem=sends.at[slot],
        recv_sem=recvs.at[slot],
        device_id=device,
        device_id_type=MESH,
    )
    copy.start()
    return copy


def rows_sum_kernel(
    outer,
    inner,
    payload,
    first_out,
    inverse_out,
    factor_out,
    a_in,
    a_acc,
    a_halves,
    a_own,
    a_all,
    b_in,
    b_acc,
    b_parts,
    b_own,
    b_row,
    b_all,
    out,
    sends,
    recvs,
):
    pair = lax.axis_index("pair")
    me_y = lax.axis_index("ylo")
    me_x = lax.axis_index("x")
    rows, width = payload.shape
    half_w = width // 2
    a_chunk = rows // inner
    a_half = a_chunk // outer
    b_half = rows // outer
    b_chunk = b_half // inner
    partner = (me_y + 1) % outer
    cols_a = pl.ds(0, half_w)
    cols_b = pl.ds(half_w, half_w)

    def x_peer(by):
        return (pair, me_y, (me_x + by) % inner)

    y_peer = (pair, partner, me_x)

    barrier = pltpu.get_barrier_semaphore()
    for by in range(1, inner):
        pl.semaphore_signal(barrier, inc=1, device_id=x_peer(by), device_id_type=MESH)
    pl.semaphore_signal(barrier, inc=1, device_id=y_peer, device_id_type=MESH)
    pl.semaphore_wait(barrier, inner)

    a_copies = []
    for by in range(1, inner):
        target = (me_x + by) % inner
        rows_k = pl.ds(pl.multiple_of(target * a_chunk, 8), a_chunk)
        a_copies.append(remote(payload.at[rows_k, cols_a], a_in.at[by - 1], sends, recvs, by - 1, x_peer(by)))
    rows_k = pl.ds(pl.multiple_of(partner * b_half, 8), b_half)
    b_copies = [remote(payload.at[rows_k, cols_b], b_in, sends, recvs, 8, y_peer)]

    for copy in a_copies:
        copy.wait()
    total = payload[pl.ds(pl.multiple_of(me_x * a_chunk, 8), a_chunk), cols_a]
    for by in range(1, inner):
        total = total + a_in[by - 1]
    a_acc[...] = total
    a_copies = [
        remote(a_acc.at[pl.ds(pl.multiple_of(partner * a_half, 8), a_half)], a_halves.at[0], sends, recvs, 3, y_peer)
    ]

    for copy in b_copies:
        copy.wait()
    b_acc[...] = payload[pl.ds(pl.multiple_of(me_y * b_half, 8), b_half), cols_b] + b_in[...]
    b_copies = []
    for by in range(1, inner):
        target = (me_x + by) % inner
        rows_k = pl.ds(pl.multiple_of(target * b_chunk, 8), b_chunk)
        b_copies.append(remote(b_acc.at[rows_k], b_parts.at[by - 1], sends, recvs, 8 + by, x_peer(by)))

    for copy in a_copies:
        copy.wait()
    a_own[...] = a_acc[pl.ds(pl.multiple_of(me_y * a_half, 8), a_half), :] + a_halves[0]
    a_copies = [remote(a_own, a_halves.at[1], sends, recvs, 4, y_peer)]

    for copy in b_copies:
        copy.wait()
    total = b_acc[pl.ds(pl.multiple_of(me_x * b_chunk, 8), b_chunk), :]
    for by in range(1, inner):
        total = total + b_parts[by - 1]
    b_own[...] = total
    b_copies = [remote(b_own, b_row.at[me_x], sends, recvs, 11 + by, x_peer(by)) for by in range(1, inner)]

    for copy in a_copies:
        copy.wait()
    a_all[me_x, pl.ds(pl.multiple_of(me_y * a_half, 8), a_half), :] = a_own[...]
    a_all[me_x, pl.ds(pl.multiple_of(partner * a_half, 8), a_half), :] = a_halves[1]
    a_copies = [remote(a_all.at[me_x], a_all.at[me_x], sends, recvs, 4 + by, x_peer(by)) for by in range(1, inner)]

    b_row[me_x] = b_own[...]
    for copy in b_copies:
        copy.wait()
    b_all[me_y] = b_row[...]
    b_copies = [remote(b_row, b_all.at[me_y], sends, recvs, 15, y_peer)]

    for copy in a_copies + b_copies:
        copy.wait()
    for k in range(inner):
        out[pl.ds(k * a_chunk, a_chunk), cols_a] = a_all[k]
    for j in range(outer):
        for k in range(inner):
            out[pl.ds(j * b_half + k * b_chunk, b_chunk), cols_b] = b_all[j, k]
    normalize_packed(out, first_out, inverse_out, factor_out)


def normalize_packed(packed, first_out, inverse_out, factor_out):
    width = packed.shape[1]
    row = lax.broadcasted_iota(jnp.int32, (width, width), 0)
    col = lax.broadcasted_iota(jnp.int32, (width, width), 1)
    eye = row == col
    top = packed[pl.ds(0, width), :]
    cross = packed[pl.ds(width, width), :]
    lower_diagonal = packed[pl.ds(2 * width, 1), :]
    strict_upper = jnp.where(col > row, top, 0.0)
    upper = jnp.where(col >= row, top, 0.0) + strict_upper.T
    strict_lower = jnp.where(col < row, top, 0.0)
    lower = strict_lower + strict_lower.T + jnp.where(eye, lower_diagonal, 0.0)
    upper_row = jnp.sum(jnp.where(eye, top, 0.0), axis=0, keepdims=True) + epsilon
    upper_col = jnp.sum(jnp.where(eye, top, 0.0), axis=1, keepdims=True) + epsilon
    lower_row = lower_diagonal + epsilon
    lower_col = jnp.sum(jnp.where(eye, lower, 0.0), axis=1, keepdims=True) + epsilon
    inv_upper_row, inv_upper_col = 1.0 / jnp.sqrt(upper_row), 1.0 / jnp.sqrt(upper_col)
    inv_lower_row, inv_lower_col = 1.0 / jnp.sqrt(lower_row), 1.0 / jnp.sqrt(lower_col)
    upper = upper * inv_upper_col * inv_upper_row
    lower = lower * inv_lower_col * inv_lower_row
    cross = cross * inv_upper_col * inv_lower_row

    def total(v):
        return jnp.sum(jnp.sum(v * v, axis=0, keepdims=True), axis=1, keepdims=True)

    squares = total(upper) + total(lower) + 2.0 * total(cross)
    spread = 1.5 * jnp.sqrt(squares) / jnp.sqrt(jnp.float32(2 * width))
    upper = upper / spread
    lower = lower / spread
    cross = cross / spread
    three = jnp.where(eye, 3.0, 0.0)
    near, far = pl.ds(0, width), pl.ds(width, width)
    first_out[near, near] = 0.5 * (three - upper)
    first_out[near, far] = 0.5 * (0.0 - cross)
    first_out[far, near] = 0.5 * (0.0 - cross.T)
    first_out[far, far] = 0.5 * (three - lower)
    inverse_out[:, near] = inv_upper_row
    inverse_out[:, far] = inv_lower_row
    factor_out[:, near] = 0.5 * jnp.sqrt(upper_row) / jnp.sqrt(spread)
    factor_out[:, far] = 0.5 * jnp.sqrt(lower_row) / jnp.sqrt(spread)


def rows_sum(v, outer, inner):
    rows, width = v.shape
    half_w = width // 2
    a_chunk = rows // inner
    a_half = a_chunk // outer
    b_half = rows // outer
    b_chunk = b_half // inner
    return pl.pallas_call(
        functools.partial(rows_sum_kernel, outer, inner),
        out_shape=(
            jax.ShapeDtypeStruct((2 * width, 2 * width), jnp.float32),
            jax.ShapeDtypeStruct((1, 2 * width), jnp.float32),
            jax.ShapeDtypeStruct((1, 2 * width), jnp.float32),
        ),
        in_specs=[pl.BlockSpec(memory_space=pltpu.VMEM)],
        out_specs=[pl.BlockSpec(memory_space=pltpu.VMEM)] * 3,
        scratch_shapes=[
            pltpu.VMEM((inner - 1, a_chunk, half_w), jnp.float32),
            pltpu.VMEM((a_chunk, half_w), jnp.float32),
            pltpu.VMEM((2, a_half, half_w), jnp.float32),
            pltpu.VMEM((a_half, half_w), jnp.float32),
            pltpu.VMEM((inner, a_chunk, half_w), jnp.float32),
            pltpu.VMEM((b_half, half_w), jnp.float32),
            pltpu.VMEM((b_half, half_w), jnp.float32),
            pltpu.VMEM((inner - 1, b_chunk, half_w), jnp.float32),
            pltpu.VMEM((b_chunk, half_w), jnp.float32),
            pltpu.VMEM((inner, b_chunk, half_w), jnp.float32),
            pltpu.VMEM((outer, inner, b_chunk, half_w), jnp.float32),
            pltpu.VMEM((rows, width), jnp.float32),
            pltpu.SemaphoreType.DMA((16,)),
            pltpu.SemaphoreType.DMA((16,)),
        ],
        compiler_params=pltpu.CompilerParams(collective_id=0, has_side_effects=True),
    )(v)


def rotate_kernel(count, current, landed, sends, recvs):
    me = lax.axis_index("pair")
    me_y = lax.axis_index("ylo")
    me_x = lax.axis_index("x")
    half = current.shape[1] // 2
    upper_cols, lower_cols = pl.ds(0, half), pl.ds(half, half)
    following = ((me + 1) % count, me_y, me_x)
    preceding = ((me + count - 1) % count, me_y, me_x)
    barrier = pltpu.get_barrier_semaphore()

    @pl.when(me < count - 1)
    def _():
        pl.semaphore_signal(barrier, inc=1, device_id=following, device_id_type=MESH)

    @pl.when(me > 0)
    def _():
        pl.semaphore_signal(barrier, inc=1, device_id=preceding, device_id_type=MESH)

    @pl.when(jnp.logical_and(me > 0, me < count - 1))
    def _():
        pl.semaphore_wait(barrier, 2)

    @pl.when(jnp.logical_or(me == 0, me == count - 1))
    def _():
        pl.semaphore_wait(barrier, 1)

    start = pl.multiple_of(jnp.where(me == 0, half, 0), 128)
    upward = pltpu.make_async_remote_copy(
        src_ref=current.at[:, pl.ds(start, half)],
        dst_ref=landed.at[:, upper_cols],
        send_sem=sends.at[0],
        recv_sem=recvs.at[0],
        device_id=following,
        device_id_type=MESH,
    )
    downward = pltpu.make_async_remote_copy(
        src_ref=current.at[:, lower_cols],
        dst_ref=landed.at[:, lower_cols],
        send_sem=sends.at[1],
        recv_sem=recvs.at[1],
        device_id=preceding,
        device_id_type=MESH,
    )

    @pl.when(me < count - 1)
    def _():
        upward.start()

    @pl.when(me > 0)
    def _():
        downward.start()

    @pl.when(me == 0)
    def _():
        landed[:, upper_cols] = current[:, upper_cols]

    @pl.when(me == count - 1)
    def _():
        landed[:, lower_cols] = current[:, upper_cols]

    @pl.when(me < count - 1)
    def _():
        upward.wait_send()
        downward.wait_recv()

    @pl.when(me > 0)
    def _():
        downward.wait_send()
        upward.wait_recv()


def rotate(current, count):
    return pl.pallas_call(
        functools.partial(rotate_kernel, count),
        out_shape=jax.ShapeDtypeStruct(current.shape, current.dtype),
        in_specs=[pl.BlockSpec(memory_space=pltpu.VMEM)],
        out_specs=pl.BlockSpec(memory_space=pltpu.VMEM),
        scratch_shapes=[
            pltpu.SemaphoreType.DMA((2,)),
            pltpu.SemaphoreType.DMA((2,)),
        ],
        compiler_params=pltpu.CompilerParams(collective_id=2, has_side_effects=True),
    )(current)


def summed_gram(upper, lower, outer, inner):
    width = upper.shape[1]
    row = lax.broadcasted_iota(jnp.int32, (width, width), 0)
    col = lax.broadcasted_iota(jnp.int32, (width, width), 1)
    top = inner_gram(upper, jnp.concatenate([upper, lower], axis=1))
    upper_gram, cross_gram = top[:, :width], top[:, width:]
    lower_gram = inner_gram(lower, lower)
    packed = jnp.where(col >= row, upper_gram, lower_gram)
    tail = jnp.zeros((64, width), jnp.float32).at[0].set(masked_diagonal(lower_gram))
    return rows_sum(jnp.concatenate([packed, cross_gram, tail]), outer, inner)


def from_behind(x, axis, by):
    count = lax.axis_size(axis)
    pairs = [(i, i + by) for i in range(count) if 0 <= i + by < count]
    return lax.ppermute(x, axis, pairs)


def inner_gram(left, right):
    return lax.dot_general(
        left, right, (((0,), (0,)), ((), ())), precision=fast, preferred_element_type=jnp.float32
    )


def masked_diagonal(block):
    width = block.shape[0]
    eye = lax.broadcasted_iota(jnp.int32, (width, width), 0) == lax.broadcasted_iota(jnp.int32, (width, width), 1)
    return jnp.sum(jnp.where(eye, block, 0.0), axis=0)


def normalize(gram, diagonal):
    width = gram.shape[0]
    diagonal = diagonal + epsilon
    inverse = 1.0 / jnp.sqrt(diagonal)
    normed = gram * inverse[:, None] * inverse[None, :]
    spread = 1.5 * jnp.sqrt(jnp.sum(normed * normed)) / jnp.sqrt(jnp.float32(width))
    scaled_gram = normed / spread
    identity = jnp.eye(width, dtype=jnp.float32)
    first_iter = 0.5 * (3.0 * identity - scaled_gram)
    factor = 0.5 * jnp.sqrt(diagonal) / jnp.sqrt(spread)
    return (scaled_gram, first_iter, inverse, factor, identity)


def per_device(matrix, plan, outer, inner):
    local_rows = matrix.shape[0]
    blocks = jnp.transpose(matrix.reshape(local_rows, -1, BLK), (1, 0, 2))
    pair_count = lax.axis_size("pair")
    slots = jnp.take(blocks, plan, axis=0, mode="clip").reshape(pair_count, 2, local_rows, BLK)
    arrived = lax.all_to_all(slots, "pair", split_axis=0, concat_axis=0, tiled=True)
    current = jnp.concatenate(
        [arrived[:, 0].reshape(-1, BLK), arrived[:, 1].reshape(-1, BLK)], axis=1
    )
    pair_index = lax.axis_index("pair")
    pair_count = lax.axis_size("pair")
    def turn(turn_index, current):
        upper = current[:, :BLK]
        lower = current[:, BLK:]
        first_iter, inverse, factor = summed_gram(upper, lower, outer, inner)
        weighted = current * inverse
        applied = jnp.dot(weighted, first_iter, precision=fast, preferred_element_type=jnp.float32)
        chain = 3.0 * applied - 2.0 * jnp.dot(
            applied, first_iter, precision=fast, preferred_element_type=jnp.float32
        )
        chain = jnp.dot(chain, first_iter, precision=fast, preferred_element_type=jnp.float32)
        chain = jnp.dot(chain, first_iter, precision=fast, preferred_element_type=jnp.float32)
        current = (3.0 * applied - chain) * factor
        return rotate(current, pair_count)

    current = lax.fori_loop(0, STEPS, turn, current)
    return current


def solution(mesh):
    pairs, rows = mesh.shape["pair"], mesh.shape["rows"]
    inner = 4
    outer = rows // inner
    split = jax.sharding.Mesh(mesh.devices.reshape(pairs, outer, inner), ("pair", "ylo", "x"))
    placed = (P(("ylo", "x", "pair"), None), P())
    return jax.shard_map(
        functools.partial(per_device, outer=outer, inner=inner),
        mesh=split,
        in_specs=placed,
        out_specs=P(("ylo", "x"), "pair"),
        check_vma=False,
    )
```
